128 devices in a mesh: prow: 8 (over z, core), pcol: 16 (over x, y).
Axes of the slice: x: 4, y: 4, z: 4, core: 2. Of those that a mesh axis runs over, the one named last changes fastest.
Arguments:
- factors: bfloat16 [4, 4096, 512], P(None, ('prow', 'pcol')), may hold values from -0.25 to 0.25
- x_factor: bfloat16 [512, 512], replicated, may hold values from -0.25 to 0.25
- zinv_factor: bfloat16 [512, 512], replicated, may hold values from -0.25 to 0.25
- placement: int32 [4096], replicated, may hold values from 0 to 4095, as said below
Outputs:
- trailing: float32 [4096, 4096], P('prow', 'pcol')
- panels: float32 [4096, 1024], P('prow', 'pcol')
The draws below stay inside these ranges and needn't reach their ends.
Inputs may be any that keep to these rules, and one draw needn't show every extreme that they name: placement is a permutation of the Schur rows; device d (grid rows slowest) assembles the rows placement[d * 32] to placement[d * 32 + 31]; among one device's rows at most 8 share the same owner grid row (natural row i belongs to grid row (i div 64) mod 8), and some device has exactly 8 such rows.
All inputs are finite; a program needn't handle non-finite values.
Results may differ from the reference program's by a relative error of at most 0.003.
Values may be sent and summed in bfloat16 or wider, within the bound.
A program may use at most 128 MiB of HBM per device.

```python
import jax
import jax.numpy as jnp
from jax import lax

NORD = 512
M = 4096
RANK = 4
NB = 64
K = 1024
ROWS_DEV = 32
N_PROW = 8
N_PCOL = 16


def draw_placement(key, part):
    devices_all = M // ROWS_DEV
    base = ROWS_DEV // N_PROW
    key_shift, key_rows, key_slots = jax.random.split(jax.random.fold_in(key, 7), 3)
    shifts = jax.random.randint(key_shift, (devices_all // 2, N_PROW // 2), -base, base + 1)
    shifts = shifts.at[0, 0].set(base)
    paired = jnp.stack([shifts, -shifts], axis=2).reshape(devices_all // 2, N_PROW)
    counts = base + jnp.stack([paired, -paired], axis=1).reshape(devices_all, N_PROW)
    offsets = jnp.cumsum(counts, axis=0) - counts
    ends = jnp.cumsum(counts, axis=1)
    begins = ends - counts
    slots = jnp.arange(ROWS_DEV)
    owner = jnp.sum((ends[:, None, :] <= slots[None, :, None]).astype(jnp.int32), axis=2)
    within = slots[None, :] - jnp.take_along_axis(begins, owner, axis=1)
    picked = jnp.take_along_axis(offsets, owner, axis=1) + within
    share = M // N_PROW
    orders = jax.vmap(lambda k: jax.random.permutation(k, share))(jax.random.split(key_rows, N_PROW))
    listed = orders[owner, picked]
    natural = listed // NB * NB * N_PROW + owner * NB + listed % NB
    shuffled = jax.vmap(lambda k, row: jax.random.permutation(k, row))(jax.random.split(key_slots, devices_all), natural)
    return shuffled.reshape(M).astype(jnp.int32)


def block_levels(stream_key, dims, cuts, low, high):
    factor_of, own = 1.0, jax.random.fold_in(stream_key, 6)
    for position, blocks in cuts:
        heights = jnp.exp(jax.random.uniform(jax.random.fold_in(own, position), (blocks,), jnp.float32, low / len(cuts), high / len(cuts)))
        factor_of = factor_of * jnp.repeat(heights, dims[position] // blocks).reshape([-1 if axis == position else 1 for axis in range(len(dims))])
    return factor_of


def gaussian(key, shape, deviation, bound, cuts=(), held_as=jnp.bfloat16):
    values = jax.random.normal(key, shape, jnp.float32) * deviation
    if len(cuts) > 0:
        values = block_levels(key, shape, cuts, -0.22, 0.18) * values
    return jnp.clip(values, min=-bound, max=bound).astype(held_as)


def setup_inputs(seed: int = 0) -> dict:
    key_of = jax.random.split(jax.random.key(seed), 5)
    factors = gaussian(key_of[0], (RANK, M, NORD), (NORD ** -0.5), 0.25, ((1, 128),))
    x_factor = gaussian(key_of[1], (NORD, NORD), NORD ** -0.5, 0.25)
    zinv_factor = gaussian(key_of[2], (NORD, NORD), NORD ** -0.5, 0.25)
    placement = draw_placement(jax.random.fold_in(key_of[4], 71), 0)
    return {"factors": factors, "x_factor": x_factor, "zinv_factor": zinv_factor, "placement": placement}


rank_signs = (1.0, 1.0, -1.0, -1.0)
block_rows = 256

def to_cyclic(matrix, which_axis, groups):
    length = matrix.shape[which_axis]
    moved = jnp.moveaxis(matrix, which_axis, 0)
    tail_shape = moved.shape[1:]
    moved = moved.reshape((length // (NB * groups), groups, NB) + tail_shape)
    moved = jnp.swapaxes(moved, 0, 1).reshape((length,) + tail_shape)
    return jnp.moveaxis(moved, 0, which_axis)

def reference(factors, x_factor, zinv_factor, placement):
    natural = jnp.zeros_like(factors).at[:, placement, :].set(factors)
    stacked = natural.reshape(RANK * M, NORD)
    proj_x = jnp.dot(stacked.astype(jnp.float32), x_factor.astype(jnp.float32), preferred_element_type=jnp.float32).astype(jnp.bfloat16)
    proj_z = jnp.dot(stacked.astype(jnp.float32), zinv_factor.astype(jnp.float32), preferred_element_type=jnp.float32).astype(jnp.bfloat16)
    cube_x = proj_x.reshape(RANK, M, NORD)
    cube_z = proj_z.reshape(RANK, M, NORD)
    weights = jnp.array(rank_signs, jnp.float32)

    def one_block(first):
        left_x = lax.dynamic_slice_in_dim(cube_x, first, block_rows, 1).reshape(RANK * block_rows, NORD)
        left_z = lax.dynamic_slice_in_dim(cube_z, first, block_rows, 1).reshape(RANK * block_rows, NORD)
        inner_x = jnp.dot(left_x.astype(jnp.float32), proj_x.T.astype(jnp.float32), preferred_element_type=jnp.float32)
        inner_z = jnp.dot(left_z.astype(jnp.float32), proj_z.T.astype(jnp.float32), preferred_element_type=jnp.float32)
        product = (inner_x * inner_z).reshape(RANK, block_rows, RANK, M)
        return jnp.einsum('r,riqj,q->ij', weights, product, weights)
    starts = (jnp.arange(M // block_rows) * block_rows).astype(jnp.int32)
    schur = lax.map(one_block, starts).reshape(M, M)
    leading = jnp.linalg.cholesky(schur[:K, :K])
    panel_rows = lax.linalg.triangular_solve(leading, schur[:, :K], left_side=False, lower=True, transpose_a=True)
    rest = schur - jnp.dot(panel_rows, panel_rows.T, precision=lax.Precision.HIGHEST)
    trailing = to_cyclic(to_cyclic(rest, 0, N_PROW), 1, N_PCOL)
    panels = to_cyclic(to_cyclic(panel_rows, 0, N_PROW), 1, N_PCOL)
    return (trailing, panels)
```

```python
import functools
import jax
import jax.numpy as jnp
from jax import lax
from jax.experimental import pallas as pl
from jax.experimental.pallas import tpu as pltpu
from jax.sharding import PartitionSpec as P

RANK = 4
NB = 64
KK = 1024
F32, BF16 = jnp.float32, jnp.bfloat16
SIGNS = (1.0, 1.0, -1.0, -1.0)
TN = (((1,), (1,)), ((), ()))


def split(v):
    hi = v.astype(BF16)
    return hi, (v - hi.astype(F32)).astype(BF16)


def spread(v):
    return jnp.broadcast_to(v, (8, 128))


def invert_block(block_ref, inv_ref):
    lane = lax.broadcasted_iota(jnp.int32, (8, 128), 1)
    sub = lax.broadcasted_iota(jnp.int32, (8, 128), 0)
    rows = [block_ref[8 * i:8 * i + 8, :] for i in range(16)]
    aug = [(lane == sub + 8 * i).astype(F32) for i in range(16)]
    for j in range(16):
        mine, extra = rows[j], aug[j]
        cols = [spread(mine[:, 8 * j + q:8 * j + q + 1]) for q in range(8)]
        a = [[None] * 8 for _ in range(8)]
        for q in range(8):
            for s in range(q, 8):
                a[s][q] = spread(cols[q][s:s + 1, :])
        r = [spread(mine[t:t + 1, :]) for t in range(8)] if j < 15 else None
        e = [spread(extra[t:t + 1, :]) for t in range(8)]
        rinv = [None] * 8
        low = [[None] * 8 for _ in range(8)]
        for t in range(8):
            rinv[t] = 1.0 / a[t][t]
            for s in range(t + 1, 8):
                low[s][t] = a[s][t] * rinv[t]
            for s in range(t + 1, 8):
                for k in range(t + 1, s + 1):
                    a[s][k] = a[s][k] - low[s][t] * a[k][t]
            for s in range(t + 1, 8):
                if r is not None:
                    r[s] = r[s] - low[s][t] * r[t]
                e[s] = e[s] - low[s][t] * e[t]
        packed_d = a[0][0]
        packed_e = e[0]
        for t in range(1, 8):
            packed_d = jnp.where(sub == t, a[t][t], packed_d)
            packed_e = jnp.where(sub == t, e[t], packed_e)
        inv_ref[8 * j:8 * j + 8, :] = packed_e * lax.rsqrt(packed_d)
        if j == 15:
            break
        w = [r[t] * rinv[t] for t in range(8)]
        we = [e[t] * rinv[t] for t in range(8)]
        for s in range(7, 0, -1):
            for t in range(s):
                w[t] = w[t] - low[s][t] * w[s]
                we[t] = we[t] - low[s][t] * we[s]
        for i in range(j + 1, 16):
            c = [spread(rows[i][:, 8 * j + q:8 * j + q + 1]) for q in range(8)]
            acc = c[0] * w[0]
            acce = c[0] * we[0]
            for q in range(1, 8):
                acc = acc + c[q] * w[q]
                acce = acce + c[q] * we[q]
            rows[i] = rows[i] - acc
            aug[i] = aug[i] - acce


def chol_kernel(lead_ref, rest_ref, out_ref, a_ref, diag_ref, inv_ref, icat_ref, pcat_ref, qcat_ref):
    n = KK // 128
    total = (KK + rest_ref.shape[0]) // 256
    a_ref[:KK, :] = lead_ref[...]
    a_ref[KK:, :] = rest_ref[...]

    def step(j, carry):
        off = pl.multiple_of(j * 128, 128)
        diag_ref[...] = a_ref[pl.ds(off, 128), pl.ds(off, 128)]
        invert_block(diag_ref, inv_ref)
        hi, lo = split(inv_ref[...])
        icat_ref[:, 0:128] = hi
        icat_ref[:, 128:256] = hi
        icat_ref[:, 256:384] = lo
        first = (j + 1) // 2

        def panel(r, c):
            base = pl.multiple_of(r * 256, 256)
            hi, lo = split(a_ref[pl.ds(base, 256), pl.ds(off, 128)])
            v = lax.dot_general(jnp.concatenate([hi, lo, hi], axis=1), icat_ref[...], TN, preferred_element_type=F32)
            hi, lo = split(v)
            pcat_ref[pl.ds(base, 256), 0:128] = hi
            pcat_ref[pl.ds(base, 256), 128:256] = lo
            pcat_ref[pl.ds(base, 256), 256:384] = hi

            @pl.when(r < KK // 256)
            def _():
                qcat_ref[pl.ds(base, 256), 0:128] = hi
                qcat_ref[pl.ds(base, 256), 128:256] = hi
                qcat_ref[pl.ds(base, 256), 256:384] = lo

            @pl.when(r >= KK // 256)
            def _():
                out_ref[pl.ds(base - KK, 256), pl.ds(off, 128)] = v
            return c
        lax.fori_loop(first, total, panel, 0)

        def update(r, c):
            base = pl.multiple_of(r * 256, 256)

            def inner(k, c):
                cb = pl.multiple_of(k * 256, 256)
                a_ref[pl.ds(base, 256), pl.ds(cb, 256)] -= lax.dot_general(
                    pcat_ref[pl.ds(base, 256), :], qcat_ref[pl.ds(cb, 256), :], TN, preferred_element_type=F32)
                return c
            return lax.fori_loop(first, jnp.minimum(r + 1, KK // 256), inner, c)
        lax.fori_loop(first, total, update, 0)
        return carry
    lax.fori_loop(0, n, step, 0)


def chol_panels(lead, rest):
    m = rest.shape[0]
    return pl.pallas_call(
        chol_kernel,
        out_shape=jax.ShapeDtypeStruct((m, KK), F32),
        in_specs=[pl.BlockSpec(memory_space=pltpu.VMEM)] * 2,
        out_specs=pl.BlockSpec(memory_space=pltpu.VMEM),
        scratch_shapes=[
            pltpu.VMEM((KK + m, KK), F32),
            pltpu.VMEM((128, 128), F32),
            pltpu.VMEM((128, 128), F32),
            pltpu.VMEM((128, 384), BF16),
            pltpu.VMEM((KK + m, 384), BF16),
            pltpu.VMEM((KK, 384), BF16),
        ],
        compiler_params=pltpu.CompilerParams(vmem_limit_bytes=48 << 20),
        name="panels",
    )(lead, rest)


def pair_kernel(rows_ref, cols_ref, x_ref, z_ref, out_ref, rx_ref, rz_ref, cx_ref, cz_ref):
    depth = x_ref.shape[0]
    count = rows_ref.shape[1]
    for src, mat, dst in ((cols_ref, x_ref, cx_ref), (cols_ref, z_ref, cz_ref), (rows_ref, x_ref, rx_ref), (rows_ref, z_ref, rz_ref)):
        for r in range(RANK):
            dst[r] = jnp.dot(src[r], mat[...], preferred_element_type=F32).astype(BF16)

    def chunk(i, carry):
        base = pl.multiple_of(i * 128, 128)
        acc = None
        for r in range(RANK):
            for q in range(RANK):
                inner_x = lax.dot_general(rx_ref[r, pl.ds(base, 128), :], cx_ref[q], TN, preferred_element_type=F32)
                inner_z = lax.dot_general(rz_ref[r, pl.ds(base, 128), :], cz_ref[q], TN, preferred_element_type=F32)
                term = inner_x * inner_z
                if acc is None:
                    acc = term
                elif SIGNS[r] * SIGNS[q] > 0:
                    acc = acc + term
                else:
                    acc = acc - term
        out_ref[pl.ds(base, 128), :] = acc
        return carry
    lax.fori_loop(0, count // 128, chunk, 0)


def pair_block(rows, cols, x_factor, z_factor):
    m, n, d = rows.shape[1], cols.shape[1], rows.shape[2]
    return pl.pallas_call(
        pair_kernel,
        out_shape=jax.ShapeDtypeStruct((m, n), F32),
        in_specs=[pl.BlockSpec(memory_space=pltpu.VMEM)] * 4,
        out_specs=pl.BlockSpec(memory_space=pltpu.VMEM),
        scratch_shapes=[pltpu.VMEM((RANK, m, d), BF16)] * 2 + [pltpu.VMEM((RANK, n, d), BF16)] * 2,
        compiler_params=pltpu.CompilerParams(vmem_limit_bytes=48 << 20),
        name="pairs",
    )(rows, cols, x_factor, z_factor)


def per_device(factors, x_factor, zinv_factor, placement):
    prow_count = lax.axis_size("prow")
    pcol_count = lax.axis_size("pcol")
    total_rows = placement.shape[0]
    local_rows = total_rows // prow_count
    local_cols = total_rows // pcol_count
    prow_id = lax.axis_index("prow")
    pcol_id = lax.axis_index("pcol")
    inverse = jnp.zeros((total_rows,), jnp.int32).at[placement].set(jnp.arange(total_rows, dtype=jnp.int32))

    def natural(length, groups, which):
        k = jnp.arange(length)
        return k // NB * NB * groups + which * NB + k % NB
    everything = lax.all_gather(factors, ("prow", "pcol"), axis=1, tiled=True)
    rows = everything[:, inverse[natural(local_rows, prow_count, prow_id)]]
    cols = everything[:, inverse[natural(local_cols, pcol_count, pcol_id)]]
    schur_local = pair_block(rows, cols, x_factor, zinv_factor)
    lead_cols = KK // pcol_count
    front_cols = schur_local[:, :lead_cols]
    row_panel = lax.all_gather(front_cols, "pcol", axis=1, tiled=True)
    lead_rows = KK // prow_count
    top_panel = lax.all_gather(row_panel[:lead_rows], "prow", axis=0, tiled=True)
    top_cols = lax.all_gather(schur_local[:lead_rows], "prow", axis=0, tiled=True)

    def natural_rows(stacked):
        return (
            stacked.reshape(prow_count, lead_rows // NB, NB, stacked.shape[1])
            .transpose(1, 0, 2, 3)
            .reshape(KK, stacked.shape[1])
        )
    lead = natural_rows(top_panel)
    rest = jnp.concatenate([row_panel, natural_rows(top_cols).T], axis=0)
    solved = chol_panels(lead, rest)
    panel_rows, panel_cols = solved[:local_rows], solved[local_rows:]
    trailing = schur_local - jnp.dot(panel_rows, panel_cols.T, precision=lax.Precision.HIGHEST)
    own_panel = lax.dynamic_index_in_dim(panel_rows.reshape(local_rows, pcol_count, NB), pcol_id, 1, keepdims=False)
    return (trailing, own_panel)


def solution(mesh):
    in_specs = (P(None, ("prow", "pcol"), None), P(), P(), P())
    out_specs = (P("prow", "pcol"), P("prow", "pcol"))
    return jax.shard_map(per_device, mesh=mesh, in_specs=in_specs, out_specs=out_specs, check_vma=False)
```

```python
import functools
import jax
import jax.numpy as jnp
from jax import lax
from jax.experimental import pallas as pl
from jax.experimental.pallas import tpu as pltpu
from jax.sharding import PartitionSpec as P

RANK = 4
NB = 64
KK = 1024
F32, BF16 = jnp.float32, jnp.bfloat16
SIGNS = (1.0, 1.0, -1.0, -1.0)
MESH = pl.DeviceIdType.MESH
TN = (((1,), (1,)), ((), ()))
NN = (((1,), (0,)), ((), ()))
TT = (((0,), (0,)), ((), ()))


def split(v):
    hi = v.astype(BF16)
    return hi, (v - hi.astype(F32)).astype(BF16)


def spread(v):
    return jnp.broadcast_to(v, (8, 128))


def invert_block(block_ref, inv_ref):
    lane = lax.broadcasted_iota(jnp.int32, (8, 128), 1)
    sub = lax.broadcasted_iota(jnp.int32, (8, 128), 0)
    rows = [block_ref[8 * i:8 * i + 8, :] for i in range(16)]
    aug = [(lane == sub + 8 * i).astype(F32) for i in range(16)]
    for j in range(16):
        mine, extra = rows[j], aug[j]
        cols = [spread(mine[:, 8 * j + q:8 * j + q + 1]) for q in range(8)]
        a = [[None] * 8 for _ in range(8)]
        for q in range(8):
            for s in range(q, 8):
                a[s][q] = spread(cols[q][s:s + 1, :])
        r = [spread(mine[t:t + 1, :]) for t in range(8)] if j < 15 else None
        e = [spread(extra[t:t + 1, :]) for t in range(8)]
        rinv = [None] * 8
        low = [[None] * 8 for _ in range(8)]
        for t in range(8):
            rinv[t] = 1.0 / a[t][t]
            for s in range(t + 1, 8):
                low[s][t] = a[s][t] * rinv[t]
            for s in range(t + 1, 8):
                for k in range(t + 1, s + 1):
                    a[s][k] = a[s][k] - low[s][t] * a[k][t]
            for s in range(t + 1, 8):
                if r is not None:
                    r[s] = r[s] - low[s][t] * r[t]
                e[s] = e[s] - low[s][t] * e[t]
        packed_d = a[0][0]
        packed_e = e[0]
        for t in range(1, 8):
            packed_d = jnp.where(sub == t, a[t][t], packed_d)
            packed_e = jnp.where(sub == t, e[t], packed_e)
        inv_ref[8 * j:8 * j + 8, :] = packed_e * lax.rsqrt(packed_d)
        if j == 15:
            break
        w = [r[t] * rinv[t] for t in range(8)]
        we = [e[t] * rinv[t] for t in range(8)]
        for s in range(7, 0, -1):
            for t in range(s):
                w[t] = w[t] - low[s][t] * w[s]
                we[t] = we[t] - low[s][t] * we[s]
        for i in range(j + 1, 16):
            c = [spread(rows[i][:, 8 * j + q:8 * j + q + 1]) for q in range(8)]
            acc = c[0] * w[0]
            acce = c[0] * we[0]
            for q in range(1, 8):
                acc = acc + c[q] * w[q]
                acce = acce + c[q] * we[q]
            rows[i] = rows[i] - acc
            aug[i] = aug[i] - acce


ORDERS = ((0, 1, 2), (1, 2, 0), (2, 0, 1))


def gather_kernel(colors, in_ref, out_ref, own_sem, send, recv, psend, precv):
    prow, pcol = lax.axis_index("prow"), lax.axis_index("pcol")
    me = (pcol // 4, pcol % 4, prow // 2)
    core = prow % 2

    def device(dim, shift):
        at = [lax.rem(v + shift + 4, 4) if d == dim else v for d, v in enumerate(me)]
        return (at[2] * 2 + core, at[0] * 4 + at[1])
    partner = (me[2] * 2 + 1 - core, pcol)
    barrier = pltpu.get_barrier_semaphore()
    for dim in range(3):
        for shift in (1, -1):
            pl.semaphore_signal(barrier, inc=1, device_id=device(dim, shift), device_id_type=MESH)
    pl.semaphore_signal(barrier, inc=1, device_id=partner, device_id_type=MESH)
    own = pltpu.make_async_copy(in_ref, out_ref.at[me[0], me[1], me[2], core], own_sem)
    own.start()
    pl.semaphore_wait(barrier, 7)

    def view(c, phase, shift, half, whose=core):
        order = ORDERS[c]
        (r0, rm, r1), (c0, c1) = colors[c]
        at = list(me)
        for j in range(phase):
            at[order[j]] = slice(None)
        at[order[phase]] = lax.rem(me[order[phase]] + shift + 4, 4)
        rows = {0: (r0, rm), 1: (rm, r1), 2: (r0, r1)}[half]
        return out_ref.at[at[0], at[1], at[2], whose, pl.ds(rows[0], rows[1] - rows[0]), pl.ds(c0, c1 - c0)]

    def ring(c, phase, which):
        dim = ORDERS[c][phase]
        shift, half, to = ((0, 2, 1), (0, 2, -1), (-1, 0, 1), (1, 1, -1))[which]
        src = view(c, phase, shift, half)
        dst = src
        if phase == 0 and which < 2:
            (r0, rm, r1), (c0, c1) = colors[c]
            src = in_ref.at[pl.ds(r0, r1 - r0), pl.ds(c0, c1 - c0)]
        n = (c * 3 + phase) * 4 + which
        return pltpu.make_async_remote_copy(src, dst, send.at[n], recv.at[n], device_id=device(dim, to), device_id_type=MESH)

    def landed(c, phase, which):
        dim = ORDERS[c][phase]
        shift, half = ((-1, 2), (1, 2), (2, 0), (2, 1))[which]
        got = view(c, phase, shift, half)
        n = (c * 3 + phase) * 4 + which
        pltpu.make_async_remote_copy(got, got, send.at[n], recv.at[n], device_id=device(dim, 1), device_id_type=MESH).wait_recv()

    def across(c, which, whose):
        shift, half = ((0, 2), (-1, 2), (1, 2), (2, 0), (2, 1))[which]
        part = view(c, 2, shift, half, whose)
        n = c * 5 + which
        return pltpu.make_async_remote_copy(part, part, psend.at[n], precv.at[n], device_id=partner, device_id_type=MESH)

    for c in range(3):
        ring(c, 0, 0).start()
        ring(c, 0, 1).start()
    for phase in range(3):
        for c in range(3):
            landed(c, phase, 0)
            ring(c, phase, 2).start()
            if phase == 2:
                across(c, 1, core).start()
            landed(c, phase, 1)
            ring(c, phase, 3).start()
            if phase == 2:
                across(c, 2, core).start()
        if phase == 0:
            own.wait()
        for c in range(3):
            landed(c, phase, 2)
            if phase == 2:
                across(c, 3, core).start()
            landed(c, phase, 3)
            if phase == 2:
                across(c, 4, core).start()
            else:
                ring(c, phase + 1, 0).start()
                ring(c, phase + 1, 1).start()
                if phase == 1:
                    across(c, 0, core).start()
    for c in range(3):
        for which in range(5):
            across(c, which, core).wait_send()
            across(c, which, 1 - core).wait_recv()
        for phase in range(3):
            for which in range(4):
                ring(c, phase, which).wait_send()


def gather_all(block, colors, ident):
    return pl.pallas_call(
        functools.partial(gather_kernel, colors),
        out_shape=jax.ShapeDtypeStruct((4, 4, 4, 2) + block.shape, block.dtype),
        in_specs=[pl.BlockSpec(memory_space=pltpu.VMEM)],
        out_specs=pl.BlockSpec(memory_space=pl.ANY),
        scratch_shapes=[
            pltpu.SemaphoreType.DMA,
            pltpu.SemaphoreType.DMA((36,)),
            pltpu.SemaphoreType.DMA((36,)),
            pltpu.SemaphoreType.DMA((15,)),
            pltpu.SemaphoreType.DMA((15,)),
        ],
        compiler_params=pltpu.CompilerParams(collective_id=ident, has_side_effects=True),
        name="gather_all_%d" % ident,
    )(block)


F_COLORS = (((0, 16, 32), (0, 640)), ((0, 16, 32), (640, 1280)), ((0, 16, 32), (1280, 2048)))
S_COLORS = (((0, 16, 24), (0, 128)), ((24, 32, 48), (0, 128)), ((48, 56, 64), (0, 128)))


def factor_kernel(tiles_ref, front_ref, top_ref, rest_ref, inv_hi_ref, inv_lo_ref, low_hi_ref, low_lo_ref,
                  a_ref, diag_ref, inv_ref, pcat_ref, qcat_ref, icat_ref, own_sem, send, recv):
    prow, pcol = lax.axis_index("prow"), lax.axis_index("pcol")
    barrier = pltpu.get_barrier_semaphore()
    for s in range(1, 16):
        pl.semaphore_signal(barrier, inc=1, device_id=(prow, lax.rem(pcol + s, 16)), device_id_type=MESH)
    for s in range(1, 8):
        pl.semaphore_signal(barrier, inc=1, device_id=(lax.rem(prow + s, 8), pcol), device_id_type=MESH)
    pl.semaphore_wait(barrier, 22)

    def front_place(c):
        return rest_ref.at[pl.ds(pl.multiple_of(c * NB, NB), NB), pl.ds(0, 512)]

    def top_place(p, h):
        return rest_ref.at[pl.ds(pl.multiple_of(h * 512 + p * NB, NB), NB), pl.ds(512, 256)]

    def front_copy(s):
        return pltpu.make_async_remote_copy(
            front_ref, front_place(pcol), send.at[s - 1], recv.at[s - 1],
            device_id=(prow, lax.rem(pcol + s, 16)), device_id_type=MESH)

    def top_copy(s, h):
        n = 15 + (s - 1) * 2 + h
        return pltpu.make_async_remote_copy(
            top_ref.at[pl.ds(h * NB, NB)], top_place(prow, h), send.at[n], recv.at[n],
            device_id=(lax.rem(prow + s, 8), pcol), device_id_type=MESH)
    own = [pltpu.make_async_copy(front_ref, front_place(pcol), own_sem.at[0])]
    for h in range(2):
        own.append(pltpu.make_async_copy(top_ref.at[pl.ds(h * NB, NB)], top_place(prow, h), own_sem.at[1 + h]))
    for c in own:
        c.start()
    for s in range(1, 16):
        front_copy(s).start()
    for s in range(1, 8):
        for h in range(2):
            top_copy(s, h).start()

    def fill(i, carry):
        for k in range(8):
            a_ref[pl.ds(pl.multiple_of(i * NB, NB), NB), 128 * k:128 * k + 128] = tiles_ref[i * 8 + k]
        return carry
    lax.fori_loop(0, 16, fill, 0)

    def step(j, carry):
        off = pl.multiple_of(j * 128, 128)
        diag_ref[...] = a_ref[pl.ds(off, 128), pl.ds(off, 128)]
        invert_block(diag_ref, inv_ref)
        hi, lo = split(inv_ref[...])
        inv_hi_ref[pl.ds(off, 128), :] = hi
        inv_lo_ref[pl.ds(off, 128), :] = lo
        icat_ref[:, 0:128] = hi
        icat_ref[:, 128:256] = hi
        icat_ref[:, 256:384] = lo
        first = (j + 1) // 2

        def panel(r, c):
            base = pl.multiple_of(r * 256, 256)
            hi, lo = split(a_ref[pl.ds(base, 256), pl.ds(off, 128)])
            v = lax.dot_general(jnp.concatenate([hi, lo, hi], axis=1), icat_ref[...], TN, preferred_element_type=F32)
            hi, lo = split(v)
            pcat_ref[pl.ds(base, 256), 0:128] = hi
            pcat_ref[pl.ds(base, 256), 128:256] = lo
            pcat_ref[pl.ds(base, 256), 256:384] = hi
            qcat_ref[pl.ds(base, 256), 0:128] = hi
            qcat_ref[pl.ds(base, 256), 128:256] = hi
            qcat_ref[pl.ds(base, 256), 256:384] = lo
            low_hi_ref[pl.ds(base, 256), pl.ds(off, 128)] = hi
            low_lo_ref[pl.ds(base, 256), pl.ds(off, 128)] = lo
            return c
        lax.fori_loop(first, KK // 256, panel, 0)

        def update(r, c):
            base = pl.multiple_of(r * 256, 256)

            def inner(k, c):
                cb = pl.multiple_of(k * 256, 256)
                a_ref[pl.ds(base, 256), pl.ds(cb, 256)] -= lax.dot_general(
                    pcat_ref[pl.ds(base, 256), :], qcat_ref[pl.ds(cb, 256), :], TN, preferred_element_type=F32)
                return c
            return lax.fori_loop(first, r + 1, inner, c)
        lax.fori_loop(first, KK // 256, update, 0)
        return carry
    lax.fori_loop(0, KK // 128, step, 0)
    for c in own:
        c.wait()
    for s in range(1, 16):
        front_copy(s).wait_send()
        place = front_place(lax.rem(pcol + 16 - s, 16))
        pltpu.make_async_remote_copy(place, place, send.at[s - 1], recv.at[s - 1],
                                     device_id=(prow, pcol), device_id_type=MESH).wait_recv()
    for s in range(1, 8):
        for h in range(2):
            n = 15 + (s - 1) * 2 + h
            top_copy(s, h).wait_send()
            place = top_place(lax.rem(prow + 8 - s, 8), h)
            pltpu.make_async_remote_copy(place, place, send.at[n], recv.at[n],
                                         device_id=(prow, pcol), device_id_type=MESH).wait_recv()


def factor(tiles, front, top):
    return pl.pallas_call(
        factor_kernel,
        out_shape=(
            jax.ShapeDtypeStruct((KK, 768), F32),
            jax.ShapeDtypeStruct((KK, 128), BF16),
            jax.ShapeDtypeStruct((KK, 128), BF16),
            jax.ShapeDtypeStruct((KK, KK), BF16),
            jax.ShapeDtypeStruct((KK, KK), BF16),
        ),
        in_specs=[pl.BlockSpec(memory_space=pltpu.VMEM)] * 3,
        out_specs=[pl.BlockSpec(memory_space=pltpu.VMEM)] * 5,
        scratch_shapes=[
            pltpu.VMEM((KK, KK), F32),
            pltpu.VMEM((128, 128), F32),
            pltpu.VMEM((128, 128), F32),
            pltpu.VMEM((KK, 384), BF16),
            pltpu.VMEM((KK, 384), BF16),
            pltpu.VMEM((128, 384), BF16),
            pltpu.SemaphoreType.DMA((3,)),
            pltpu.SemaphoreType.DMA((29,)),
            pltpu.SemaphoreType.DMA((29,)),
        ],
        compiler_params=pltpu.CompilerParams(collective_id=3, has_side_effects=True, vmem_limit_bytes=40 << 20),
        name="factor",
    )(tiles, front, top)


def solve_kernel(rest_ref, inv_hi_ref, inv_lo_ref, low_hi_ref, low_lo_ref, local_ref, trail_ref, panel_ref,
                 hi_ref, lo_ref, p_ref):
    for j in range(KK // 128):
        x = rest_ref[128 * j:128 * j + 128, :]
        if j:
            lh, ll = low_hi_ref[128 * j:128 * j + 128, :128 * j], low_lo_ref[128 * j:128 * j + 128, :128 * j]
            ph, pw = hi_ref[:128 * j, :], lo_ref[:128 * j, :]
            x = x - (lax.dot_general(lh, ph, NN, preferred_element_type=F32)
                     + lax.dot_general(lh, pw, NN, preferred_element_type=F32)
                     + lax.dot_general(ll, ph, NN, preferred_element_type=F32))
        xh, xl = split(x)
        ih, il = inv_hi_ref[128 * j:128 * j + 128, :], inv_lo_ref[128 * j:128 * j + 128, :]
        v = (lax.dot_general(ih, xh, NN, preferred_element_type=F32)
             + lax.dot_general(ih, xl, NN, preferred_element_type=F32)
             + lax.dot_general(il, xh, NN, preferred_element_type=F32))
        p_ref[128 * j:128 * j + 128, :] = v[:, :512]
        vh, vl = split(v)
        hi_ref[128 * j:128 * j + 128, :] = vh
        lo_ref[128 * j:128 * j + 128, :] = vl
    rh, rl = hi_ref[:, :512], lo_ref[:, :512]
    ch, cl = hi_ref[:, 512:], lo_ref[:, 512:]
    trail_ref[...] = local_ref[...] - (lax.dot_general(rh, ch, TT, preferred_element_type=F32)
                                       + lax.dot_general(rh, cl, TT, preferred_element_type=F32)
                                       + lax.dot_general(rl, ch, TT, preferred_element_type=F32))
    pcol = lax.axis_index("pcol")
    panel_ref[...] = p_ref[pl.ds(pl.multiple_of(pcol * NB, NB), NB), :].T


def solve(rest, inv_hi, inv_lo, low_hi, low_lo, local):
    return pl.pallas_call(
        solve_kernel,
        out_shape=(jax.ShapeDtypeStruct((512, 256), F32), jax.ShapeDtypeStruct((512, NB), F32)),
        in_specs=[pl.BlockSpec(memory_space=pltpu.VMEM)] * 6,
        out_specs=[pl.BlockSpec(memory_space=pltpu.VMEM)] * 2,
        scratch_shapes=[pltpu.VMEM((KK, 768), BF16)] * 2 + [pltpu.VMEM((KK, 512), F32)],
        compiler_params=pltpu.CompilerParams(vmem_limit_bytes=40 << 20),
        name="solve",
    )(rest, inv_hi, inv_lo, low_hi, low_lo, local)


def pair_kernel(rows_ref, mats_ref, local_ref, front_ref, tile_ref, x_ref, z_ref):
    depth = mats_ref.shape[0]
    for r in range(RANK):
        images = jnp.dot(rows_ref[:, r * depth:(r + 1) * depth], mats_ref[...], preferred_element_type=F32).astype(BF16)
        x_ref[r] = images[:, :depth]
        z_ref[r] = images[:, depth:]

    def pair(base, m, other, n):
        acc = None
        for r in range(RANK):
            for q in range(RANK):
                inner_x = lax.dot_general(x_ref[r, pl.ds(base, m), :], x_ref[q, other:other + n, :], TN, preferred_element_type=F32)
                inner_z = lax.dot_general(z_ref[r, pl.ds(base, m), :], z_ref[q, other:other + n, :], TN, preferred_element_type=F32)
                term = inner_x * inner_z
                if acc is None:
                    acc = term
                elif SIGNS[r] * SIGNS[q] > 0:
                    acc = acc + term
                else:
                    acc = acc - term
        return acc

    tile_ref[...] = pair(512, 64, 768, 128)

    def chunk(i, carry):
        base = pl.multiple_of(i * 128, 128)
        block = pair(base, 128, 512, 256)
        local_ref[pl.ds(base, 128), :] = block
        front_ref[:, pl.ds(base, 128)] = block[:, :128].T[:NB, :]
        return carry
    lax.fori_loop(0, 4, chunk, 0)


def pair_blocks(rows, mats):
    n, d = rows.shape[0], mats.shape[0]
    return pl.pallas_call(
        pair_kernel,
        out_shape=(
            jax.ShapeDtypeStruct((512, 256), F32),
            jax.ShapeDtypeStruct((NB, 512), F32),
            jax.ShapeDtypeStruct((NB, 128), F32),
        ),
        in_specs=[pl.BlockSpec(memory_space=pltpu.VMEM)] * 2,
        out_specs=[pl.BlockSpec(memory_space=pltpu.VMEM)] * 3,
        scratch_shapes=[pltpu.VMEM((RANK, n, d), BF16)] * 2,
        compiler_params=pltpu.CompilerParams(vmem_limit_bytes=48 << 20),
        name="pairs",
    )(rows, mats)


def per_device(factors, x_factor, zinv_factor, placement):
    rows_dev = factors.shape[1]
    total_rows = placement.shape[0]
    prow, pcol = lax.axis_index("prow"), lax.axis_index("pcol")
    flat = factors.transpose(1, 0, 2).reshape(rows_dev, -1)
    everything = gather_all(flat, F_COLORS, 1).reshape(total_rows, -1)
    k = jnp.arange(512)
    kc = jnp.arange(256)
    wanted = jnp.concatenate([
        k // NB * (NB * 8) + prow * NB + k % NB,
        kc // NB * (NB * 16) + pcol * NB + kc % NB,
        prow * 128 + jnp.arange(128),
    ])
    slot = jnp.arange(total_rows)
    device = slot // rows_dev
    place = (device % 16 * 8 + device // 16) * rows_dev + slot % rows_dev
    where = jnp.sum(jnp.where(wanted[:, None] == placement[None, :], place[None, :], 0), axis=1)
    rows = everything[where]
    mats = jnp.concatenate([x_factor, zinv_factor], axis=1)
    local, front, tile = pair_blocks(rows, mats)
    tiles = gather_all(tile, S_COLORS, 2).reshape(128, NB, 128)
    rest, inv_hi, inv_lo, low_hi, low_lo = factor(tiles, front, local[:128])
    return solve(rest, inv_hi, inv_lo, low_hi, low_lo, local)


def solution(mesh):
    in_specs = (P(None, ("prow", "pcol"), None), P(), P(), P())
    out_specs = (P("prow", "pcol"), P("prow", "pcol"))
    return jax.shard_map(per_device, mesh=mesh, in_specs=in_specs, out_specs=out_specs, check_vma=False)
```

```python
import functools
import jax
import jax.numpy as jnp
from jax import lax
from jax.experimental import pallas as pl
from jax.experimental.pallas import tpu as pltpu
from jax.sharding import PartitionSpec as P

RANK = 4
NB = 64
KK = 1024
F32, BF16 = jnp.float32, jnp.bfloat16
SIGNS = (1.0, 1.0, -1.0, -1.0)
MESH = pl.DeviceIdType.MESH
TN = (((1,), (1,)), ((), ()))
NN = (((1,), (0,)), ((), ()))
TT = (((0,), (0,)), ((), ()))


def split(v):
    hi = v.astype(BF16)
    return hi, (v - hi.astype(F32)).astype(BF16)


def spread(v):
    return jnp.broadcast_to(v, (8, 128))


def invert_block(block_ref, inv_ref):
    lane = lax.broadcasted_iota(jnp.int32, (8, 128), 1)
    sub = lax.broadcasted_iota(jnp.int32, (8, 128), 0)
    rows = [block_ref[8 * i:8 * i + 8, :] for i in range(16)]
    aug = [(lane == sub + 8 * i).astype(F32) for i in range(16)]
    for j in range(16):
        mine, extra = rows[j], aug[j]
        cols = [spread(mine[:, 8 * j + q:8 * j + q + 1]) for q in range(8)]
        a = [[None] * 8 for _ in range(8)]
        for q in range(8):
            for s in range(q, 8):
                a[s][q] = spread(cols[q][s:s + 1, :])
        r = [spread(mine[t:t + 1, :]) for t in range(8)] if j < 15 else None
        e = [spread(extra[t:t + 1, :]) for t in range(8)]
        rinv = [None] * 8
        low = [[None] * 8 for _ in range(8)]
        for t in range(8):
            rinv[t] = 1.0 / a[t][t]
            for s in range(t + 1, 8):
                low[s][t] = a[s][t] * rinv[t]
            for s in range(t + 1, 8):
                for k in range(t + 1, s + 1):
                    a[s][k] = a[s][k] - low[s][t] * a[k][t]
            for s in range(t + 1, 8):
                if r is not None:
                    r[s] = r[s] - low[s][t] * r[t]
                e[s] = e[s] - low[s][t] * e[t]
        packed_d = a[0][0]
        packed_e = e[0]
        for t in range(1, 8):
            packed_d = jnp.where(sub == t, a[t][t], packed_d)
            packed_e = jnp.where(sub == t, e[t], packed_e)
        inv_ref[8 * j:8 * j + 8, :] = packed_e * lax.rsqrt(packed_d)
        if j == 15:
            break
        w = [r[t] * rinv[t] for t in range(8)]
        we = [e[t] * rinv[t] for t in range(8)]
        for s in range(7, 0, -1):
            for t in range(s):
                w[t] = w[t] - low[s][t] * w[s]
                we[t] = we[t] - low[s][t] * we[s]
        for i in range(j + 1, 16):
            c = [spread(rows[i][:, 8 * j + q:8 * j + q + 1]) for q in range(8)]
            acc = c[0] * w[0]
            acce = c[0] * we[0]
            for q in range(1, 8):
                acc = acc + c[q] * w[q]
                acce = acce + c[q] * we[q]
            rows[i] = rows[i] - acc
            aug[i] = aug[i] - acce


ORDERS = ((0, 1, 2), (1, 2, 0), (2, 0, 1))
COLORS = (((0, 16, 24), (0, 128)), ((24, 32, 48), (0, 128)), ((48, 56, 64), (0, 128)))


W = 2176


def before(n):
    return (lax.broadcasted_iota(jnp.int32, (n, n), 0) > lax.broadcasted_iota(jnp.int32, (n, n), 1)).astype(BF16)


def earlier(mask):
    n = mask.shape[0]
    wide = jnp.broadcast_to(mask.astype(F32), (n, 128)).astype(BF16)
    return jnp.dot(before(n), wide, preferred_element_type=F32)[:, 0:1].astype(jnp.int32)


def pick(index, valid, n):
    lane = lax.broadcasted_iota(jnp.int32, (index.shape[0], n), 1)
    hit = lane == index
    if valid is not None:
        hit = hit & valid
    return hit.astype(F32).astype(BF16)


def route_kernel(flat_ref, mine_ref, order_ref, rows_ref, cols_ref,
                 send_a, got_a, send_b, got_b, piece_ref, ss, rs):
    prow, pcol = lax.axis_index("prow"), lax.axis_index("pcol")
    twin = (lax.rem(pcol, 8), prow + 8 * (pcol // 8))
    at_home = prow == lax.rem(pcol, 8)
    barrier = pltpu.get_barrier_semaphore()
    for s in range(1, 16):
        pl.semaphore_signal(barrier, inc=1, device_id=(prow, lax.rem(pcol + s, 16)), device_id_type=MESH)
    for s in range(1, 8):
        pl.semaphore_signal(barrier, inc=1, device_id=(lax.rem(prow + s, 8), pcol), device_id_type=MESH)

    @pl.when(jnp.logical_not(at_home))
    def _():
        pl.semaphore_signal(barrier, inc=1, device_id=twin, device_id_type=MESH)

    group = (mine_ref[...] >> 6) & 7
    row = lax.broadcasted_iota(jnp.int32, (64, 32), 0)
    match = group == (row >> 3)
    ahead = (lax.broadcasted_iota(jnp.int32, (32, 32), 0) < lax.broadcasted_iota(jnp.int32, (32, 32), 1)).astype(BF16)
    rank = jnp.dot(match.astype(F32).astype(BF16), ahead, preferred_element_type=F32).astype(jnp.int32)
    sel = (match & (rank == (row & 7))).astype(F32).astype(BF16)
    send_a[...] = jnp.dot(sel, flat_ref[...], preferred_element_type=F32).reshape(8, 8, W).astype(BF16)
    got_a[prow] = send_a[prow]

    kind = (order_ref[...] >> 6) & 15
    prior = lax.broadcasted_iota(jnp.int32, kind.shape, 0) < pcol
    base = [jnp.sum((prior & (kind == prow + 8 * h)).astype(F32), keepdims=True).astype(jnp.int32) for h in range(2)]

    pl.semaphore_wait(barrier, jnp.where(at_home, 22, 23))

    def copy(src, dst, n, to):
        return pltpu.make_async_remote_copy(src, dst, ss.at[n], rs.at[n], device_id=to, device_id_type=MESH)

    def along_prow(s):
        return (lax.rem(prow + s, 8), pcol)

    def along_pcol(s):
        return (prow, lax.rem(pcol + s, 16))

    def slab(ref, i, n):
        return ref.at[pl.ds(pl.multiple_of(i * n, n), n)]

    def a_copy(s):
        return copy(send_a.at[lax.rem(prow + s, 8)], got_a.at[prow], s - 1, along_prow(s))

    def b_copy(s):
        return copy(send_b.at[lax.rem(pcol + s, 16)], got_b.at[pcol], 7 + s - 1, along_pcol(s))

    def row_copy(s):
        return copy(piece_ref, slab(rows_ref, pcol, 32), 22 + s - 1, along_pcol(s))

    def twin_copy():
        return copy(piece_ref, slab(cols_ref, twin[0], 32), 37, twin)

    def col_copy(s):
        return copy(slab(cols_ref, prow, 32), slab(cols_ref, prow, 32), 38 + s - 1, along_prow(s))

    for s in range(1, 8):
        a_copy(s).start()
    for s in range(1, 8):
        spot = got_a.at[lax.rem(prow + 8 - s, 8)]
        copy(spot, spot, s - 1, along_prow(1)).wait_recv()

    got = got_a[...].astype(F32).reshape(64, W).astype(BF16)
    tags = got[:, 2048:].astype(F32)
    valid = tags[:, 2:3] > 0.5
    half = (tags[:, 0:1].astype(jnp.int32) >> 3) & 1
    slot = jnp.zeros((64, 1), jnp.int32)
    for h in range(2):
        li = earlier(valid & (half == h))
        slot = jnp.where(half == h, (8 * h + ((base[h] + li) & 7)) * 8 + (li >> 3), slot)
    send_b[...] = lax.dot_general(pick(slot, valid, 128), got, TT, preferred_element_type=F32).reshape(16, 8, W).astype(BF16)
    got_b[pcol] = send_b[pcol]
    for s in range(1, 16):
        b_copy(s).start()
    for s in range(1, 16):
        spot = got_b.at[lax.rem(pcol + 16 - s, 16)]
        copy(spot, spot, 7 + s - 1, along_prow(1)).wait_recv()

    got = got_b[...].astype(F32).reshape(128, W).astype(BF16)
    valid = got[:, 2048:].astype(F32)[:, 2:3] > 0.5
    piece = lax.dot_general(pick(earlier(valid), valid, 32), got, TT, preferred_element_type=F32).astype(BF16)
    piece_ref[...] = piece
    rows_ref[pl.ds(pl.multiple_of(pcol * 32, 32), 32), :] = piece

    @pl.when(at_home)
    def _():
        cols_ref[pl.ds(pl.multiple_of(prow * 32, 32), 32), :] = piece

    @pl.when(jnp.logical_not(at_home))
    def _():
        twin_copy().start()
    for s in range(1, 16):
        row_copy(s).start()

    @pl.when(jnp.logical_not(at_home))
    def _():
        spot = slab(cols_ref, prow, 32)
        copy(spot, spot, 37, twin).wait_recv()
    for s in range(1, 8):
        col_copy(s).start()
    for s in range(1, 8):
        spot = slab(cols_ref, lax.rem(prow + 8 - s, 8), 32)
        copy(spot, spot, 38 + s - 1, along_prow(1)).wait_recv()
    for s in range(1, 16):
        spot = slab(rows_ref, lax.rem(pcol + 16 - s, 16), 32)
        copy(spot, spot, 22 + s - 1, along_prow(1)).wait_recv()
    for s in range(1, 8):
        a_copy(s).wait_send()
        col_copy(s).wait_send()
    for s in range(1, 16):
        b_copy(s).wait_send()
        row_copy(s).wait_send()

    @pl.when(jnp.logical_not(at_home))
    def _():
        twin_copy().wait_send()


def route(flat, mine, order):
    return pl.pallas_call(
        route_kernel,
        out_shape=(jax.ShapeDtypeStruct((512, W), BF16), jax.ShapeDtypeStruct((256, W), BF16)),
        in_specs=[pl.BlockSpec(memory_space=pltpu.VMEM)] * 3,
        out_specs=[pl.BlockSpec(memory_space=pltpu.VMEM)] * 2,
        scratch_shapes=[
            pltpu.VMEM((8, 8, W), BF16),
            pltpu.VMEM((8, 8, W), BF16),
            pltpu.VMEM((16, 8, W), BF16),
            pltpu.VMEM((16, 8, W), BF16),
            pltpu.VMEM((32, W), BF16),
            pltpu.SemaphoreType.DMA((45,)),
            pltpu.SemaphoreType.DMA((45,)),
        ],
        compiler_params=pltpu.CompilerParams(collective_id=1, has_side_effects=True, vmem_limit_bytes=24 << 20),
        name="route",
    )(flat, mine, order)


def pair_kernel(rows_ref, cols_ref, mats_ref, local_ref, front_ref, out_ref, in_ref, x_ref, z_ref, own_sem, send, recv, psend, precv):
    colors = COLORS
    prow, pcol = lax.axis_index("prow"), lax.axis_index("pcol")
    me = (pcol // 4, pcol % 4, prow // 2)
    core = prow % 2

    def device(dim, shift):
        at = [lax.rem(v + shift + 4, 4) if d == dim else v for d, v in enumerate(me)]
        return (at[2] * 2 + core, at[0] * 4 + at[1])
    partner = (me[2] * 2 + 1 - core, pcol)
    barrier = pltpu.get_barrier_semaphore()
    for dim in range(3):
        for shift in (1, -1):
            pl.semaphore_signal(barrier, inc=1, device_id=device(dim, shift), device_id_type=MESH)
    pl.semaphore_signal(barrier, inc=1, device_id=partner, device_id_type=MESH)
    depth = mats_ref.shape[0]

    def load(src, first, count, shift, at):
        tags = src[:, 2048:].astype(F32).astype(jnp.int32)
        spot = (tags[:, 0:1] >> shift) * NB + tags[:, 1:2] - first
        rows = lax.dot_general(pick(spot, None, count), src[:, :2048], TT, preferred_element_type=F32).astype(BF16)
        for r in range(RANK):
            images = jnp.dot(rows[:, r * depth:(r + 1) * depth], mats_ref[...], preferred_element_type=F32).astype(BF16)
            x_ref[r, at:at + count, :] = images[:, :depth]
            z_ref[r, at:at + count, :] = images[:, depth:]

    def pair(base, m, other, n):
        acc = None
        for r in range(RANK):
            for q in range(RANK):
                inner_x = lax.dot_general(x_ref[r, base:base + m, :], x_ref[q, other:other + n, :], TN, preferred_element_type=F32)
                inner_z = lax.dot_general(z_ref[r, base:base + m, :], z_ref[q, other:other + n, :], TN, preferred_element_type=F32)
                term = inner_x * inner_z
                if acc is None:
                    acc = term
                elif SIGNS[r] * SIGNS[q] > 0:
                    acc = acc + term
                else:
                    acc = acc - term
        return acc

    def chunk(base):
        block = pair(base, 128, 512, 256)
        local_ref[base:base + 128, :] = block
        front_ref[:, base:base + 128] = block[:, :128].T[:NB, :]

    load(cols_ref, 0, 64, 4, 512)
    load(rows_ref, 0, 128, 3, 0)
    in_ref[...] = pair(512, 64, 0, 128)
    own = pltpu.make_async_copy(in_ref, out_ref.at[me[0], me[1], me[2], core], own_sem)
    own.start()
    pl.semaphore_wait(barrier, 7)

    def view(c, phase, shift, half, whose=core):
        order = ORDERS[c]
        (r0, rm, r1), (c0, c1) = colors[c]
        at = list(me)
        for j in range(phase):
            at[order[j]] = slice(None)
        at[order[phase]] = lax.rem(me[order[phase]] + shift + 4, 4)
        rows = {0: (r0, rm), 1: (rm, r1), 2: (r0, r1)}[half]
        return out_ref.at[at[0], at[1], at[2], whose, pl.ds(rows[0], rows[1] - rows[0]), pl.ds(c0, c1 - c0)]

    def ring(c, phase, which):
        dim = ORDERS[c][phase]
        shift, half, to = ((0, 2, 1), (0, 2, -1), (-1, 0, 1), (1, 1, -1))[which]
        src = view(c, phase, shift, half)
        dst = src
        if phase == 0 and which < 2:
            (r0, rm, r1), (c0, c1) = colors[c]
            src = in_ref.at[pl.ds(r0, r1 - r0), pl.ds(c0, c1 - c0)]
        n = (c * 3 + phase) * 4 + which
        return pltpu.make_async_remote_copy(src, dst, send.at[n], recv.at[n], device_id=device(dim, to), device_id_type=MESH)

    def landed(c, phase, which):
        dim = ORDERS[c][phase]
        shift, half = ((-1, 2), (1, 2), (2, 0), (2, 1))[which]
        got = view(c, phase, shift, half)
        n = (c * 3 + phase) * 4 + which
        pltpu.make_async_remote_copy(got, got, send.at[n], recv.at[n], device_id=device(dim, 1), device_id_type=MESH).wait_recv()

    def across(c, which, whose):
        shift, half = ((0, 2), (-1, 2), (1, 2), (2, 0), (2, 1))[which]
        part = view(c, 2, shift, half, whose)
        n = c * 5 + which
        return pltpu.make_async_remote_copy(part, part, psend.at[n], precv.at[n], device_id=partner, device_id_type=MESH)

    for c in range(3):
        ring(c, 0, 0).start()
        ring(c, 0, 1).start()
    jobs = [
        lambda: load(cols_ref, 64, 192, 4, 576),
        lambda: load(rows_ref, 128, 384, 3, 128),
        lambda: chunk(0),
        lambda: chunk(128),
        lambda: chunk(256),
        lambda: chunk(384),
    ]
    for phase in range(3):
        jobs[2 * phase]()
        for c in range(3):
            landed(c, phase, 0)
            ring(c, phase, 2).start()
            if phase == 2:
                across(c, 1, core).start()
            landed(c, phase, 1)
            ring(c, phase, 3).start()
            if phase == 2:
                across(c, 2, core).start()
        if phase == 0:
            own.wait()
        jobs[2 * phase + 1]()
        for c in range(3):
            landed(c, phase, 2)
            if phase == 2:
                across(c, 3, core).start()
            landed(c, phase, 3)
            if phase == 2:
                across(c, 4, core).start()
            else:
                ring(c, phase + 1, 0).start()
                ring(c, phase + 1, 1).start()
                if phase == 1:
                    across(c, 0, core).start()
    for c in range(3):
        for which in range(5):
            across(c, which, core).wait_send()
            across(c, which, 1 - core).wait_recv()
        for phase in range(3):
            for which in range(4):
                ring(c, phase, which).wait_send()


def pair_blocks(rows, cols, mats):
    d = mats.shape[0]
    return pl.pallas_call(
        pair_kernel,
        out_shape=(
            jax.ShapeDtypeStruct((512, 256), F32),
            jax.ShapeDtypeStruct((NB, 512), F32),
            jax.ShapeDtypeStruct((4, 4, 4, 2, NB, 128), F32),
        ),
        in_specs=[pl.BlockSpec(memory_space=pltpu.VMEM)] * 3,
        out_specs=[pl.BlockSpec(memory_space=pltpu.VMEM)] * 3,
        scratch_shapes=[
            pltpu.VMEM((NB, 128), F32),
            pltpu.VMEM((RANK, 768, d), BF16),
            pltpu.VMEM((RANK, 768, d), BF16),
            pltpu.SemaphoreType.DMA,
            pltpu.SemaphoreType.DMA((36,)),
            pltpu.SemaphoreType.DMA((36,)),
            pltpu.SemaphoreType.DMA((15,)),
            pltpu.SemaphoreType.DMA((15,)),
        ],
        compiler_params=pltpu.CompilerParams(collective_id=2, has_side_effects=True, vmem_limit_bytes=40 << 20),
        name="pairs",
    )(rows, cols, mats)


def factor_kernel(tiles_ref, front_ref, top_ref, rest_ref, inv_hi_ref, inv_lo_ref, low_hi_ref, low_lo_ref,
                  a_ref, diag_ref, inv_ref, pcat_ref, qcat_ref, icat_ref, own_sem, send, recv):
    prow, pcol = lax.axis_index("prow"), lax.axis_index("pcol")
    barrier = pltpu.get_barrier_semaphore()
    for s in range(1, 16):
        pl.semaphore_signal(barrier, inc=1, device_id=(prow, lax.rem(pcol + s, 16)), device_id_type=MESH)
    for s in range(1, 8):
        pl.semaphore_signal(barrier, inc=1, device_id=(lax.rem(prow + s, 8), pcol), device_id_type=MESH)
    pl.semaphore_wait(barrier, 22)

    def front_place(c):
        return rest_ref.at[pl.ds(pl.multiple_of(c * NB, NB), NB), pl.ds(0, 512)]

    def top_place(p, h):
        return rest_ref.at[pl.ds(pl.multiple_of(h * 512 + p * NB, NB), NB), pl.ds(512, 256)]

    def front_copy(s):
        return pltpu.make_async_remote_copy(
            front_ref, front_place(pcol), send.at[s - 1], recv.at[s - 1],
            device_id=(prow, lax.rem(pcol + s, 16)), device_id_type=MESH)

    def top_copy(s, h):
        n = 15 + (s - 1) * 2 + h
        return pltpu.make_async_remote_copy(
            top_ref.at[pl.ds(h * NB, NB)], top_place(prow, h), send.at[n], recv.at[n],
            device_id=(lax.rem(prow + s, 8), pcol), device_id_type=MESH)
    own = [pltpu.make_async_copy(front_ref, front_place(pcol), own_sem.at[0])]
    for h in range(2):
        own.append(pltpu.make_async_copy(top_ref.at[pl.ds(h * NB, NB)], top_place(prow, h), own_sem.at[1 + h]))
    for c in own:
        c.start()
    for s in range(1, 16):
        front_copy(s).start()
    for s in range(1, 8):
        for h in range(2):
            top_copy(s, h).start()

    left = lax.broadcasted_iota(jnp.int32, (NB, 128), 1) < NB

    def fill(i, carry):
        at = pl.ds(pl.multiple_of(i * NB, NB), NB)
        for k in range(4):
            even, odd = tiles_ref[i * 8 + 2 * k], tiles_ref[i * 8 + 2 * k + 1]
            a_ref[at, 128 * k:128 * k + 128] = jnp.where(left, even, pltpu.roll(odd, NB, 1))
            a_ref[at, 512 + 128 * k:640 + 128 * k] = jnp.where(left, pltpu.roll(even, NB, 1), odd)
        return carry
    lax.fori_loop(0, 16, fill, 0)

    def step(j, carry):
        off = pl.multiple_of(j * 128, 128)
        diag_ref[...] = a_ref[pl.ds(off, 128), pl.ds(off, 128)]
        invert_block(diag_ref, inv_ref)
        hi, lo = split(inv_ref[...])
        inv_hi_ref[pl.ds(off, 128), :] = hi
        inv_lo_ref[pl.ds(off, 128), :] = lo
        icat_ref[:, 0:128] = hi
        icat_ref[:, 128:256] = hi
        icat_ref[:, 256:384] = lo
        first = (j + 1) // 2

        def panel(r, c):
            base = pl.multiple_of(r * 256, 256)
            hi, lo = split(a_ref[pl.ds(base, 256), pl.ds(off, 128)])
            v = lax.dot_general(jnp.concatenate([hi, lo, hi], axis=1), icat_ref[...], TN, preferred_element_type=F32)
            hi, lo = split(v)
            pcat_ref[pl.ds(base, 256), 0:128] = hi
            pcat_ref[pl.ds(base, 256), 128:256] = lo
            pcat_ref[pl.ds(base, 256), 256:384] = hi
            qcat_ref[pl.ds(base, 256), 0:128] = hi
            qcat_ref[pl.ds(base, 256), 128:256] = hi
            qcat_ref[pl.ds(base, 256), 256:384] = lo
            low_hi_ref[pl.ds(base, 256), pl.ds(off, 128)] = hi
            low_lo_ref[pl.ds(base, 256), pl.ds(off, 128)] = lo
            return c
        lax.fori_loop(first, KK // 256, panel, 0)

        def update(r, c):
            base = pl.multiple_of(r * 256, 256)

            def inner(k, c):
                cb = pl.multiple_of(k * 256, 256)
                a_ref[pl.ds(base, 256), pl.ds(cb, 256)] -= lax.dot_general(
                    pcat_ref[pl.ds(base, 256), :], qcat_ref[pl.ds(cb, 256), :], TN, preferred_element_type=F32)
                return c
            return lax.fori_loop(first, r + 1, inner, c)
        lax.fori_loop(first, KK // 256, update, 0)
        return carry
    lax.fori_loop(0, KK // 128, step, 0)
    for c in own:
        c.wait()
    for s in range(1, 16):
        front_copy(s).wait_send()
        place = front_place(lax.rem(pcol + 16 - s, 16))
        pltpu.make_async_remote_copy(place, place, send.at[s - 1], recv.at[s - 1],
                                     device_id=(prow, pcol), device_id_type=MESH).wait_recv()
    for s in range(1, 8):
        for h in range(2):
            n = 15 + (s - 1) * 2 + h
            top_copy(s, h).wait_send()
            place = top_place(lax.rem(prow + 8 - s, 8), h)
            pltpu.make_async_remote_copy(place, place, send.at[n], recv.at[n],
                                         device_id=(prow, pcol), device_id_type=MESH).wait_recv()


def factor(tiles, front, top):
    return pl.pallas_call(
        factor_kernel,
        out_shape=(
            jax.ShapeDtypeStruct((KK, 768), F32),
            jax.ShapeDtypeStruct((KK, 128), BF16),
            jax.ShapeDtypeStruct((KK, 128), BF16),
            jax.ShapeDtypeStruct((KK, KK), BF16),
            jax.ShapeDtypeStruct((KK, KK), BF16),
        ),
        in_specs=[pl.BlockSpec(memory_space=pltpu.VMEM)] * 3,
        out_specs=[pl.BlockSpec(memory_space=pltpu.VMEM)] * 5,
        scratch_shapes=[
            pltpu.VMEM((KK, KK), F32),
            pltpu.VMEM((128, 128), F32),
            pltpu.VMEM((128, 128), F32),
            pltpu.VMEM((KK, 384), BF16),
            pltpu.VMEM((KK, 384), BF16),
            pltpu.VMEM((128, 384), BF16),
            pltpu.SemaphoreType.DMA((3,)),
            pltpu.SemaphoreType.DMA((29,)),
            pltpu.SemaphoreType.DMA((29,)),
        ],
        compiler_params=pltpu.CompilerParams(collective_id=3, has_side_effects=True, vmem_limit_bytes=40 << 20),
        name="factor",
    )(tiles, front, top)


def solve_kernel(rest_ref, inv_hi_ref, inv_lo_ref, low_hi_ref, low_lo_ref, local_ref, trail_ref, panel_ref,
                 hi_ref, lo_ref, p_ref):
    for j in range(KK // 128):
        x = rest_ref[128 * j:128 * j + 128, :]
        if j:
            lh, ll = low_hi_ref[128 * j:128 * j + 128, :128 * j], low_lo_ref[128 * j:128 * j + 128, :128 * j]
            ph, pw = hi_ref[:128 * j, :], lo_ref[:128 * j, :]
            x = x - (lax.dot_general(lh, ph, NN, preferred_element_type=F32)
                     + lax.dot_general(lh, pw, NN, preferred_element_type=F32)
                     + lax.dot_general(ll, ph, NN, preferred_element_type=F32))
        xh, xl = split(x)
        ih, il = inv_hi_ref[128 * j:128 * j + 128, :], inv_lo_ref[128 * j:128 * j + 128, :]
        v = (lax.dot_general(ih, xh, NN, preferred_element_type=F32)
             + lax.dot_general(ih, xl, NN, preferred_element_type=F32)
             + lax.dot_general(il, xh, NN, preferred_element_type=F32))
        p_ref[128 * j:128 * j + 128, :] = v[:, :512]
        vh, vl = split(v)
        hi_ref[128 * j:128 * j + 128, :] = vh
        lo_ref[128 * j:128 * j + 128, :] = vl
    rh, rl = hi_ref[:, :512], lo_ref[:, :512]
    ch, cl = hi_ref[:, 512:], lo_ref[:, 512:]
    trail_ref[...] = local_ref[...] - (lax.dot_general(rh, ch, TT, preferred_element_type=F32)
                                       + lax.dot_general(rh, cl, TT, preferred_element_type=F32)
                                       + lax.dot_general(rl, ch, TT, preferred_element_type=F32))
    pcol = lax.axis_index("pcol")
    panel_ref[...] = p_ref[pl.ds(pl.multiple_of(pcol * NB, NB), NB), :].T


def solve(rest, inv_hi, inv_lo, low_hi, low_lo, local):
    return pl.pallas_call(
        solve_kernel,
        out_shape=(jax.ShapeDtypeStruct((512, 256), F32), jax.ShapeDtypeStruct((512, NB), F32)),
        in_specs=[pl.BlockSpec(memory_space=pltpu.VMEM)] * 6,
        out_specs=[pl.BlockSpec(memory_space=pltpu.VMEM)] * 2,
        scratch_shapes=[pltpu.VMEM((KK, 768), BF16)] * 2 + [pltpu.VMEM((KK, 512), F32)],
        compiler_params=pltpu.CompilerParams(vmem_limit_bytes=40 << 20),
        name="solve",
    )(rest, inv_hi, inv_lo, low_hi, low_lo, local)


def per_device(factors, x_factor, zinv_factor, placement):
    rows_dev = factors.shape[1]
    prow, pcol = lax.axis_index("prow"), lax.axis_index("pcol")
    mine = lax.dynamic_slice_in_dim(placement, (prow * 16 + pcol) * rows_dev, rows_dev)
    lane = jnp.arange(128)[None, :]
    tags = jnp.where(lane == 0, (mine >> 6)[:, None], jnp.where(lane == 1, (mine & 63)[:, None], (lane == 2).astype(jnp.int32)))
    flat = jnp.concatenate([factors.transpose(1, 0, 2).reshape(rows_dev, -1), tags.astype(BF16)], axis=1)
    order = placement.reshape(8, 16, rows_dev).transpose(1, 0, 2).reshape(16, 8 * rows_dev)
    rows, cols = route(flat, mine[None, :], order)
    mats = jnp.concatenate([x_factor, zinv_factor], axis=1)
    local, front, tiles = pair_blocks(rows, cols, mats)
    rest, inv_hi, inv_lo, low_hi, low_lo = factor(tiles.reshape(128, NB, 128), front, local[:128])
    return solve(rest, inv_hi, inv_lo, low_hi, low_lo, local)


def solution(mesh):
    in_specs = (P(None, ("prow", "pcol"), None), P(), P(), P())
    out_specs = (P("prow", "pcol"), P("prow", "pcol"))
    return jax.shard_map(per_device, mesh=mesh, in_specs=in_specs, out_specs=out_specs, check_vma=False)
```

```python
import functools
import jax
import jax.numpy as jnp
from jax import lax
from jax.experimental import pallas as pl
from jax.experimental.pallas import tpu as pltpu
from jax.sharding import PartitionSpec as P

RANK = 4
NB = 64
KK = 1024
F32, BF16 = jnp.float32, jnp.bfloat16
SIGNS = (1.0, 1.0, -1.0, -1.0)
MESH = pl.DeviceIdType.MESH
TN = (((1,), (1,)), ((), ()))
NN = (((1,), (0,)), ((), ()))
TT = (((0,), (0,)), ((), ()))


def split(v):
    hi = v.astype(BF16)
    return hi, (v - hi.astype(F32)).astype(BF16)


def spread(v):
    return jnp.broadcast_to(v, (8, 128))


def invert_block(block_ref, inv_ref):
    lane = lax.broadcasted_iota(jnp.int32, (8, 128), 1)
    sub = lax.broadcasted_iota(jnp.int32, (8, 128), 0)
    rows = [block_ref[8 * i:8 * i + 8, :] for i in range(16)]
    aug = [(lane == sub + 8 * i).astype(F32) for i in range(16)]
    for j in range(16):
        mine, extra = rows[j], aug[j]
        cols = [spread(mine[:, 8 * j + q:8 * j + q + 1]) for q in range(8)]
        a = [[None] * 8 for _ in range(8)]
        for q in range(8):
            for s in range(q, 8):
                a[s][q] = spread(cols[q][s:s + 1, :])
        r = [spread(mine[t:t + 1, :]) for t in range(8)] if j < 15 else None
        e = [spread(extra[t:t + 1, :]) for t in range(8)]
        rinv = [None] * 8
        low = [[None] * 8 for _ in range(8)]
        for t in range(8):
            rinv[t] = 1.0 / a[t][t]
            for s in range(t + 1, 8):
                low[s][t] = a[s][t] * rinv[t]
            for s in range(t + 1, 8):
                for k in range(t + 1, s + 1):
                    a[s][k] = a[s][k] - low[s][t] * a[k][t]
            for s in range(t + 1, 8):
                if r is not None:
                    r[s] = r[s] - low[s][t] * r[t]
                e[s] = e[s] - low[s][t] * e[t]
        packed_d = a[0][0]
        packed_e = e[0]
        for t in range(1, 8):
            packed_d = jnp.where(sub == t, a[t][t], packed_d)
            packed_e = jnp.where(sub == t, e[t], packed_e)
        inv_ref[8 * j:8 * j + 8, :] = packed_e * lax.rsqrt(packed_d)
        if j == 15:
            break
        w = [r[t] * rinv[t] for t in range(8)]
        we = [e[t] * rinv[t] for t in range(8)]
        for s in range(7, 0, -1):
            for t in range(s):
                w[t] = w[t] - low[s][t] * w[s]
                we[t] = we[t] - low[s][t] * we[s]
        for i in range(j + 1, 16):
            c = [spread(rows[i][:, 8 * j + q:8 * j + q + 1]) for q in range(8)]
            acc = c[0] * w[0]
            acce = c[0] * we[0]
            for q in range(1, 8):
                acc = acc + c[q] * w[q]
                acce = acce + c[q] * we[q]
            rows[i] = rows[i] - acc
            aug[i] = aug[i] - acce


OFFS = 4


class Plane:
    def __init__(self, view, send, recv, arrived):
        self.prow, self.pcol = lax.axis_index("prow"), lax.axis_index("pcol")
        self.me = (self.pcol // 4, lax.rem(self.pcol, 4))
        self.sign = 1 - 2 * lax.rem(self.prow, 2)
        self.offs = (0, -self.sign, self.sign, 2)
        self.raw, self.send, self.recv, self.arrived = view, send, recv, arrived

    def view(self, colour, first, second):
        steps = (first, second) if colour == 0 else (second, first)
        at = [lax.rem(v + s + OFFS, 4) for v, s in zip(self.me, steps)]
        return self.raw(colour, at[0], at[1])

    def peer(self, colour, leg, step):
        dim = leg if colour == 0 else 1 - leg
        at = [lax.rem(v + step + OFFS, 4) if d == dim else v for d, v in enumerate(self.me)]
        return (self.prow, at[0] * 4 + at[1])

    def message(self, colour, leg, o, kind):
        n = colour * 15 + (kind if leg == 0 else 3 + o * 3 + kind)
        carried = -self.sign if kind == 2 else 0
        part = self.view(colour, carried, 0) if leg == 0 else self.view(colour, self.offs[o], carried)
        to = self.peer(colour, leg, -self.sign if kind == 1 else self.sign)
        return pltpu.make_async_remote_copy(part, part, self.send.at[n], self.recv.at[n], device_id=to, device_id_type=MESH)

    def landed(self, colour, leg, o, kind):
        n = colour * 15 + (kind if leg == 0 else 3 + o * 3 + kind)
        come = (-self.sign, self.sign, 2)[kind]
        part = self.view(colour, come, 0) if leg == 0 else self.view(colour, self.offs[o], come)
        pltpu.make_async_remote_copy(part, part, self.send.at[n], self.recv.at[n],
                                     device_id=self.peer(colour, leg, 1), device_id_type=MESH).wait_recv()
        if self.arrived is not None:
            self.arrived(colour, part, 1 + (kind if leg == 0 else 3 + o * 3 + kind))

    def both(self, colour, leg, o):
        self.message(colour, leg, o, 0).start()
        self.message(colour, leg, o, 1).start()

    def stages(self):
        def relay(c, leg, o):
            self.landed(c, leg, o, 0)
            self.message(c, leg, o, 2).start()

        def s0():
            for c in range(2):
                self.both(c, 0, 0)
            for c in range(2):
                self.both(c, 1, 0)

        def s1():
            for c in range(2):
                relay(c, 0, 0)
                self.both(c, 1, 1)

        def s2():
            for c in range(2):
                self.landed(c, 0, 0, 1)
                self.both(c, 1, 2)

        def s3():
            for c in range(2):
                relay(c, 1, 0)

        def s4():
            for c in range(2):
                self.landed(c, 0, 0, 2)
                self.both(c, 1, 3)

        def s5():
            for o in (1, 2):
                for c in range(2):
                    relay(c, 1, o)

        def s6():
            for c in range(2):
                relay(c, 1, 3)

        def s7():
            for o in range(4):
                for c in range(2):
                    self.landed(c, 1, o, 1)
            for o in range(4):
                for c in range(2):
                    self.landed(c, 1, o, 2)
        return [s0, s1, s2, s3, s4, s5, s6, s7]

    def drain(self):
        for c in range(2):
            for kind in range(3):
                self.message(c, 0, 0, kind).wait_send()
                for o in range(4):
                    self.message(c, 1, o, kind).wait_send()


class Column:
    def __init__(self, view, send, recv):
        self.prow, self.pcol = lax.axis_index("prow"), lax.axis_index("pcol")
        self.z, self.core = self.prow // 2, lax.rem(self.prow, 2)
        self.sign = 1 - 2 * self.core
        self.raw, self.send, self.recv = view, send, recv

    def message(self, kind):
        part = self.raw(lax.rem(self.z + (-self.sign if kind == 2 else 0) + OFFS, 4), self.core)
        to = lax.rem(self.z + (-self.sign if kind == 1 else self.sign) + OFFS, 4)
        return pltpu.make_async_remote_copy(part, part, self.send.at[kind], self.recv.at[kind],
                                            device_id=(to * 2 + self.core, self.pcol), device_id_type=MESH)

    def landed(self, kind):
        at = lax.rem(self.z + (-self.sign, self.sign, 2)[kind] + OFFS, 4)
        part = self.raw(at, self.core)
        pltpu.make_async_remote_copy(part, part, self.send.at[kind], self.recv.at[kind],
                                     device_id=(self.prow, self.pcol), device_id_type=MESH).wait_recv()
        return at

    def drain(self):
        for kind in range(3):
            self.message(kind).wait_send()


W = 2176


def before(n):
    return (lax.broadcasted_iota(jnp.int32, (n, n), 0) > lax.broadcasted_iota(jnp.int32, (n, n), 1)).astype(BF16)


def earlier(mask):
    n = mask.shape[0]
    wide = jnp.broadcast_to(mask.astype(F32), (n, 128)).astype(BF16)
    return jnp.dot(before(n), wide, preferred_element_type=F32)[:, 0:1].astype(jnp.int32)


def pick(index, valid, n):
    lane = lax.broadcasted_iota(jnp.int32, (index.shape[0], n), 1)
    hit = lane == index
    if valid is not None:
        hit = hit & valid
    return hit.astype(F32).astype(BF16)


def route_kernel(flat_ref, mine_ref, order_ref, rows_ref, cols_ref,
                 send_a, got_a, send_b, got_b, piece_ref, ss, rs, ps, pr, zs, zr, xs, xr):
    prow, pcol = lax.axis_index("prow"), lax.axis_index("pcol")
    twin = (lax.rem(pcol, 8), prow + 8 * (pcol // 8))
    at_home = prow == lax.rem(pcol, 8)
    barrier = pltpu.get_barrier_semaphore()
    for s in range(1, 16):
        pl.semaphore_signal(barrier, inc=1, device_id=(prow, lax.rem(pcol + s, 16)), device_id_type=MESH)
    for s in range(1, 8):
        pl.semaphore_signal(barrier, inc=1, device_id=(lax.rem(prow + s, 8), pcol), device_id_type=MESH)

    @pl.when(jnp.logical_not(at_home))
    def _():
        pl.semaphore_signal(barrier, inc=1, device_id=twin, device_id_type=MESH)

    group = (mine_ref[...] >> 6) & 7
    row = lax.broadcasted_iota(jnp.int32, (64, 32), 0)
    match = group == (row >> 3)
    ahead = (lax.broadcasted_iota(jnp.int32, (32, 32), 0) < lax.broadcasted_iota(jnp.int32, (32, 32), 1)).astype(BF16)
    rank = jnp.dot(match.astype(F32).astype(BF16), ahead, preferred_element_type=F32).astype(jnp.int32)
    sel = (match & (rank == (row & 7))).astype(F32).astype(BF16)
    send_a[...] = jnp.dot(sel, flat_ref[...], preferred_element_type=F32).reshape(8, 8, W).astype(BF16)
    got_a[prow] = send_a[prow]

    kind = (order_ref[...] >> 6) & 15
    prior = lax.broadcasted_iota(jnp.int32, kind.shape, 0) < pcol
    base = [jnp.sum((prior & (kind == prow + 8 * h)).astype(F32), keepdims=True).astype(jnp.int32) for h in range(2)]

    pl.semaphore_wait(barrier, jnp.where(at_home, 22, 23))

    def copy(src, dst, n, to):
        return pltpu.make_async_remote_copy(src, dst, ss.at[n], rs.at[n], device_id=to, device_id_type=MESH)

    def along_prow(s):
        return (lax.rem(prow + s, 8), pcol)

    def along_pcol(s):
        return (prow, lax.rem(pcol + s, 16))

    def slab(ref, i, n):
        return ref.at[pl.ds(pl.multiple_of(i * n, n), n)]

    def a_copy(s):
        return copy(send_a.at[lax.rem(prow + s, 8)], got_a.at[prow], s - 1, along_prow(s))

    def b_copy(s):
        return copy(send_b.at[lax.rem(pcol + s, 16)], got_b.at[pcol], 7 + s - 1, along_pcol(s))

    def twin_copy():
        return copy(piece_ref, cols_ref.at[twin[0]], 22, twin)

    def rows_view(colour, x, y):
        return rows_ref.at[x, y, :, pl.ds(1152 * colour, 1152 if colour == 0 else 1024)]

    def cols_view(z, core):
        return cols_ref.at[z * 2 + core]

    for s in range(1, 8):
        a_copy(s).start()
    for s in range(1, 8):
        spot = got_a.at[lax.rem(prow + 8 - s, 8)]
        copy(spot, spot, s - 1, along_prow(1)).wait_recv()

    got = got_a[...].astype(F32).reshape(64, W).astype(BF16)
    tags = got[:, 2048:].astype(F32)
    valid = tags[:, 2:3] > 0.5
    half = (tags[:, 0:1].astype(jnp.int32) >> 3) & 1
    slot = jnp.zeros((64, 1), jnp.int32)
    for h in range(2):
        li = earlier(valid & (half == h))
        slot = jnp.where(half == h, (8 * h + ((base[h] + li) & 7)) * 8 + (li >> 3), slot)
    send_b[...] = lax.dot_general(pick(slot, valid, 128), got, TT, preferred_element_type=F32).reshape(16, 8, W).astype(BF16)
    got_b[pcol] = send_b[pcol]
    for s in range(1, 16):
        b_copy(s).start()
    for s in range(1, 16):
        spot = got_b.at[lax.rem(pcol + 16 - s, 16)]
        copy(spot, spot, 7 + s - 1, along_prow(1)).wait_recv()

    got = got_b[...].astype(F32).reshape(128, W).astype(BF16)
    valid = got[:, 2048:].astype(F32)[:, 2:3] > 0.5
    piece = lax.dot_general(pick(earlier(valid), valid, 32), got, TT, preferred_element_type=F32).astype(BF16)
    piece_ref[...] = piece
    rows_ref[pcol // 4, lax.rem(pcol, 4)] = piece

    @pl.when(at_home)
    def _():
        cols_ref[prow] = piece

    @pl.when(jnp.logical_not(at_home))
    def _():
        twin_copy().start()
    plane = Plane(rows_view, ps, pr, None)
    column = Column(cols_view, zs, zr)
    core = lax.rem(prow, 2)
    other = prow + 1 - 2 * core

    def across(n, z, whose):
        part = cols_view(z, whose)
        return pltpu.make_async_remote_copy(part, part, xs.at[n], xr.at[n], device_id=(other, pcol), device_id_type=MESH)
    todo = plane.stages()
    todo[0]()
    todo[1]()

    @pl.when(jnp.logical_not(at_home))
    def _():
        copy(cols_ref.at[prow], cols_ref.at[prow], 22, twin).wait_recv()
    column.message(0).start()
    column.message(1).start()
    across(0, prow // 2, core).start()
    todo[2]()
    todo[3]()
    at = [prow // 2, column.landed(0)]
    column.message(2).start()
    across(1, at[1], core).start()
    todo[4]()
    at.append(column.landed(1))
    across(2, at[2], core).start()
    todo[5]()
    at.append(column.landed(2))
    across(3, at[3], core).start()
    todo[6]()
    todo[7]()
    sign = 1 - 2 * core
    for n, shift in enumerate((0, sign, -sign, 2)):
        across(n, lax.rem(prow // 2 + shift + OFFS, 4), 1 - core).wait_recv()
        across(n, at[n], core).wait_send()
    plane.drain()
    column.drain()
    for s in range(1, 8):
        a_copy(s).wait_send()
    for s in range(1, 16):
        b_copy(s).wait_send()

    @pl.when(jnp.logical_not(at_home))
    def _():
        twin_copy().wait_send()


def route(flat, mine, order):
    return pl.pallas_call(
        route_kernel,
        out_shape=(jax.ShapeDtypeStruct((4, 4, 32, W), BF16), jax.ShapeDtypeStruct((8, 32, W), BF16)),
        in_specs=[pl.BlockSpec(memory_space=pltpu.VMEM)] * 3,
        out_specs=[pl.BlockSpec(memory_space=pltpu.VMEM)] * 2,
        scratch_shapes=[
            pltpu.VMEM((8, 8, W), BF16),
            pltpu.VMEM((8, 8, W), BF16),
            pltpu.VMEM((16, 8, W), BF16),
            pltpu.VMEM((16, 8, W), BF16),
            pltpu.VMEM((32, W), BF16),
            pltpu.SemaphoreType.DMA((23,)),
            pltpu.SemaphoreType.DMA((23,)),
            pltpu.SemaphoreType.DMA((30,)),
            pltpu.SemaphoreType.DMA((30,)),
            pltpu.SemaphoreType.DMA((3,)),
            pltpu.SemaphoreType.DMA((3,)),
            pltpu.SemaphoreType.DMA((4,)),
            pltpu.SemaphoreType.DMA((4,)),
        ],
        compiler_params=pltpu.CompilerParams(collective_id=1, has_side_effects=True, vmem_limit_bytes=24 << 20),
        name="route",
    )(flat, mine, order)


def pair_kernel(rows_ref, cols_ref, mats_ref, local_ref, front_ref, out_ref, x_ref, z_ref, send, recv, zsend, zrecv, psend, precv):
    prow, pcol = lax.axis_index("prow"), lax.axis_index("pcol")
    z, core = prow // 2, lax.rem(prow, 2)
    other = (prow + 1 - 2 * core, pcol)

    def tile_view(at, whose):
        return out_ref.at[pcol // 4, lax.rem(pcol, 4), at, whose]

    def block_view(colour, x, y):
        return out_ref.at[x, y, :, core, pl.ds(32 * colour, 32)]

    def across(colour, part, n):
        return pltpu.make_async_remote_copy(part, part, psend.at[colour * 16 + n], precv.at[colour * 16 + n],
                                            device_id=other, device_id_type=MESH)
    plane = Plane(block_view, send, recv, lambda colour, part, n: across(colour, part, n).start())
    column = Column(tile_view, zsend, zrecv)
    barrier = pltpu.get_barrier_semaphore()
    for step in (1, -1):
        pl.semaphore_signal(barrier, inc=1, device_id=plane.peer(0, 0, step), device_id_type=MESH)
        pl.semaphore_signal(barrier, inc=1, device_id=plane.peer(0, 1, step), device_id_type=MESH)
        pl.semaphore_signal(barrier, inc=1, device_id=(lax.rem(z + step + OFFS, 4) * 2 + core, pcol), device_id_type=MESH)
    pl.semaphore_signal(barrier, inc=1, device_id=other, device_id_type=MESH)
    depth = mats_ref.shape[0]

    def load(src, first, count, shift, at):
        tags = src[:, 2048:].astype(F32).astype(jnp.int32)
        spot = (tags[:, 0:1] >> shift) * NB + tags[:, 1:2] - first
        rows = lax.dot_general(pick(spot, None, count), src[:, :2048], TT, preferred_element_type=F32).astype(BF16)
        for r in range(RANK):
            images = jnp.dot(rows[:, r * depth:(r + 1) * depth], mats_ref[...], preferred_element_type=F32).astype(BF16)
            x_ref[r, at:at + count, :] = images[:, :depth]
            z_ref[r, at:at + count, :] = images[:, depth:]

    def pair(base, m, other, n):
        acc = None
        for r in range(RANK):
            for q in range(RANK):
                inner_x = lax.dot_general(x_ref[r, base:base + m, :], x_ref[q, other:other + n, :], TN, preferred_element_type=F32)
                inner_z = lax.dot_general(z_ref[r, base:base + m, :], z_ref[q, other:other + n, :], TN, preferred_element_type=F32)
                term = inner_x * inner_z
                if acc is None:
                    acc = term
                elif SIGNS[r] * SIGNS[q] > 0:
                    acc = acc + term
                else:
                    acc = acc - term
        return acc

    def chunk(base):
        block = pair(base, 128, 512, 256)
        local_ref[base:base + 128, :] = block
        front_ref[:, base:base + 128] = block[:, :128].T[:NB, :]

    load(cols_ref, 0, 64, 4, 512)
    load(rows_ref, 0, 128, 3, 0)
    out_ref[pcol // 4, lax.rem(pcol, 4), z, core] = pair(512, 64, 0, 128)
    pl.semaphore_wait(barrier, 7)
    column.message(0).start()
    column.message(1).start()
    load(cols_ref, 64, 192, 4, 576)
    column.landed(0)
    column.message(2).start()
    column.landed(1)
    load(rows_ref, 128, 384, 3, 128)
    column.landed(2)
    todo = plane.stages()
    todo[0]()
    for colour in range(2):
        across(colour, plane.view(colour, 0, 0), 0).start()
    for n in range(4):
        chunk(128 * n)
        todo[1 + n]()
    for n in range(5, 8):
        todo[n]()
    plane.drain()
    column.drain()
    mirror = Plane(lambda colour, x, y: out_ref.at[x, y, :, 1 - core, pl.ds(32 * colour, 32)], send, recv, None)
    for colour in range(2):
        for n in range(16):
            leg, o, kind = (0, 0, n - 1) if n < 4 else (1, (n - 4) // 3, (n - 4) % 3)
            come = (-plane.sign, plane.sign, 2)[kind]
            first, second = (0, 0) if n == 0 else ((come, 0) if leg == 0 else (plane.offs[o], come))
            across(colour, plane.view(colour, first, second), n).wait_send()
            come = (plane.sign, -plane.sign, 2)[kind]
            hop = (0, plane.sign, -plane.sign, 2)[o]
            first, second = (0, 0) if n == 0 else ((come, 0) if leg == 0 else (hop, come))
            across(colour, mirror.view(colour, first, second), n).wait_recv()


def pair_blocks(rows, cols, mats):
    d = mats.shape[0]
    return pl.pallas_call(
        pair_kernel,
        out_shape=(
            jax.ShapeDtypeStruct((512, 256), F32),
            jax.ShapeDtypeStruct((NB, 512), F32),
            jax.ShapeDtypeStruct((4, 4, 4, 2, NB, 128), F32),
        ),
        in_specs=[pl.BlockSpec(memory_space=pltpu.VMEM)] * 3,
        out_specs=[pl.BlockSpec(memory_space=pltpu.VMEM)] * 3,
        scratch_shapes=[
            pltpu.VMEM((RANK, 768, d), BF16),
            pltpu.VMEM((RANK, 768, d), BF16),
            pltpu.SemaphoreType.DMA((30,)),
            pltpu.SemaphoreType.DMA((30,)),
            pltpu.SemaphoreType.DMA((3,)),
            pltpu.SemaphoreType.DMA((3,)),
            pltpu.SemaphoreType.DMA((32,)),
            pltpu.SemaphoreType.DMA((32,)),
        ],
        compiler_params=pltpu.CompilerParams(collective_id=2, has_side_effects=True, vmem_limit_bytes=40 << 20),
        name="pairs",
    )(rows, cols, mats)


def factor_kernel(tiles_ref, front_ref, top_ref, rest_ref, inv_hi_ref, inv_lo_ref, low_hi_ref, low_lo_ref,
                  a_ref, diag_ref, inv_ref, pcat_ref, qcat_ref, icat_ref, own_sem, send, recv):
    prow, pcol = lax.axis_index("prow"), lax.axis_index("pcol")
    barrier = pltpu.get_barrier_semaphore()
    for s in range(1, 16):
        pl.semaphore_signal(barrier, inc=1, device_id=(prow, lax.rem(pcol + s, 16)), device_id_type=MESH)
    for s in range(1, 8):
        pl.semaphore_signal(barrier, inc=1, device_id=(lax.rem(prow + s, 8), pcol), device_id_type=MESH)
    pl.semaphore_wait(barrier, 22)

    def front_place(c):
        return rest_ref.at[pl.ds(pl.multiple_of(c * NB, NB), NB), pl.ds(0, 512)]

    def top_place(p, h):
        return rest_ref.at[pl.ds(pl.multiple_of(h * 512 + p * NB, NB), NB), pl.ds(512, 256)]

    def front_copy(s):
        return pltpu.make_async_remote_copy(
            front_ref, front_place(pcol), send.at[s - 1], recv.at[s - 1],
            device_id=(prow, lax.rem(pcol + s, 16)), device_id_type=MESH)

    def top_copy(s, h):
        n = 15 + (s - 1) * 2 + h
        return pltpu.make_async_remote_copy(
            top_ref.at[pl.ds(h * NB, NB)], top_place(prow, h), send.at[n], recv.at[n],
            device_id=(lax.rem(prow + s, 8), pcol), device_id_type=MESH)
    own = [pltpu.make_async_copy(front_ref, front_place(pcol), own_sem.at[0])]
    for h in range(2):
        own.append(pltpu.make_async_copy(top_ref.at[pl.ds(h * NB, NB)], top_place(prow, h), own_sem.at[1 + h]))
    for c in own:
        c.start()
    for s in range(1, 16):
        front_copy(s).start()
    for s in range(1, 8):
        for h in range(2):
            top_copy(s, h).start()

    left = lax.broadcasted_iota(jnp.int32, (NB, 128), 1) < NB

    def fill(i, carry):
        at = pl.ds(pl.multiple_of(i * NB, NB), NB)
        for k in range(4):
            even, odd = tiles_ref[i * 8 + 2 * k], tiles_ref[i * 8 + 2 * k + 1]
            a_ref[at, 128 * k:128 * k + 128] = jnp.where(left, even, pltpu.roll(odd, NB, 1))
            a_ref[at, 512 + 128 * k:640 + 128 * k] = jnp.where(left, pltpu.roll(even, NB, 1), odd)
        return carry
    lax.fori_loop(0, 16, fill, 0)

    def step(j, carry):
        off = pl.multiple_of(j * 128, 128)
        diag_ref[...] = a_ref[pl.ds(off, 128), pl.ds(off, 128)]
        invert_block(diag_ref, inv_ref)
        hi, lo = split(inv_ref[...])
        inv_hi_ref[pl.ds(off, 128), :] = hi
        inv_lo_ref[pl.ds(off, 128), :] = lo
        icat_ref[:, 0:128] = hi
        icat_ref[:, 128:256] = hi
        icat_ref[:, 256:384] = lo
        first = (j + 1) // 2

        def panel(r, c):
            base = pl.multiple_of(r * 256, 256)
            hi, lo = split(a_ref[pl.ds(base, 256), pl.ds(off, 128)])
            v = lax.dot_general(jnp.concatenate([hi, lo, hi], axis=1), icat_ref[...], TN, preferred_element_type=F32)
            hi, lo = split(v)
            pcat_ref[pl.ds(base, 256), 0:128] = hi
            pcat_ref[pl.ds(base, 256), 128:256] = lo
            pcat_ref[pl.ds(base, 256), 256:384] = hi
            qcat_ref[pl.ds(base, 256), 0:128] = hi
            qcat_ref[pl.ds(base, 256), 128:256] = hi
            qcat_ref[pl.ds(base, 256), 256:384] = lo
            low_hi_ref[pl.ds(base, 256), pl.ds(off, 128)] = hi
            low_lo_ref[pl.ds(base, 256), pl.ds(off, 128)] = lo
            return c
        lax.fori_loop(first, KK // 256, panel, 0)

        def update(r, c):
            base = pl.multiple_of(r * 256, 256)

            def inner(k, c):
                cb = pl.multiple_of(k * 256, 256)
                a_ref[pl.ds(base, 256), pl.ds(cb, 256)] -= lax.dot_general(
                    pcat_ref[pl.ds(base, 256), :], qcat_ref[pl.ds(cb, 256), :], TN, preferred_element_type=F32)
                return c
            return lax.fori_loop(first, r + 1, inner, c)
        lax.fori_loop(first, KK // 256, update, 0)
        return carry
    lax.fori_loop(0, KK // 128, step, 0)
    for c in own:
        c.wait()
    for s in range(1, 16):
        front_copy(s).wait_send()
        place = front_place(lax.rem(pcol + 16 - s, 16))
        pltpu.make_async_remote_copy(place, place, send.at[s - 1], recv.at[s - 1],
                                     device_id=(prow, pcol), device_id_type=MESH).wait_recv()
    for s in range(1, 8):
        for h in range(2):
            n = 15 + (s - 1) * 2 + h
            top_copy(s, h).wait_send()
            place = top_place(lax.rem(prow + 8 - s, 8), h)
            pltpu.make_async_remote_copy(place, place, send.at[n], recv.at[n],
                                         device_id=(prow, pcol), device_id_type=MESH).wait_recv()


def factor(tiles, front, top):
    return pl.pallas_call(
        factor_kernel,
        out_shape=(
            jax.ShapeDtypeStruct((KK, 768), F32),
            jax.ShapeDtypeStruct((KK, 128), BF16),
            jax.ShapeDtypeStruct((KK, 128), BF16),
            jax.ShapeDtypeStruct((KK, KK), BF16),
            jax.ShapeDtypeStruct((KK, KK), BF16),
        ),
        in_specs=[pl.BlockSpec(memory_space=pltpu.VMEM)] * 3,
        out_specs=[pl.BlockSpec(memory_space=pltpu.VMEM)] * 5,
        scratch_shapes=[
            pltpu.VMEM((KK, KK), F32),
            pltpu.VMEM((128, 128), F32),
            pltpu.VMEM((128, 128), F32),
            pltpu.VMEM((KK, 384), BF16),
            pltpu.VMEM((KK, 384), BF16),
            pltpu.VMEM((128, 384), BF16),
            pltpu.SemaphoreType.DMA((3,)),
            pltpu.SemaphoreType.DMA((29,)),
            pltpu.SemaphoreType.DMA((29,)),
        ],
        compiler_params=pltpu.CompilerParams(collective_id=3, has_side_effects=True, vmem_limit_bytes=40 << 20),
        name="factor",
    )(tiles, front, top)


def solve_kernel(rest_ref, inv_hi_ref, inv_lo_ref, low_hi_ref, low_lo_ref, local_ref, trail_ref, panel_ref,
                 hi_ref, lo_ref, p_ref):
    for j in range(KK // 128):
        x = rest_ref[128 * j:128 * j + 128, :]
        if j:
            lh, ll = low_hi_ref[128 * j:128 * j + 128, :128 * j], low_lo_ref[128 * j:128 * j + 128, :128 * j]
            ph, pw = hi_ref[:128 * j, :], lo_ref[:128 * j, :]
            x = x - (lax.dot_general(lh, ph, NN, preferred_element_type=F32)
                     + lax.dot_general(lh, pw, NN, preferred_element_type=F32)
                     + lax.dot_general(ll, ph, NN, preferred_element_type=F32))
        xh, xl = split(x)
        ih, il = inv_hi_ref[128 * j:128 * j + 128, :], inv_lo_ref[128 * j:128 * j + 128, :]
        v = (lax.dot_general(ih, xh, NN, preferred_element_type=F32)
             + lax.dot_general(ih, xl, NN, preferred_element_type=F32)
             + lax.dot_general(il, xh, NN, preferred_element_type=F32))
        p_ref[128 * j:128 * j + 128, :] = v[:, :512]
        vh, vl = split(v)
        hi_ref[128 * j:128 * j + 128, :] = vh
        lo_ref[128 * j:128 * j + 128, :] = vl
    rh, rl = hi_ref[:, :512], lo_ref[:, :512]
    ch, cl = hi_ref[:, 512:], lo_ref[:, 512:]
    trail_ref[...] = local_ref[...] - (lax.dot_general(rh, ch, TT, preferred_element_type=F32)
                                       + lax.dot_general(rh, cl, TT, preferred_element_type=F32)
                                       + lax.dot_general(rl, ch, TT, preferred_element_type=F32))
    pcol = lax.axis_index("pcol")
    panel_ref[...] = p_ref[pl.ds(pl.multiple_of(pcol * NB, NB), NB), :].T


def solve(rest, inv_hi, inv_lo, low_hi, low_lo, local):
    return pl.pallas_call(
        solve_kernel,
        out_shape=(jax.ShapeDtypeStruct((512, 256), F32), jax.ShapeDtypeStruct((512, NB), F32)),
        in_specs=[pl.BlockSpec(memory_space=pltpu.VMEM)] * 6,
        out_specs=[pl.BlockSpec(memory_space=pltpu.VMEM)] * 2,
        scratch_shapes=[pltpu.VMEM((KK, 768), BF16)] * 2 + [pltpu.VMEM((KK, 512), F32)],
        compiler_params=pltpu.CompilerParams(vmem_limit_bytes=40 << 20),
        name="solve",
    )(rest, inv_hi, inv_lo, low_hi, low_lo, local)


def per_device(factors, x_factor, zinv_factor, placement):
    rows_dev = factors.shape[1]
    prow, pcol = lax.axis_index("prow"), lax.axis_index("pcol")
    mine = lax.dynamic_slice_in_dim(placement, (prow * 16 + pcol) * rows_dev, rows_dev)
    lane = jnp.arange(128)[None, :]
    tags = jnp.where(lane == 0, (mine >> 6)[:, None], jnp.where(lane == 1, (mine & 63)[:, None], (lane == 2).astype(jnp.int32)))
    flat = jnp.concatenate([factors.transpose(1, 0, 2).reshape(rows_dev, -1), tags.astype(BF16)], axis=1)
    order = placement.reshape(8, 16, rows_dev).transpose(1, 0, 2).reshape(16, 8 * rows_dev)
    rows, cols = route(flat, mine[None, :], order)
    mats = jnp.concatenate([x_factor, zinv_factor], axis=1)
    local, front, tiles = pair_blocks(rows.reshape(512, W), cols.reshape(256, W), mats)
    rest, inv_hi, inv_lo, low_hi, low_lo = factor(tiles.reshape(128, NB, 128), front, local[:128])
    return solve(rest, inv_hi, inv_lo, low_hi, low_lo, local)


def solution(mesh):
    in_specs = (P(None, ("prow", "pcol"), None), P(), P(), P())
    out_specs = (P("prow", "pcol"), P("prow", "pcol"))
    return jax.shard_map(per_device, mesh=mesh, in_specs=in_specs, out_specs=out_specs, check_vma=False)
```

```python
import functools
import jax
import jax.numpy as jnp
from jax import lax
from jax.experimental import pallas as pl
from jax.experimental.pallas import tpu as pltpu
from jax.sharding import PartitionSpec as P

RANK = 4
NB = 64
KK = 1024
F32, BF16 = jnp.float32, jnp.bfloat16
SIGNS = (1.0, 1.0, -1.0, -1.0)
MESH = pl.DeviceIdType.MESH
TN = (((1,), (1,)), ((), ()))
NN = (((1,), (0,)), ((), ()))
TT = (((0,), (0,)), ((), ()))


def split(v):
    hi = v.astype(BF16)
    return hi, (v - hi.astype(F32)).astype(BF16)


def spread(v):
    return jnp.broadcast_to(v, (8, 128))


def invert_block(block_ref, inv_ref, tmp_ref):
    lane = lax.broadcasted_iota(jnp.int32, (8, 128), 1)
    sub = lax.broadcasted_iota(jnp.int32, (8, 128), 0)
    rows = [block_ref[8 * i:8 * i + 8, :] for i in range(16)]
    for j in range(16):
        here = (lane >= 8 * j) & (lane < 8 * j + 8)
        mine = rows[j]
        spot = 72 * (j % 2)
        for q in range(8):
            tmp_ref[spot + 8 * q:spot + 8 * q + 8, :] = spread(mine[:, 8 * j + q:8 * j + q + 1])
        tmp_ref[spot + 64:spot + 72, :] = jnp.where(here, (lane == sub + 8 * j).astype(F32), mine)
        a = [[None] * 8 for _ in range(8)]
        for q in range(8):
            for s in range(q, 8):
                a[s][q] = tmp_ref[pl.ds(spot + 8 * q + s, 8, stride=0), :]
        r = [tmp_ref[pl.ds(spot + 64 + t, 8, stride=0), :] for t in range(8)]
        pivots, low = [], []
        for t in range(0, 8, 2):
            u = t + 1
            det = a[t][t] * a[u][u] - a[u][t] * a[u][t]
            inv_det = 1.0 / det
            p00, p01, p11 = a[u][u] * inv_det, -a[u][t] * inv_det, a[t][t] * inv_det
            pivots.append((p00, p01, p11, a[t][t], a[u][t], det))
            m = [[None] * 2 for _ in range(8)]
            for s in range(t + 2, 8):
                m[s][0] = a[s][t] * p00 + a[s][u] * p01
                m[s][1] = a[s][t] * p01 + a[s][u] * p11
            for s in range(t + 2, 8):
                for k in range(t + 2, s + 1):
                    a[s][k] = a[s][k] - (m[s][0] * a[k][t] + m[s][1] * a[k][u])
                r[s] = r[s] - (m[s][0] * r[t] + m[s][1] * r[u])
            low.append(m)
        packed, packed_d = r[0], pivots[0][3]
        for t in range(1, 8):
            p00, p01, p11, a00, a10, det = pivots[t // 2]
            row = a00 * r[t] - a10 * r[t - 1] if t % 2 else r[t]
            packed = jnp.where(sub == t, row, packed)
            packed_d = jnp.where(sub == t, a00 * det if t % 2 else a00, packed_d)
        inv_ref[8 * j:8 * j + 8, :] = jnp.where(lane < 8 * j + 8, packed * lax.rsqrt(packed_d), 0.0)
        if j == 15:
            break
        w = [None] * 8
        for t in (6, 4, 2, 0):
            p00, p01, p11 = pivots[t // 2][:3]
            w[t] = r[t] * p00 + r[t + 1] * p01
            w[t + 1] = r[t] * p01 + r[t + 1] * p11
            for s in range(t + 2, 8):
                w[t] = w[t] - low[t // 2][s][0] * w[s]
                w[t + 1] = w[t + 1] - low[t // 2][s][1] * w[s]
        for i in range(j + 1, 16):
            acc = jnp.where(here, 0.0, rows[i])
            for q in range(8):
                acc = acc - spread(rows[i][:, 8 * j + q:8 * j + q + 1]) * w[q]
            rows[i] = acc


OFFS = 4


class Plane:
    def __init__(self, view, send, recv, arrived):
        self.prow, self.pcol = lax.axis_index("prow"), lax.axis_index("pcol")
        self.me = (self.pcol // 4, lax.rem(self.pcol, 4))
        self.sign = 1 - 2 * lax.rem(self.prow, 2)
        self.offs = (0, -self.sign, self.sign, 2)
        self.raw, self.send, self.recv, self.arrived = view, send, recv, arrived

    def view(self, colour, first, second):
        steps = (first, second) if colour == 0 else (second, first)
        at = [lax.rem(v + s + OFFS, 4) for v, s in zip(self.me, steps)]
        return self.raw(colour, at[0], at[1])

    def peer(self, colour, leg, step):
        dim = leg if colour == 0 else 1 - leg
        at = [lax.rem(v + step + OFFS, 4) if d == dim else v for d, v in enumerate(self.me)]
        return (self.prow, at[0] * 4 + at[1])

    def message(self, colour, leg, o, kind):
        n = colour * 15 + (kind if leg == 0 else 3 + o * 3 + kind)
        carried = -self.sign if kind == 2 else 0
        part = self.view(colour, carried, 0) if leg == 0 else self.view(colour, self.offs[o], carried)
        to = self.peer(colour, leg, -self.sign if kind == 1 else self.sign)
        return pltpu.make_async_remote_copy(part, part, self.send.at[n], self.recv.at[n], device_id=to, device_id_type=MESH)

    def landed(self, colour, leg, o, kind):
        n = colour * 15 + (kind if leg == 0 else 3 + o * 3 + kind)
        come = (-self.sign, self.sign, 2)[kind]
        part = self.view(colour, come, 0) if leg == 0 else self.view(colour, self.offs[o], come)
        pltpu.make_async_remote_copy(part, part, self.send.at[n], self.recv.at[n],
                                     device_id=self.peer(colour, leg, 1), device_id_type=MESH).wait_recv()
        if self.arrived is not None:
            self.arrived(colour, part, 1 + (kind if leg == 0 else 3 + o * 3 + kind))

    def both(self, colour, leg, o):
        self.message(colour, leg, o, 0).start()
        self.message(colour, leg, o, 1).start()

    def stages(self):
        def relay(c, leg, o):
            self.landed(c, leg, o, 0)
            self.message(c, leg, o, 2).start()

        def s0():
            for c in range(2):
                self.both(c, 0, 0)
            for c in range(2):
                self.both(c, 1, 0)

        def s1():
            for c in range(2):
                relay(c, 0, 0)
                self.both(c, 1, 1)

        def s2():
            for c in range(2):
                self.landed(c, 0, 0, 1)
                self.both(c, 1, 2)

        def s3():
            for c in range(2):
                relay(c, 1, 0)

        def s4():
            for c in range(2):
                self.landed(c, 0, 0, 2)
                self.both(c, 1, 3)

        def s5():
            for o in (1, 2):
                for c in range(2):
                    relay(c, 1, o)

        def s6():
            for c in range(2):
                relay(c, 1, 3)

        def s7():
            for o in range(4):
                for c in range(2):
                    self.landed(c, 1, o, 1)
            for o in range(4):
                for c in range(2):
                    self.landed(c, 1, o, 2)
        return [s0, s1, s2, s3, s4, s5, s6, s7]

    def drain(self):
        for c in range(2):
            for kind in range(3):
                self.message(c, 0, 0, kind).wait_send()
                for o in range(4):
                    self.message(c, 1, o, kind).wait_send()


class Column:
    def __init__(self, view, send, recv):
        self.prow, self.pcol = lax.axis_index("prow"), lax.axis_index("pcol")
        self.z, self.core = self.prow // 2, lax.rem(self.prow, 2)
        self.sign = 1 - 2 * self.core
        self.raw, self.send, self.recv = view, send, recv

    def message(self, kind):
        part = self.raw(lax.rem(self.z + (-self.sign if kind == 2 else 0) + OFFS, 4), self.core)
        to = lax.rem(self.z + (-self.sign if kind == 1 else self.sign) + OFFS, 4)
        return pltpu.make_async_remote_copy(part, part, self.send.at[kind], self.recv.at[kind],
                                            device_id=(to * 2 + self.core, self.pcol), device_id_type=MESH)

    def landed(self, kind):
        at = lax.rem(self.z + (-self.sign, self.sign, 2)[kind] + OFFS, 4)
        part = self.raw(at, self.core)
        pltpu.make_async_remote_copy(part, part, self.send.at[kind], self.recv.at[kind],
                                     device_id=(self.prow, self.pcol), device_id_type=MESH).wait_recv()
        return at

    def drain(self):
        for kind in range(3):
            self.message(kind).wait_send()


W = 2176


def before(n):
    return (lax.broadcasted_iota(jnp.int32, (n, n), 0) > lax.broadcasted_iota(jnp.int32, (n, n), 1)).astype(BF16)


def earlier(mask):
    n = mask.shape[0]
    wide = jnp.broadcast_to(mask.astype(F32), (n, 128)).astype(BF16)
    return jnp.dot(before(n), wide, preferred_element_type=F32)[:, 0:1].astype(jnp.int32)


def pick(index, valid, n):
    lane = lax.broadcasted_iota(jnp.int32, (index.shape[0], n), 1)
    hit = lane == index
    if valid is not None:
        hit = hit & valid
    return hit.astype(F32).astype(BF16)


def route_kernel(flat_ref, mine_ref, order_ref, rows_ref, cols_ref,
                 send_a, got_a, send_b, got_b, piece_ref, ss, rs, ps, pr, zs, zr, xs, xr):
    prow, pcol = lax.axis_index("prow"), lax.axis_index("pcol")
    twin = (lax.rem(pcol, 8), prow + 8 * (pcol // 8))
    at_home = prow == lax.rem(pcol, 8)
    barrier = pltpu.get_barrier_semaphore()
    for s in range(1, 16):
        pl.semaphore_signal(barrier, inc=1, device_id=(prow, lax.rem(pcol + s, 16)), device_id_type=MESH)
    for s in range(1, 8):
        pl.semaphore_signal(barrier, inc=1, device_id=(lax.rem(prow + s, 8), pcol), device_id_type=MESH)

    @pl.when(jnp.logical_not(at_home))
    def _():
        pl.semaphore_signal(barrier, inc=1, device_id=twin, device_id_type=MESH)

    group = (mine_ref[...] >> 6) & 7
    row = lax.broadcasted_iota(jnp.int32, (64, 32), 0)
    match = group == (row >> 3)
    ahead = (lax.broadcasted_iota(jnp.int32, (32, 32), 0) < lax.broadcasted_iota(jnp.int32, (32, 32), 1)).astype(BF16)
    rank = jnp.dot(match.astype(F32).astype(BF16), ahead, preferred_element_type=F32).astype(jnp.int32)
    sel = (match & (rank == (row & 7))).astype(F32).astype(BF16)
    send_a[...] = jnp.dot(sel, flat_ref[...], preferred_element_type=F32).reshape(8, 8, W).astype(BF16)
    got_a[prow] = send_a[prow]

    kind = (order_ref[...] >> 6) & 15
    prior = lax.broadcasted_iota(jnp.int32, kind.shape, 0) < pcol
    base = [jnp.sum((prior & (kind == prow + 8 * h)).astype(F32), keepdims=True).astype(jnp.int32) for h in range(2)]

    pl.semaphore_wait(barrier, jnp.where(at_home, 22, 23))

    def copy(src, dst, n, to):
        return pltpu.make_async_remote_copy(src, dst, ss.at[n], rs.at[n], device_id=to, device_id_type=MESH)

    def along_prow(s):
        return (lax.rem(prow + s, 8), pcol)

    def along_pcol(s):
        return (prow, lax.rem(pcol + s, 16))

    def slab(ref, i, n):
        return ref.at[pl.ds(pl.multiple_of(i * n, n), n)]

    def a_copy(s):
        return copy(send_a.at[lax.rem(prow + s, 8)], got_a.at[prow], s - 1, along_prow(s))

    def b_copy(s):
        return copy(send_b.at[lax.rem(pcol + s, 16)], got_b.at[pcol], 7 + s - 1, along_pcol(s))

    def twin_copy():
        return copy(piece_ref, cols_ref.at[twin[0]], 22, twin)

    def rows_view(colour, x, y):
        return rows_ref.at[x, y, :, pl.ds(1152 * colour, 1152 if colour == 0 else 1024)]

    def cols_view(z, core):
        return cols_ref.at[z * 2 + core]

    for s in range(1, 8):
        a_copy(s).start()
    for s in range(1, 8):
        spot = got_a.at[lax.rem(prow + 8 - s, 8)]
        copy(spot, spot, s - 1, along_prow(1)).wait_recv()

    got = got_a[...].astype(F32).reshape(64, W).astype(BF16)
    tags = got[:, 2048:].astype(F32)
    valid = tags[:, 2:3] > 0.5
    half = (tags[:, 0:1].astype(jnp.int32) >> 3) & 1
    slot = jnp.zeros((64, 1), jnp.int32)
    for h in range(2):
        li = earlier(valid & (half == h))
        slot = jnp.where(half == h, (8 * h + ((base[h] + li) & 7)) * 8 + (li >> 3), slot)
    send_b[...] = lax.dot_general(pick(slot, valid, 128), got, TT, preferred_element_type=F32).reshape(16, 8, W).astype(BF16)
    got_b[pcol] = send_b[pcol]
    for s in range(1, 16):
        b_copy(s).start()
    for s in range(1, 16):
        spot = got_b.at[lax.rem(pcol + 16 - s, 16)]
        copy(spot, spot, 7 + s - 1, along_prow(1)).wait_recv()

    got = got_b[...].astype(F32).reshape(128, W).astype(BF16)
    valid = got[:, 2048:].astype(F32)[:, 2:3] > 0.5
    piece = lax.dot_general(pick(earlier(valid), valid, 32), got, TT, preferred_element_type=F32).astype(BF16)
    piece_ref[...] = piece
    rows_ref[pcol // 4, lax.rem(pcol, 4)] = piece

    @pl.when(at_home)
    def _():
        cols_ref[prow] = piece

    @pl.when(jnp.logical_not(at_home))
    def _():
        twin_copy().start()
    plane = Plane(rows_view, ps, pr, None)
    column = Column(cols_view, zs, zr)
    core = lax.rem(prow, 2)
    other = prow + 1 - 2 * core

    def across(n, z, whose):
        part = cols_view(z, whose)
        return pltpu.make_async_remote_copy(part, part, xs.at[n], xr.at[n], device_id=(other, pcol), device_id_type=MESH)
    todo = plane.stages()
    todo[0]()
    todo[1]()

    @pl.when(jnp.logical_not(at_home))
    def _():
        copy(cols_ref.at[prow], cols_ref.at[prow], 22, twin).wait_recv()
    column.message(0).start()
    column.message(1).start()
    across(0, prow // 2, core).start()
    todo[2]()
    todo[3]()
    at = [prow // 2, column.landed(0)]
    column.message(2).start()
    across(1, at[1], core).start()
    todo[4]()
    at.append(column.landed(1))
    across(2, at[2], core).start()
    todo[5]()
    at.append(column.landed(2))
    across(3, at[3], core).start()
    todo[6]()
    todo[7]()
    sign = 1 - 2 * core
    for n, shift in enumerate((0, sign, -sign, 2)):
        across(n, lax.rem(prow // 2 + shift + OFFS, 4), 1 - core).wait_recv()
        across(n, at[n], core).wait_send()
    plane.drain()
    column.drain()
    for s in range(1, 8):
        a_copy(s).wait_send()
    for s in range(1, 16):
        b_copy(s).wait_send()

    @pl.when(jnp.logical_not(at_home))
    def _():
        twin_copy().wait_send()


def route(flat, mine, order):
    return pl.pallas_call(
        route_kernel,
        out_shape=(jax.ShapeDtypeStruct((4, 4, 32, W), BF16), jax.ShapeDtypeStruct((8, 32, W), BF16)),
        in_specs=[pl.BlockSpec(memory_space=pltpu.VMEM)] * 3,
        out_specs=[pl.BlockSpec(memory_space=pltpu.VMEM)] * 2,
        scratch_shapes=[
            pltpu.VMEM((8, 8, W), BF16),
            pltpu.VMEM((8, 8, W), BF16),
            pltpu.VMEM((16, 8, W), BF16),
            pltpu.VMEM((16, 8, W), BF16),
            pltpu.VMEM((32, W), BF16),
            pltpu.SemaphoreType.DMA((23,)),
            pltpu.SemaphoreType.DMA((23,)),
            pltpu.SemaphoreType.DMA((30,)),
            pltpu.SemaphoreType.DMA((30,)),
            pltpu.SemaphoreType.DMA((3,)),
            pltpu.SemaphoreType.DMA((3,)),
            pltpu.SemaphoreType.DMA((4,)),
            pltpu.SemaphoreType.DMA((4,)),
        ],
        compiler_params=pltpu.CompilerParams(collective_id=1, has_side_effects=True, vmem_limit_bytes=24 << 20),
        name="route",
    )(flat, mine, order)


def pair_kernel(rows_ref, cols_ref, mats_ref, local_ref, front_ref, out_ref, x_ref, z_ref, send, recv, zsend, zrecv, psend, precv):
    prow, pcol = lax.axis_index("prow"), lax.axis_index("pcol")
    z, core = prow // 2, lax.rem(prow, 2)
    other = (prow + 1 - 2 * core, pcol)

    def tile_view(at, whose):
        return out_ref.at[pcol // 4, lax.rem(pcol, 4), at, whose]

    def block_view(colour, x, y):
        return out_ref.at[x, y, :, core, pl.ds(32 * colour, 32)]

    def across(colour, part, n):
        return pltpu.make_async_remote_copy(part, part, psend.at[colour * 16 + n], precv.at[colour * 16 + n],
                                            device_id=other, device_id_type=MESH)
    plane = Plane(block_view, send, recv, lambda colour, part, n: across(colour, part, n).start())
    column = Column(tile_view, zsend, zrecv)
    barrier = pltpu.get_barrier_semaphore()
    for step in (1, -1):
        pl.semaphore_signal(barrier, inc=1, device_id=plane.peer(0, 0, step), device_id_type=MESH)
        pl.semaphore_signal(barrier, inc=1, device_id=plane.peer(0, 1, step), device_id_type=MESH)
        pl.semaphore_signal(barrier, inc=1, device_id=(lax.rem(z + step + OFFS, 4) * 2 + core, pcol), device_id_type=MESH)
    pl.semaphore_signal(barrier, inc=1, device_id=other, device_id_type=MESH)
    depth = mats_ref.shape[0]

    def load(src, first, count, shift, at):
        tags = src[:, 2048:].astype(F32).astype(jnp.int32)
        spot = (tags[:, 0:1] >> shift) * NB + tags[:, 1:2] - first
        rows = lax.dot_general(pick(spot, None, count), src[:, :2048], TT, preferred_element_type=F32).astype(BF16)
        for r in range(RANK):
            images = jnp.dot(rows[:, r * depth:(r + 1) * depth], mats_ref[...], preferred_element_type=F32).astype(BF16)
            x_ref[r, at:at + count, :] = images[:, :depth]
            z_ref[r, at:at + count, :] = images[:, depth:]

    def pair(base, m, other, n):
        acc = None
        for r in range(RANK):
            for q in range(RANK):
                inner_x = lax.dot_general(x_ref[r, base:base + m, :], x_ref[q, other:other + n, :], TN, preferred_element_type=F32)
                inner_z = lax.dot_general(z_ref[r, base:base + m, :], z_ref[q, other:other + n, :], TN, preferred_element_type=F32)
                term = inner_x * inner_z
                if acc is None:
                    acc = term
                elif SIGNS[r] * SIGNS[q] > 0:
                    acc = acc + term
                else:
                    acc = acc - term
        return acc

    def chunk(base):
        block = pair(base, 128, 512, 256)
        local_ref[base:base + 128, :] = block
        front_ref[:, base:base + 128] = block[:, :128].T[:NB, :]

    load(cols_ref, 0, 64, 4, 512)
    load(rows_ref, 0, 128, 3, 0)
    out_ref[pcol // 4, lax.rem(pcol, 4), z, core] = pair(512, 64, 0, 128)
    pl.semaphore_wait(barrier, 7)
    column.message(0).start()
    column.message(1).start()
    load(cols_ref, 64, 192, 4, 576)
    column.landed(0)
    column.message(2).start()
    column.landed(1)
    load(rows_ref, 128, 384, 3, 128)
    column.landed(2)
    todo = plane.stages()
    todo[0]()
    for colour in range(2):
        across(colour, plane.view(colour, 0, 0), 0).start()
    for n in range(4):
        chunk(128 * n)
        todo[1 + n]()
    for n in range(5, 8):
        todo[n]()
    plane.drain()
    column.drain()
    mirror = Plane(lambda colour, x, y: out_ref.at[x, y, :, 1 - core, pl.ds(32 * colour, 32)], send, recv, None)
    for colour in range(2):
        for n in range(16):
            leg, o, kind = (0, 0, n - 1) if n < 4 else (1, (n - 4) // 3, (n - 4) % 3)
            come = (-plane.sign, plane.sign, 2)[kind]
            first, second = (0, 0) if n == 0 else ((come, 0) if leg == 0 else (plane.offs[o], come))
            across(colour, plane.view(colour, first, second), n).wait_send()
            come = (plane.sign, -plane.sign, 2)[kind]
            hop = (0, plane.sign, -plane.sign, 2)[o]
            first, second = (0, 0) if n == 0 else ((come, 0) if leg == 0 else (hop, come))
            across(colour, mirror.view(colour, first, second), n).wait_recv()


def pair_blocks(rows, cols, mats):
    d = mats.shape[0]
    return pl.pallas_call(
        pair_kernel,
        out_shape=(
            jax.ShapeDtypeStruct((512, 256), F32),
            jax.ShapeDtypeStruct((NB, 512), F32),
            jax.ShapeDtypeStruct((4, 4, 4, 2, NB, 128), F32),
        ),
        in_specs=[pl.BlockSpec(memory_space=pltpu.VMEM)] * 3,
        out_specs=[pl.BlockSpec(memory_space=pltpu.VMEM)] * 3,
        scratch_shapes=[
            pltpu.VMEM((RANK, 768, d), BF16),
            pltpu.VMEM((RANK, 768, d), BF16),
            pltpu.SemaphoreType.DMA((30,)),
            pltpu.SemaphoreType.DMA((30,)),
            pltpu.SemaphoreType.DMA((3,)),
            pltpu.SemaphoreType.DMA((3,)),
            pltpu.SemaphoreType.DMA((32,)),
            pltpu.SemaphoreType.DMA((32,)),
        ],
        compiler_params=pltpu.CompilerParams(collective_id=2, has_side_effects=True, vmem_limit_bytes=40 << 20),
        name="pairs",
    )(rows, cols, mats)


def factor_kernel(tiles_ref, front_ref, top_ref, rest_ref, inv_hi_ref, inv_lo_ref, low_hi_ref, low_lo_ref,
                  a_ref, diag_ref, inv_ref, tmp_ref, pcat_ref, qcat_ref, icat_ref, own_sem, send, recv):
    prow, pcol = lax.axis_index("prow"), lax.axis_index("pcol")
    barrier = pltpu.get_barrier_semaphore()
    for s in range(1, 16):
        pl.semaphore_signal(barrier, inc=1, device_id=(prow, lax.rem(pcol + s, 16)), device_id_type=MESH)
    for s in range(1, 8):
        pl.semaphore_signal(barrier, inc=1, device_id=(lax.rem(prow + s, 8), pcol), device_id_type=MESH)
    pl.semaphore_wait(barrier, 22)

    def front_place(c):
        return rest_ref.at[pl.ds(pl.multiple_of(c * NB, NB), NB), pl.ds(0, 512)]

    def top_place(p, h):
        return rest_ref.at[pl.ds(pl.multiple_of(h * 512 + p * NB, NB), NB), pl.ds(512, 256)]

    def front_copy(s):
        return pltpu.make_async_remote_copy(
            front_ref, front_place(pcol), send.at[s - 1], recv.at[s - 1],
            device_id=(prow, lax.rem(pcol + s, 16)), device_id_type=MESH)

    def top_copy(s, h):
        n = 15 + (s - 1) * 2 + h
        return pltpu.make_async_remote_copy(
            top_ref.at[pl.ds(h * NB, NB)], top_place(prow, h), send.at[n], recv.at[n],
            device_id=(lax.rem(prow + s, 8), pcol), device_id_type=MESH)
    own = [pltpu.make_async_copy(front_ref, front_place(pcol), own_sem.at[0])]
    for h in range(2):
        own.append(pltpu.make_async_copy(top_ref.at[pl.ds(h * NB, NB)], top_place(prow, h), own_sem.at[1 + h]))
    for c in own:
        c.start()
    for s in range(1, 16):
        front_copy(s).start()
    for s in range(1, 8):
        for h in range(2):
            top_copy(s, h).start()

    left = lax.broadcasted_iota(jnp.int32, (NB, 128), 1) < NB

    def fill(i, carry):
        at = pl.ds(pl.multiple_of(i * NB, NB), NB)
        for k in range(4):
            even, odd = tiles_ref[i * 8 + 2 * k], tiles_ref[i * 8 + 2 * k + 1]
            a_ref[at, 128 * k:128 * k + 128] = jnp.where(left, even, pltpu.roll(odd, NB, 1))
            a_ref[at, 512 + 128 * k:640 + 128 * k] = jnp.where(left, pltpu.roll(even, NB, 1), odd)
        return carry
    lax.fori_loop(0, 16, fill, 0)

    def step(j, carry):
        off = pl.multiple_of(j * 128, 128)
        diag_ref[...] = a_ref[pl.ds(off, 128), pl.ds(off, 128)]
        invert_block(diag_ref, inv_ref, tmp_ref)
        hi, lo = split(inv_ref[...])
        inv_hi_ref[pl.ds(off, 128), :] = hi
        inv_lo_ref[pl.ds(off, 128), :] = lo
        icat_ref[:, 0:128] = hi
        icat_ref[:, 128:256] = hi
        icat_ref[:, 256:384] = lo
        first = (j + 1) // 2

        def panel(r, c):
            base = pl.multiple_of(r * 256, 256)
            hi, lo = split(a_ref[pl.ds(base, 256), pl.ds(off, 128)])
            v = lax.dot_general(jnp.concatenate([hi, lo, hi], axis=1), icat_ref[...], TN, preferred_element_type=F32)
            hi, lo = split(v)
            pcat_ref[pl.ds(base, 256), 0:128] = hi
            pcat_ref[pl.ds(base, 256), 128:256] = lo
            pcat_ref[pl.ds(base, 256), 256:384] = hi
            qcat_ref[pl.ds(base, 256), 0:128] = hi
            qcat_ref[pl.ds(base, 256), 128:256] = hi
            qcat_ref[pl.ds(base, 256), 256:384] = lo
            low_hi_ref[pl.ds(base, 256), pl.ds(off, 128)] = hi
            low_lo_ref[pl.ds(base, 256), pl.ds(off, 128)] = lo
            return c
        lax.fori_loop(first, KK // 256, panel, 0)

        def update(r, c):
            base = pl.multiple_of(r * 256, 256)

            def inner(k, c):
                cb = pl.multiple_of(k * 256, 256)
                a_ref[pl.ds(base, 256), pl.ds(cb, 256)] -= lax.dot_general(
                    pcat_ref[pl.ds(base, 256), :], qcat_ref[pl.ds(cb, 256), :], TN, preferred_element_type=F32)
                return c
            return lax.fori_loop(first, r + 1, inner, c)
        lax.fori_loop(first, KK // 256, update, 0)
        return carry
    lax.fori_loop(0, KK // 128, step, 0)
    for c in own:
        c.wait()
    for s in range(1, 16):
        front_copy(s).wait_send()
        place = front_place(lax.rem(pcol + 16 - s, 16))
        pltpu.make_async_remote_copy(place, place, send.at[s - 1], recv.at[s - 1],
                                     device_id=(prow, pcol), device_id_type=MESH).wait_recv()
    for s in range(1, 8):
        for h in range(2):
            n = 15 + (s - 1) * 2 + h
            top_copy(s, h).wait_send()
            place = top_place(lax.rem(prow + 8 - s, 8), h)
            pltpu.make_async_remote_copy(place, place, send.at[n], recv.at[n],
                                         device_id=(prow, pcol), device_id_type=MESH).wait_recv()


def factor(tiles, front, top):
    return pl.pallas_call(
        factor_kernel,
        out_shape=(
            jax.ShapeDtypeStruct((KK, 768), F32),
            jax.ShapeDtypeStruct((KK, 128), BF16),
            jax.ShapeDtypeStruct((KK, 128), BF16),
            jax.ShapeDtypeStruct((KK, KK), BF16),
            jax.ShapeDtypeStruct((KK, KK), BF16),
        ),
        in_specs=[pl.BlockSpec(memory_space=pltpu.VMEM)] * 3,
        out_specs=[pl.BlockSpec(memory_space=pltpu.VMEM)] * 5,
        scratch_shapes=[
            pltpu.VMEM((KK, KK), F32),
            pltpu.VMEM((128, 128), F32),
            pltpu.VMEM((128, 128), F32),
            pltpu.VMEM((144, 128), F32),
            pltpu.VMEM((KK, 384), BF16),
            pltpu.VMEM((KK, 384), BF16),
            pltpu.VMEM((128, 384), BF16),
            pltpu.SemaphoreType.DMA((3,)),
            pltpu.SemaphoreType.DMA((29,)),
            pltpu.SemaphoreType.DMA((29,)),
        ],
        compiler_params=pltpu.CompilerParams(collective_id=3, has_side_effects=True, vmem_limit_bytes=40 << 20),
        name="factor",
    )(tiles, front, top)


def solve_kernel(rest_ref, inv_hi_ref, inv_lo_ref, low_hi_ref, low_lo_ref, local_ref, trail_ref, panel_ref,
                 hi_ref, lo_ref, p_ref):
    for j in range(KK // 128):
        x = rest_ref[128 * j:128 * j + 128, :]
        if j:
            lh, ll = low_hi_ref[128 * j:128 * j + 128, :128 * j], low_lo_ref[128 * j:128 * j + 128, :128 * j]
            ph, pw = hi_ref[:128 * j, :], lo_ref[:128 * j, :]
            x = x - (lax.dot_general(lh, ph, NN, preferred_element_type=F32)
                     + lax.dot_general(lh, pw, NN, preferred_element_type=F32)
                     + lax.dot_general(ll, ph, NN, preferred_element_type=F32))
        xh, xl = split(x)
        ih, il = inv_hi_ref[128 * j:128 * j + 128, :], inv_lo_ref[128 * j:128 * j + 128, :]
        v = (lax.dot_general(ih, xh, NN, preferred_element_type=F32)
             + lax.dot_general(ih, xl, NN, preferred_element_type=F32)
             + lax.dot_general(il, xh, NN, preferred_element_type=F32))
        p_ref[128 * j:128 * j + 128, :] = v[:, :512]
        vh, vl = split(v)
        hi_ref[128 * j:128 * j + 128, :] = vh
        lo_ref[128 * j:128 * j + 128, :] = vl
    rh, rl = hi_ref[:, :512], lo_ref[:, :512]
    ch, cl = hi_ref[:, 512:], lo_ref[:, 512:]
    trail_ref[...] = local_ref[...] - (lax.dot_general(rh, ch, TT, preferred_element_type=F32)
                                       + lax.dot_general(rh, cl, TT, preferred_element_type=F32)
                                       + lax.dot_general(rl, ch, TT, preferred_element_type=F32))
    pcol = lax.axis_index("pcol")
    panel_ref[...] = p_ref[pl.ds(pl.multiple_of(pcol * NB, NB), NB), :].T


def solve(rest, inv_hi, inv_lo, low_hi, low_lo, local):
    return pl.pallas_call(
        solve_kernel,
        out_shape=(jax.ShapeDtypeStruct((512, 256), F32), jax.ShapeDtypeStruct((512, NB), F32)),
        in_specs=[pl.BlockSpec(memory_space=pltpu.VMEM)] * 6,
        out_specs=[pl.BlockSpec(memory_space=pltpu.VMEM)] * 2,
        scratch_shapes=[pltpu.VMEM((KK, 768), BF16)] * 2 + [pltpu.VMEM((KK, 512), F32)],
        compiler_params=pltpu.CompilerParams(vmem_limit_bytes=40 << 20),
        name="solve",
    )(rest, inv_hi, inv_lo, low_hi, low_lo, local)


def per_device(factors, x_factor, zinv_factor, placement):
    rows_dev = factors.shape[1]
    prow, pcol = lax.axis_index("prow"), lax.axis_index("pcol")
    mine = lax.dynamic_slice_in_dim(placement, (prow * 16 + pcol) * rows_dev, rows_dev)
    lane = jnp.arange(128)[None, :]
    tags = jnp.where(lane == 0, (mine >> 6)[:, None], jnp.where(lane == 1, (mine & 63)[:, None], (lane == 2).astype(jnp.int32)))
    flat = jnp.concatenate([factors.transpose(1, 0, 2).reshape(rows_dev, -1), tags.astype(BF16)], axis=1)
    order = placement.reshape(8, 16, rows_dev).transpose(1, 0, 2).reshape(16, 8 * rows_dev)
    rows, cols = route(flat, mine[None, :], order)
    mats = jnp.concatenate([x_factor, zinv_factor], axis=1)
    local, front, tiles = pair_blocks(rows.reshape(512, W), cols.reshape(256, W), mats)
    rest, inv_hi, inv_lo, low_hi, low_lo = factor(tiles.reshape(128, NB, 128), front, local[:128])
    return solve(rest, inv_hi, inv_lo, low_hi, low_lo, local)


def solution(mesh):
    in_specs = (P(None, ("prow", "pcol"), None), P(), P(), P())
    out_specs = (P("prow", "pcol"), P("prow", "pcol"))
    return jax.shard_map(per_device, mesh=mesh, in_specs=in_specs, out_specs=out_specs, check_vma=False)
```

```python
import functools
import jax
import jax.numpy as jnp
from jax import lax
from jax.experimental import pallas as pl
from jax.experimental.pallas import tpu as pltpu
from jax.sharding import PartitionSpec as P

RANK = 4
NB = 64
KK = 1024
F32, BF16 = jnp.float32, jnp.bfloat16
SIGNS = (1.0, 1.0, -1.0, -1.0)
MESH = pl.DeviceIdType.MESH
TN = (((1,), (1,)), ((), ()))
NN = (((1,), (0,)), ((), ()))
TT = (((0,), (0,)), ((), ()))


def split(v):
    hi = v.astype(BF16)
    return hi, (v - hi.astype(F32)).astype(BF16)


def spread(v):
    return jnp.broadcast_to(v, (8, 128))


def invert_block(block_ref, inv_ref, tmp_ref):
    lane = lax.broadcasted_iota(jnp.int32, (8, 128), 1)
    sub = lax.broadcasted_iota(jnp.int32, (8, 128), 0)
    rows = [block_ref[8 * i:8 * i + 8, :] for i in range(16)]
    for j in range(16):
        here = (lane >= 8 * j) & (lane < 8 * j + 8)
        mine = rows[j]
        spot = 72 * (j % 2)
        for q in range(8):
            tmp_ref[spot + 8 * q:spot + 8 * q + 8, :] = spread(mine[:, 8 * j + q:8 * j + q + 1])
        tmp_ref[spot + 64:spot + 72, :] = jnp.where(here, (lane == sub + 8 * j).astype(F32), mine)
        a = [[None] * 8 for _ in range(8)]
        for q in range(8):
            for s in range(q, 8):
                a[s][q] = tmp_ref[pl.ds(spot + 8 * q + s, 8, stride=0), :]
        r = [tmp_ref[pl.ds(spot + 64 + t, 8, stride=0), :] for t in range(8)]
        pivots, low = [], []
        for t in range(0, 8, 2):
            u = t + 1
            det = a[t][t] * a[u][u] - a[u][t] * a[u][t]
            inv_det = 1.0 / det
            p00, p01, p11 = a[u][u] * inv_det, -a[u][t] * inv_det, a[t][t] * inv_det
            pivots.append((p00, p01, p11, a[t][t], a[u][t], det))
            m = [[None] * 2 for _ in range(8)]
            for s in range(t + 2, 8):
                m[s][0] = a[s][t] * p00 + a[s][u] * p01
                m[s][1] = a[s][t] * p01 + a[s][u] * p11
            for s in range(t + 2, 8):
                for k in range(t + 2, s + 1):
                    a[s][k] = a[s][k] - (m[s][0] * a[k][t] + m[s][1] * a[k][u])
                r[s] = r[s] - (m[s][0] * r[t] + m[s][1] * r[u])
            low.append(m)
        packed, packed_d = r[0], pivots[0][3]
        for t in range(1, 8):
            p00, p01, p11, a00, a10, det = pivots[t // 2]
            row = a00 * r[t] - a10 * r[t - 1] if t % 2 else r[t]
            packed = jnp.where(sub == t, row, packed)
            packed_d = jnp.where(sub == t, a00 * det if t % 2 else a00, packed_d)
        inv_ref[8 * j:8 * j + 8, :] = jnp.where(lane < 8 * j + 8, packed * lax.rsqrt(packed_d), 0.0)
        if j == 15:
            break
        w = [None] * 8
        for t in (6, 4, 2, 0):
            p00, p01, p11 = pivots[t // 2][:3]
            w[t] = r[t] * p00 + r[t + 1] * p01
            w[t + 1] = r[t] * p01 + r[t + 1] * p11
            for s in range(t + 2, 8):
                w[t] = w[t] - low[t // 2][s][0] * w[s]
                w[t + 1] = w[t + 1] - low[t // 2][s][1] * w[s]
        for i in range(j + 1, 16):
            acc = jnp.where(here, 0.0, rows[i])
            for q in range(8):
                acc = acc - spread(rows[i][:, 8 * j + q:8 * j + q + 1]) * w[q]
            rows[i] = acc


OFFS = 4


class Plane:
    def __init__(self, view, send, recv, arrived):
        self.prow, self.pcol = lax.axis_index("prow"), lax.axis_index("pcol")
        self.me = (self.pcol // 4, lax.rem(self.pcol, 4))
        self.sign = 1 - 2 * lax.rem(self.prow, 2)
        self.offs = (0, -self.sign, self.sign, 2)
        self.raw, self.send, self.recv, self.arrived = view, send, recv, arrived

    def view(self, colour, first, second):
        steps = (first, second) if colour == 0 else (second, first)
        at = [lax.rem(v + s + OFFS, 4) for v, s in zip(self.me, steps)]
        return self.raw(colour, at[0], at[1])

    def peer(self, colour, leg, step):
        dim = leg if colour == 0 else 1 - leg
        at = [lax.rem(v + step + OFFS, 4) if d == dim else v for d, v in enumerate(self.me)]
        return (self.prow, at[0] * 4 + at[1])

    def message(self, colour, leg, o, kind):
        n = colour * 15 + (kind if leg == 0 else 3 + o * 3 + kind)
        carried = -self.sign if kind == 2 else 0
        part = self.view(colour, carried, 0) if leg == 0 else self.view(colour, self.offs[o], carried)
        to = self.peer(colour, leg, -self.sign if kind == 1 else self.sign)
        return pltpu.make_async_remote_copy(part, part, self.send.at[n], self.recv.at[n], device_id=to, device_id_type=MESH)

    def landed(self, colour, leg, o, kind):
        n = colour * 15 + (kind if leg == 0 else 3 + o * 3 + kind)
        come = (-self.sign, self.sign, 2)[kind]
        part = self.view(colour, come, 0) if leg == 0 else self.view(colour, self.offs[o], come)
        pltpu.make_async_remote_copy(part, part, self.send.at[n], self.recv.at[n],
                                     device_id=self.peer(colour, leg, 1), device_id_type=MESH).wait_recv()
        if self.arrived is not None:
            self.arrived(colour, part, 1 + (kind if leg == 0 else 3 + o * 3 + kind))

    def both(self, colour, leg, o):
        self.message(colour, leg, o, 0).start()
        self.message(colour, leg, o, 1).start()

    def stages(self):
        def relay(c, leg, o):
            self.landed(c, leg, o, 0)
            self.message(c, leg, o, 2).start()

        def s0():
            for c in range(2):
                self.both(c, 0, 0)
            for c in range(2):
                self.both(c, 1, 0)

        def s1():
            for c in range(2):
                relay(c, 0, 0)
                self.both(c, 1, 1)

        def s2():
            for c in range(2):
                self.landed(c, 0, 0, 1)
                self.both(c, 1, 2)

        def s3():
            for c in range(2):
                relay(c, 1, 0)

        def s4():
            for c in range(2):
                self.landed(c, 0, 0, 2)
                self.both(c, 1, 3)

        def s5():
            for o in (1, 2):
                for c in range(2):
                    relay(c, 1, o)

        def s6():
            for c in range(2):
                relay(c, 1, 3)

        def s7():
            for o in range(4):
                for c in range(2):
                    self.landed(c, 1, o, 1)
            for o in range(4):
                for c in range(2):
                    self.landed(c, 1, o, 2)
        return [s0, s1, s2, s3, s4, s5, s6, s7]

    def drain(self):
        for c in range(2):
            for kind in range(3):
                self.message(c, 0, 0, kind).wait_send()
                for o in range(4):
                    self.message(c, 1, o, kind).wait_send()


class Column:
    def __init__(self, view, send, recv):
        self.prow, self.pcol = lax.axis_index("prow"), lax.axis_index("pcol")
        self.z, self.core = self.prow // 2, lax.rem(self.prow, 2)
        self.sign = 1 - 2 * self.core
        self.raw, self.send, self.recv = view, send, recv

    def message(self, kind):
        part = self.raw(lax.rem(self.z + (-self.sign if kind == 2 else 0) + OFFS, 4), self.core)
        to = lax.rem(self.z + (-self.sign if kind == 1 else self.sign) + OFFS, 4)
        return pltpu.make_async_remote_copy(part, part, self.send.at[kind], self.recv.at[kind],
                                            device_id=(to * 2 + self.core, self.pcol), device_id_type=MESH)

    def landed(self, kind):
        at = lax.rem(self.z + (-self.sign, self.sign, 2)[kind] + OFFS, 4)
        part = self.raw(at, self.core)
        pltpu.make_async_remote_copy(part, part, self.send.at[kind], self.recv.at[kind],
                                     device_id=(self.prow, self.pcol), device_id_type=MESH).wait_recv()
        return at

    def drain(self):
        for kind in range(3):
            self.message(kind).wait_send()


W = 2176


def before(n):
    return (lax.broadcasted_iota(jnp.int32, (n, n), 0) > lax.broadcasted_iota(jnp.int32, (n, n), 1)).astype(BF16)


def earlier(mask):
    n = mask.shape[0]
    wide = jnp.broadcast_to(mask.astype(F32), (n, 128)).astype(BF16)
    return jnp.dot(before(n), wide, preferred_element_type=F32)[:, 0:1].astype(jnp.int32)


def pick(index, valid, n):
    lane = lax.broadcasted_iota(jnp.int32, (index.shape[0], n), 1)
    hit = lane == index
    if valid is not None:
        hit = hit & valid
    return hit.astype(F32).astype(BF16)


def route_kernel(factors_ref, placed_ref, rows_ref, cols_ref,
                 send_a, got_a, send_b, got_b, piece_ref, ss, rs, ps, pr, zs, zr, xs, xr):
    prow, pcol = lax.axis_index("prow"), lax.axis_index("pcol")
    twin = (lax.rem(pcol, 8), prow + 8 * (pcol // 8))
    at_home = prow == lax.rem(pcol, 8)
    barrier = pltpu.get_barrier_semaphore()
    for s in range(1, 16):
        pl.semaphore_signal(barrier, inc=1, device_id=(prow, lax.rem(pcol + s, 16)), device_id_type=MESH)
    for s in range(1, 8):
        pl.semaphore_signal(barrier, inc=1, device_id=(lax.rem(prow + s, 8), pcol), device_id_type=MESH)

    @pl.when(jnp.logical_not(at_home))
    def _():
        pl.semaphore_signal(barrier, inc=1, device_id=twin, device_id_type=MESH)

    device = prow * 16 + pcol
    line = jnp.broadcast_to(placed_ref[pl.ds(device // 4, 1), :], (8, 128))
    mine = pltpu.roll(line, lax.rem(4 - lax.rem(device, 4), 4) * 32, 1)[0:1, :32]
    group = (mine >> 6) & 7
    row = lax.broadcasted_iota(jnp.int32, (64, 32), 0)
    match = group == (row >> 3)
    ahead = (lax.broadcasted_iota(jnp.int32, (32, 32), 0) < lax.broadcasted_iota(jnp.int32, (32, 32), 1)).astype(BF16)
    rank = jnp.dot(match.astype(F32).astype(BF16), ahead, preferred_element_type=F32).astype(jnp.int32)
    chosen = match & (rank == (row & 7))
    sel = chosen.astype(F32).astype(BF16)
    for r in range(RANK):
        send_a[:, :, 512 * r:512 * r + 512] = jnp.dot(sel, factors_ref[r], preferred_element_type=F32).reshape(8, 8, 512).astype(BF16)

    def total(v):
        return jnp.sum(jnp.where(chosen, v.astype(F32), 0.0), axis=1, keepdims=True)
    lane = lax.broadcasted_iota(jnp.int32, (64, 128), 1)
    tags = jnp.where(lane == 0, total(mine >> 6), jnp.where(lane == 1, total(mine & 63), jnp.where(lane == 2, total(mine * 0 + 1), 0.0)))
    send_a[:, :, 2048:] = tags.reshape(8, 8, 128).astype(BF16)
    got_a[prow] = send_a[prow]

    kind = (placed_ref[...] >> 6) & 15
    spot = lax.broadcasted_iota(jnp.int32, kind.shape, 0) * 4 + (lax.broadcasted_iota(jnp.int32, kind.shape, 1) >> 5)
    prior = (spot & 15) < pcol
    base = [jnp.sum((prior & (kind == prow + 8 * h)).astype(F32), keepdims=True).astype(jnp.int32) for h in range(2)]

    pl.semaphore_wait(barrier, jnp.where(at_home, 22, 23))

    def copy(src, dst, n, to):
        return pltpu.make_async_remote_copy(src, dst, ss.at[n], rs.at[n], device_id=to, device_id_type=MESH)

    def along_prow(s):
        return (lax.rem(prow + s, 8), pcol)

    def along_pcol(s):
        return (prow, lax.rem(pcol + s, 16))

    def slab(ref, i, n):
        return ref.at[pl.ds(pl.multiple_of(i * n, n), n)]

    def a_copy(s):
        return copy(send_a.at[lax.rem(prow + s, 8)], got_a.at[prow], s - 1, along_prow(s))

    def b_copy(s):
        return copy(send_b.at[lax.rem(pcol + s, 16)], got_b.at[pcol], 7 + s - 1, along_pcol(s))

    def twin_copy():
        return copy(piece_ref, cols_ref.at[twin[0]], 22, twin)

    def rows_view(colour, x, y):
        return rows_ref.at[x, y, :, pl.ds(1152 * colour, 1152 if colour == 0 else 1024)]

    def cols_view(z, core):
        return cols_ref.at[z * 2 + core]

    for s in range(1, 8):
        a_copy(s).start()
    for s in range(1, 8):
        spot = got_a.at[lax.rem(prow + 8 - s, 8)]
        copy(spot, spot, s - 1, along_prow(1)).wait_recv()

    got = got_a[...].astype(F32).reshape(64, W).astype(BF16)
    tags = got[:, 2048:].astype(F32)
    valid = tags[:, 2:3] > 0.5
    half = (tags[:, 0:1].astype(jnp.int32) >> 3) & 1
    slot = jnp.zeros((64, 1), jnp.int32)
    for h in range(2):
        li = earlier(valid & (half == h))
        slot = jnp.where(half == h, (8 * h + ((base[h] + li) & 7)) * 8 + (li >> 3), slot)
    send_b[...] = lax.dot_general(pick(slot, valid, 128), got, TT, preferred_element_type=F32).reshape(16, 8, W).astype(BF16)
    got_b[pcol] = send_b[pcol]
    for s in range(1, 16):
        b_copy(s).start()
    for s in range(1, 16):
        spot = got_b.at[lax.rem(pcol + 16 - s, 16)]
        copy(spot, spot, 7 + s - 1, along_prow(1)).wait_recv()

    got = got_b[...].astype(F32).reshape(128, W).astype(BF16)
    valid = got[:, 2048:].astype(F32)[:, 2:3] > 0.5
    piece = lax.dot_general(pick(earlier(valid), valid, 32), got, TT, preferred_element_type=F32).astype(BF16)
    piece_ref[...] = piece
    rows_ref[pcol // 4, lax.rem(pcol, 4)] = piece

    @pl.when(at_home)
    def _():
        cols_ref[prow] = piece

    @pl.when(jnp.logical_not(at_home))
    def _():
        twin_copy().start()
    plane = Plane(rows_view, ps, pr, None)
    column = Column(cols_view, zs, zr)
    core = lax.rem(prow, 2)
    other = prow + 1 - 2 * core

    def across(n, z, whose):
        part = cols_view(z, whose)
        return pltpu.make_async_remote_copy(part, part, xs.at[n], xr.at[n], device_id=(other, pcol), device_id_type=MESH)
    todo = plane.stages()
    todo[0]()
    todo[1]()

    @pl.when(jnp.logical_not(at_home))
    def _():
        copy(cols_ref.at[prow], cols_ref.at[prow], 22, twin).wait_recv()
    column.message(0).start()
    column.message(1).start()
    across(0, prow // 2, core).start()
    todo[2]()
    todo[3]()
    at = [prow // 2, column.landed(0)]
    column.message(2).start()
    across(1, at[1], core).start()
    todo[4]()
    at.append(column.landed(1))
    across(2, at[2], core).start()
    todo[5]()
    at.append(column.landed(2))
    across(3, at[3], core).start()
    todo[6]()
    todo[7]()
    sign = 1 - 2 * core
    for n, shift in enumerate((0, sign, -sign, 2)):
        across(n, lax.rem(prow // 2 + shift + OFFS, 4), 1 - core).wait_recv()
        across(n, at[n], core).wait_send()
    plane.drain()
    column.drain()
    for s in range(1, 8):
        a_copy(s).wait_send()
    for s in range(1, 16):
        b_copy(s).wait_send()

    @pl.when(jnp.logical_not(at_home))
    def _():
        twin_copy().wait_send()


def route(factors, placed):
    return pl.pallas_call(
        route_kernel,
        out_shape=(jax.ShapeDtypeStruct((4, 4, 32, W), BF16), jax.ShapeDtypeStruct((8, 32, W), BF16)),
        in_specs=[pl.BlockSpec(memory_space=pltpu.VMEM)] * 2,
        out_specs=[pl.BlockSpec(memory_space=pltpu.VMEM)] * 2,
        scratch_shapes=[
            pltpu.VMEM((8, 8, W), BF16),
            pltpu.VMEM((8, 8, W), BF16),
            pltpu.VMEM((16, 8, W), BF16),
            pltpu.VMEM((16, 8, W), BF16),
            pltpu.VMEM((32, W), BF16),
            pltpu.SemaphoreType.DMA((23,)),
            pltpu.SemaphoreType.DMA((23,)),
            pltpu.SemaphoreType.DMA((30,)),
            pltpu.SemaphoreType.DMA((30,)),
            pltpu.SemaphoreType.DMA((3,)),
            pltpu.SemaphoreType.DMA((3,)),
            pltpu.SemaphoreType.DMA((4,)),
            pltpu.SemaphoreType.DMA((4,)),
        ],
        compiler_params=pltpu.CompilerParams(collective_id=1, has_side_effects=True, vmem_limit_bytes=24 << 20),
        name="route",
    )(factors, placed)


def pair_kernel(rows_ref, cols_ref, xf_ref, zf_ref, local_ref, front_ref, out_ref, x_ref, z_ref, send, recv, zsend, zrecv, psend, precv):
    prow, pcol = lax.axis_index("prow"), lax.axis_index("pcol")
    z, core = prow // 2, lax.rem(prow, 2)
    other = (prow + 1 - 2 * core, pcol)

    def tile_view(at, whose):
        return out_ref.at[pcol // 4, lax.rem(pcol, 4), at, whose]

    def block_view(colour, x, y):
        return out_ref.at[x, y, :, core, pl.ds(32 * colour, 32)]

    def across(colour, part, n):
        return pltpu.make_async_remote_copy(part, part, psend.at[colour * 16 + n], precv.at[colour * 16 + n],
                                            device_id=other, device_id_type=MESH)
    plane = Plane(block_view, send, recv, lambda colour, part, n: across(colour, part, n).start())
    column = Column(tile_view, zsend, zrecv)
    barrier = pltpu.get_barrier_semaphore()
    for step in (1, -1):
        pl.semaphore_signal(barrier, inc=1, device_id=plane.peer(0, 0, step), device_id_type=MESH)
        pl.semaphore_signal(barrier, inc=1, device_id=plane.peer(0, 1, step), device_id_type=MESH)
        pl.semaphore_signal(barrier, inc=1, device_id=(lax.rem(z + step + OFFS, 4) * 2 + core, pcol), device_id_type=MESH)
    pl.semaphore_signal(barrier, inc=1, device_id=other, device_id_type=MESH)
    depth = xf_ref.shape[0]

    def load(src, first, count, shift, at):
        tags = src[:, 2048:].astype(F32).astype(jnp.int32)
        spot = (tags[:, 0:1] >> shift) * NB + tags[:, 1:2] - first
        rows = lax.dot_general(pick(spot, None, count), src[:, :2048], TT, preferred_element_type=F32).astype(BF16)
        for r in range(RANK):
            mine = rows[:, r * depth:(r + 1) * depth]
            x_ref[r, at:at + count, :] = jnp.dot(mine, xf_ref[...], preferred_element_type=F32).astype(BF16)
            z_ref[r, at:at + count, :] = jnp.dot(mine, zf_ref[...], preferred_element_type=F32).astype(BF16)

    def pair(base, m, other, n):
        acc = None
        for r in range(RANK):
            for q in range(RANK):
                inner_x = lax.dot_general(x_ref[r, base:base + m, :], x_ref[q, other:other + n, :], TN, preferred_element_type=F32)
                inner_z = lax.dot_general(z_ref[r, base:base + m, :], z_ref[q, other:other + n, :], TN, preferred_element_type=F32)
                term = inner_x * inner_z
                if acc is None:
                    acc = term
                elif SIGNS[r] * SIGNS[q] > 0:
                    acc = acc + term
                else:
                    acc = acc - term
        return acc

    def chunk(base):
        block = pair(base, 128, 512, 256)
        local_ref[base:base + 128, :] = block
        front_ref[:, base:base + 128] = block[:, :128].T[:NB, :]

    load(cols_ref, 0, 64, 4, 512)
    load(rows_ref, 0, 128, 3, 0)
    out_ref[pcol // 4, lax.rem(pcol, 4), z, core] = pair(512, 64, 0, 128)
    pl.semaphore_wait(barrier, 7)
    column.message(0).start()
    column.message(1).start()
    load(cols_ref, 64, 192, 4, 576)
    column.landed(0)
    column.message(2).start()
    column.landed(1)
    load(rows_ref, 128, 384, 3, 128)
    column.landed(2)
    todo = plane.stages()
    todo[0]()
    for colour in range(2):
        across(colour, plane.view(colour, 0, 0), 0).start()
    for n in range(4):
        chunk(128 * n)
        todo[1 + n]()
    for n in range(5, 8):
        todo[n]()
    plane.drain()
    column.drain()
    mirror = Plane(lambda colour, x, y: out_ref.at[x, y, :, 1 - core, pl.ds(32 * colour, 32)], send, recv, None)
    for colour in range(2):
        for n in range(16):
            leg, o, kind = (0, 0, n - 1) if n < 4 else (1, (n - 4) // 3, (n - 4) % 3)
            come = (-plane.sign, plane.sign, 2)[kind]
            first, second = (0, 0) if n == 0 else ((come, 0) if leg == 0 else (plane.offs[o], come))
            across(colour, plane.view(colour, first, second), n).wait_send()
            come = (plane.sign, -plane.sign, 2)[kind]
            hop = (0, plane.sign, -plane.sign, 2)[o]
            first, second = (0, 0) if n == 0 else ((come, 0) if leg == 0 else (hop, come))
            across(colour, mirror.view(colour, first, second), n).wait_recv()


def pair_blocks(rows, cols, x_factor, z_factor):
    d = x_factor.shape[0]
    return pl.pallas_call(
        pair_kernel,
        out_shape=(
            jax.ShapeDtypeStruct((512, 256), F32),
            jax.ShapeDtypeStruct((NB, 512), F32),
            jax.ShapeDtypeStruct((4, 4, 4, 2, NB, 128), F32),
        ),
        in_specs=[pl.BlockSpec(memory_space=pltpu.VMEM)] * 4,
        out_specs=[pl.BlockSpec(memory_space=pltpu.VMEM)] * 3,
        scratch_shapes=[
            pltpu.VMEM((RANK, 768, d), BF16),
            pltpu.VMEM((RANK, 768, d), BF16),
            pltpu.SemaphoreType.DMA((30,)),
            pltpu.SemaphoreType.DMA((30,)),
            pltpu.SemaphoreType.DMA((3,)),
            pltpu.SemaphoreType.DMA((3,)),
            pltpu.SemaphoreType.DMA((32,)),
            pltpu.SemaphoreType.DMA((32,)),
        ],
        compiler_params=pltpu.CompilerParams(collective_id=2, has_side_effects=True, vmem_limit_bytes=40 << 20),
        name="pairs",
    )(rows, cols, x_factor, z_factor)


def factor_kernel(tiles_ref, front_ref, top_ref, rest_ref, inv_hi_ref, inv_lo_ref, low_hi_ref, low_lo_ref,
                  a_ref, diag_ref, inv_ref, tmp_ref, pcat_ref, qcat_ref, icat_ref, send, recv, ps, pr):
    prow, pcol = lax.axis_index("prow"), lax.axis_index("pcol")

    def front_view(colour, x, y):
        return rest_ref.at[pl.ds(pl.multiple_of((x * 4 + y) * NB, NB), NB), pl.ds(256 * colour, 256)]

    def top_place(p, h):
        return rest_ref.at[pl.ds(pl.multiple_of(h * 512 + p * NB, NB), NB), pl.ds(512, 256)]

    plane = Plane(front_view, ps, pr, None)
    todo = plane.stages()
    barrier = pltpu.get_barrier_semaphore()
    for leg in range(2):
        for step in (1, -1):
            pl.semaphore_signal(barrier, inc=1, device_id=plane.peer(0, leg, step), device_id_type=MESH)
    for s in range(1, 8):
        pl.semaphore_signal(barrier, inc=1, device_id=(lax.rem(prow + s, 8), pcol), device_id_type=MESH)
    rest_ref[pl.ds(pl.multiple_of(pcol * NB, NB), NB), 0:512] = front_ref[...]
    for h in range(2):
        rest_ref[pl.ds(pl.multiple_of(h * 512 + prow * NB, NB), NB), 512:768] = top_ref[h * NB:h * NB + NB]

    def top_copy(s, h):
        n = (s - 1) * 2 + h
        return pltpu.make_async_remote_copy(
            top_ref.at[pl.ds(h * NB, NB)], top_place(prow, h), send.at[n], recv.at[n],
            device_id=(lax.rem(prow + s, 8), pcol), device_id_type=MESH)

    left = lax.broadcasted_iota(jnp.int32, (NB, 128), 1) < NB

    def fill(i, carry):
        at = pl.ds(pl.multiple_of(i * NB, NB), NB)
        for k in range(4):
            even, odd = tiles_ref[i * 8 + 2 * k], tiles_ref[i * 8 + 2 * k + 1]
            a_ref[at, 128 * k:128 * k + 128] = jnp.where(left, even, pltpu.roll(odd, NB, 1))
            a_ref[at, 512 + 128 * k:640 + 128 * k] = jnp.where(left, pltpu.roll(even, NB, 1), odd)
        return carry
    lax.fori_loop(0, 16, fill, 0)
    pl.semaphore_wait(barrier, 11)
    for s in range(1, 8):
        for h in range(2):
            top_copy(s, h).start()

    def step(j, carry):
        for n in range(8):
            @pl.when(j == n)
            def _(n=n):
                todo[n]()
        off = pl.multiple_of(j * 128, 128)
        diag_ref[...] = a_ref[pl.ds(off, 128), pl.ds(off, 128)]
        invert_block(diag_ref, inv_ref, tmp_ref)
        hi, lo = split(inv_ref[...])
        inv_hi_ref[pl.ds(off, 128), :] = hi
        inv_lo_ref[pl.ds(off, 128), :] = lo
        icat_ref[:, 0:128] = hi
        icat_ref[:, 128:256] = hi
        icat_ref[:, 256:384] = lo
        first = (j + 1) // 2

        def panel(r, c):
            base = pl.multiple_of(r * 256, 256)
            hi, lo = split(a_ref[pl.ds(base, 256), pl.ds(off, 128)])
            v = lax.dot_general(jnp.concatenate([hi, lo, hi], axis=1), icat_ref[...], TN, preferred_element_type=F32)
            hi, lo = split(v)
            pcat_ref[pl.ds(base, 256), 0:128] = hi
            pcat_ref[pl.ds(base, 256), 128:256] = lo
            pcat_ref[pl.ds(base, 256), 256:384] = hi
            qcat_ref[pl.ds(base, 256), 0:128] = hi
            qcat_ref[pl.ds(base, 256), 128:256] = hi
            qcat_ref[pl.ds(base, 256), 256:384] = lo
            low_hi_ref[pl.ds(base, 256), pl.ds(off, 128)] = hi
            low_lo_ref[pl.ds(base, 256), pl.ds(off, 128)] = lo
            return c
        lax.fori_loop(first, KK // 256, panel, 0)

        def update(r, c):
            base = pl.multiple_of(r * 256, 256)

            def inner(k, c):
                cb = pl.multiple_of(k * 256, 256)
                a_ref[pl.ds(base, 256), pl.ds(cb, 256)] -= lax.dot_general(
                    pcat_ref[pl.ds(base, 256), :], qcat_ref[pl.ds(cb, 256), :], TN, preferred_element_type=F32)
                return c
            return lax.fori_loop(first, r + 1, inner, c)
        lax.fori_loop(first, KK // 256, update, 0)
        return carry
    lax.fori_loop(0, KK // 128, step, 0)
    plane.drain()
    for s in range(1, 8):
        for h in range(2):
            n = (s - 1) * 2 + h
            top_copy(s, h).wait_send()
            place = top_place(lax.rem(prow + 8 - s, 8), h)
            pltpu.make_async_remote_copy(place, place, send.at[n], recv.at[n],
                                         device_id=(prow, pcol), device_id_type=MESH).wait_recv()


def factor(tiles, front, top):
    return pl.pallas_call(
        factor_kernel,
        out_shape=(
            jax.ShapeDtypeStruct((KK, 768), F32),
            jax.ShapeDtypeStruct((KK, 128), BF16),
            jax.ShapeDtypeStruct((KK, 128), BF16),
            jax.ShapeDtypeStruct((KK, KK), BF16),
            jax.ShapeDtypeStruct((KK, KK), BF16),
        ),
        in_specs=[pl.BlockSpec(memory_space=pltpu.VMEM)] * 3,
        out_specs=[pl.BlockSpec(memory_space=pltpu.VMEM)] * 5,
        scratch_shapes=[
            pltpu.VMEM((KK, KK), F32),
            pltpu.VMEM((128, 128), F32),
            pltpu.VMEM((128, 128), F32),
            pltpu.VMEM((144, 128), F32),
            pltpu.VMEM((KK, 384), BF16),
            pltpu.VMEM((KK, 384), BF16),
            pltpu.VMEM((128, 384), BF16),
            pltpu.SemaphoreType.DMA((14,)),
            pltpu.SemaphoreType.DMA((14,)),
            pltpu.SemaphoreType.DMA((30,)),
            pltpu.SemaphoreType.DMA((30,)),
        ],
        compiler_params=pltpu.CompilerParams(collective_id=3, has_side_effects=True, vmem_limit_bytes=40 << 20),
        name="factor",
    )(tiles, front, top)


def solve_kernel(rest_ref, inv_hi_ref, inv_lo_ref, low_hi_ref, low_lo_ref, local_ref, trail_ref, panel_ref,
                 hi_ref, lo_ref, p_ref):
    for j in range(KK // 128):
        x = rest_ref[128 * j:128 * j + 128, :]
        if j:
            lh, ll = low_hi_ref[128 * j:128 * j + 128, :128 * j], low_lo_ref[128 * j:128 * j + 128, :128 * j]
            ph, pw = hi_ref[:128 * j, :], lo_ref[:128 * j, :]
            x = x - (lax.dot_general(lh, ph, NN, preferred_element_type=F32)
                     + lax.dot_general(lh, pw, NN, preferred_element_type=F32)
                     + lax.dot_general(ll, ph, NN, preferred_element_type=F32))
        xh, xl = split(x)
        ih, il = inv_hi_ref[128 * j:128 * j + 128, :], inv_lo_ref[128 * j:128 * j + 128, :]
        v = (lax.dot_general(ih, xh, NN, preferred_element_type=F32)
             + lax.dot_general(ih, xl, NN, preferred_element_type=F32)
             + lax.dot_general(il, xh, NN, preferred_element_type=F32))
        p_ref[128 * j:128 * j + 128, :] = v[:, :512]
        vh, vl = split(v)
        hi_ref[128 * j:128 * j + 128, :] = vh
        lo_ref[128 * j:128 * j + 128, :] = vl
    rh, rl = hi_ref[:, :512], lo_ref[:, :512]
    ch, cl = hi_ref[:, 512:], lo_ref[:, 512:]
    trail_ref[...] = local_ref[...] - (lax.dot_general(rh, ch, TT, preferred_element_type=F32)
                                       + lax.dot_general(rh, cl, TT, preferred_element_type=F32)
                                       + lax.dot_general(rl, ch, TT, preferred_element_type=F32))
    pcol = lax.axis_index("pcol")
    panel_ref[...] = p_ref[pl.ds(pl.multiple_of(pcol * NB, NB), NB), :].T


def solve(rest, inv_hi, inv_lo, low_hi, low_lo, local):
    return pl.pallas_call(
        solve_kernel,
        out_shape=(jax.ShapeDtypeStruct((512, 256), F32), jax.ShapeDtypeStruct((512, NB), F32)),
        in_specs=[pl.BlockSpec(memory_space=pltpu.VMEM)] * 6,
        out_specs=[pl.BlockSpec(memory_space=pltpu.VMEM)] * 2,
        scratch_shapes=[pltpu.VMEM((KK, 768), BF16)] * 2 + [pltpu.VMEM((KK, 512), F32)],
        compiler_params=pltpu.CompilerParams(vmem_limit_bytes=40 << 20),
        name="solve",
    )(rest, inv_hi, inv_lo, low_hi, low_lo, local)


def per_device(factors, x_factor, zinv_factor, placement):
    rows, cols = route(factors, placement.reshape(32, 128))
    local, front, tiles = pair_blocks(rows.reshape(512, W), cols.reshape(256, W), x_factor, zinv_factor)
    rest, inv_hi, inv_lo, low_hi, low_lo = factor(tiles.reshape(128, NB, 128), front, local[:128])
    return solve(rest, inv_hi, inv_lo, low_hi, low_lo, local)


def solution(mesh):
    in_specs = (P(None, ("prow", "pcol"), None), P(), P(), P())
    out_specs = (P("prow", "pcol"), P("prow", "pcol"))
    return jax.shard_map(per_device, mesh=mesh, in_specs=in_specs, out_specs=out_specs, check_vma=False)
```

```python
import functools
import jax
import jax.numpy as jnp
from jax import lax
from jax.experimental import pallas as pl
from jax.experimental.pallas import tpu as pltpu
from jax.sharding import PartitionSpec as P

RANK = 4
NB = 64
KK = 1024
F32, BF16 = jnp.float32, jnp.bfloat16
SIGNS = (1.0, 1.0, -1.0, -1.0)
MESH = pl.DeviceIdType.MESH
TN = (((1,), (1,)), ((), ()))
NN = (((1,), (0,)), ((), ()))
TT = (((0,), (0,)), ((), ()))


def split(v):
    hi = v.astype(BF16)
    return hi, (v - hi.astype(F32)).astype(BF16)


def spread(v):
    return jnp.broadcast_to(v, (8, 128))


def invert_block(block_ref, inv_ref, tmp_ref):
    lane = lax.broadcasted_iota(jnp.int32, (8, 128), 1)
    sub = lax.broadcasted_iota(jnp.int32, (8, 128), 0)
    rows = [block_ref[8 * i:8 * i + 8, :] for i in range(16)]
    for j in range(16):
        here = (lane >= 8 * j) & (lane < 8 * j + 8)
        mine = rows[j]
        spot = 72 * (j % 2)
        for q in range(8):
            tmp_ref[spot + 8 * q:spot + 8 * q + 8, :] = spread(mine[:, 8 * j + q:8 * j + q + 1])
        tmp_ref[spot + 64:spot + 72, :] = jnp.where(here, (lane == sub + 8 * j).astype(F32), mine)
        a = [[None] * 8 for _ in range(8)]
        for q in range(8):
            for s in range(q, 8):
                a[s][q] = tmp_ref[pl.ds(spot + 8 * q + s, 8, stride=0), :]
        r = [tmp_ref[pl.ds(spot + 64 + t, 8, stride=0), :] for t in range(8)]
        pivots, low = [], []
        for t in range(0, 8, 2):
            u = t + 1
            det = a[t][t] * a[u][u] - a[u][t] * a[u][t]
            inv_det = 1.0 / det
            p00, p01, p11 = a[u][u] * inv_det, -a[u][t] * inv_det, a[t][t] * inv_det
            pivots.append((p00, p01, p11, a[t][t], a[u][t], det))
            m = [[None] * 2 for _ in range(8)]
            for s in range(t + 2, 8):
                m[s][0] = a[s][t] * p00 + a[s][u] * p01
                m[s][1] = a[s][t] * p01 + a[s][u] * p11
            for s in range(t + 2, 8):
                for k in range(t + 2, s + 1):
                    a[s][k] = a[s][k] - (m[s][0] * a[k][t] + m[s][1] * a[k][u])
                r[s] = r[s] - (m[s][0] * r[t] + m[s][1] * r[u])
            low.append(m)
        packed, packed_d = r[0], pivots[0][3]
        for t in range(1, 8):
            p00, p01, p11, a00, a10, det = pivots[t // 2]
            row = a00 * r[t] - a10 * r[t - 1] if t % 2 else r[t]
            packed = jnp.where(sub == t, row, packed)
            packed_d = jnp.where(sub == t, a00 * det if t % 2 else a00, packed_d)
        inv_ref[8 * j:8 * j + 8, :] = jnp.where(lane < 8 * j + 8, packed * lax.rsqrt(packed_d), 0.0)
        if j == 15:
            break
        w = [None] * 8
        for t in (6, 4, 2, 0):
            p00, p01, p11 = pivots[t // 2][:3]
            w[t] = r[t] * p00 + r[t + 1] * p01
            w[t + 1] = r[t] * p01 + r[t + 1] * p11
            for s in range(t + 2, 8):
                w[t] = w[t] - low[t // 2][s][0] * w[s]
                w[t + 1] = w[t + 1] - low[t // 2][s][1] * w[s]
        for i in range(j + 1, 16):
            acc = jnp.where(here, 0.0, rows[i])
            for q in range(8):
                acc = acc - spread(rows[i][:, 8 * j + q:8 * j + q + 1]) * w[q]
            rows[i] = acc


OFFS = 4


class Plane:
    def __init__(self, view, send, recv, arrived):
        self.prow, self.pcol = lax.axis_index("prow"), lax.axis_index("pcol")
        self.me = (self.pcol // 4, lax.rem(self.pcol, 4))
        self.sign = 1 - 2 * lax.rem(self.prow, 2)
        self.offs = (0, -self.sign, self.sign, 2)
        self.raw, self.send, self.recv, self.arrived = view, send, recv, arrived

    def view(self, colour, first, second):
        steps = (first, second) if colour == 0 else (second, first)
        at = [lax.rem(v + s + OFFS, 4) for v, s in zip(self.me, steps)]
        return self.raw(colour, at[0], at[1])

    def peer(self, colour, leg, step):
        dim = leg if colour == 0 else 1 - leg
        at = [lax.rem(v + step + OFFS, 4) if d == dim else v for d, v in enumerate(self.me)]
        return (self.prow, at[0] * 4 + at[1])

    def message(self, colour, leg, o, kind):
        n = colour * 15 + (kind if leg == 0 else 3 + o * 3 + kind)
        carried = -self.sign if kind == 2 else 0
        part = self.view(colour, carried, 0) if leg == 0 else self.view(colour, self.offs[o], carried)
        to = self.peer(colour, leg, -self.sign if kind == 1 else self.sign)
        return pltpu.make_async_remote_copy(part, part, self.send.at[n], self.recv.at[n], device_id=to, device_id_type=MESH)

    def landed(self, colour, leg, o, kind):
        n = colour * 15 + (kind if leg == 0 else 3 + o * 3 + kind)
        come = (-self.sign, self.sign, 2)[kind]
        part = self.view(colour, come, 0) if leg == 0 else self.view(colour, self.offs[o], come)
        pltpu.make_async_remote_copy(part, part, self.send.at[n], self.recv.at[n],
                                     device_id=self.peer(colour, leg, 1), device_id_type=MESH).wait_recv()
        if self.arrived is not None:
            self.arrived(colour, part, 1 + (kind if leg == 0 else 3 + o * 3 + kind))

    def both(self, colour, leg, o):
        self.message(colour, leg, o, 0).start()
        self.message(colour, leg, o, 1).start()

    def stages(self):
        def relay(c, leg, o):
            self.landed(c, leg, o, 0)
            self.message(c, leg, o, 2).start()

        def s0():
            for c in range(2):
                self.both(c, 0, 0)
            for c in range(2):
                self.both(c, 1, 0)

        def s1():
            for c in range(2):
                relay(c, 0, 0)
                self.both(c, 1, 1)

        def s2():
            for c in range(2):
                self.landed(c, 0, 0, 1)
                self.both(c, 1, 2)

        def s3():
            for c in range(2):
                relay(c, 1, 0)

        def s4():
            for c in range(2):
                self.landed(c, 0, 0, 2)
                self.both(c, 1, 3)

        def s5():
            for o in (1, 2):
                for c in range(2):
                    relay(c, 1, o)

        def s6():
            for c in range(2):
                relay(c, 1, 3)

        def s7():
            for o in range(4):
                for c in range(2):
                    self.landed(c, 1, o, 1)
            for o in range(4):
                for c in range(2):
                    self.landed(c, 1, o, 2)
        return [s0, s1, s2, s3, s4, s5, s6, s7]

    def drain(self):
        for c in range(2):
            for kind in range(3):
                self.message(c, 0, 0, kind).wait_send()
                for o in range(4):
                    self.message(c, 1, o, kind).wait_send()


class Column:
    def __init__(self, view, send, recv):
        self.prow, self.pcol = lax.axis_index("prow"), lax.axis_index("pcol")
        self.z, self.core = self.prow // 2, lax.rem(self.prow, 2)
        self.sign = 1 - 2 * self.core
        self.raw, self.send, self.recv = view, send, recv

    def message(self, kind):
        part = self.raw(lax.rem(self.z + (-self.sign if kind == 2 else 0) + OFFS, 4), self.core)
        to = lax.rem(self.z + (-self.sign if kind == 1 else self.sign) + OFFS, 4)
        return pltpu.make_async_remote_copy(part, part, self.send.at[kind], self.recv.at[kind],
                                            device_id=(to * 2 + self.core, self.pcol), device_id_type=MESH)

    def landed(self, kind):
        at = lax.rem(self.z + (-self.sign, self.sign, 2)[kind] + OFFS, 4)
        part = self.raw(at, self.core)
        pltpu.make_async_remote_copy(part, part, self.send.at[kind], self.recv.at[kind],
                                     device_id=(self.prow, self.pcol), device_id_type=MESH).wait_recv()
        return at

    def drain(self):
        for kind in range(3):
            self.message(kind).wait_send()


W = 2176


def before(n):
    return (lax.broadcasted_iota(jnp.int32, (n, n), 0) > lax.broadcasted_iota(jnp.int32, (n, n), 1)).astype(BF16)


def earlier(mask):
    n = mask.shape[0]
    wide = jnp.broadcast_to(mask.astype(F32), (n, 128)).astype(BF16)
    return jnp.dot(before(n), wide, preferred_element_type=F32)[:, 0:1].astype(jnp.int32)


def pick(index, valid, n):
    lane = lax.broadcasted_iota(jnp.int32, (index.shape[0], n), 1)
    hit = lane == index
    if valid is not None:
        hit = hit & valid
    return hit.astype(F32).astype(BF16)


def route_kernel(factors_ref, placed_ref, rows_ref, cols_ref,
                 send_a, got_a, send_b, got_b, piece_ref, ss, rs, ps, pr, zs, zr, xs, xr):
    prow, pcol = lax.axis_index("prow"), lax.axis_index("pcol")
    twin = (lax.rem(pcol, 8), prow + 8 * (pcol // 8))
    at_home = prow == lax.rem(pcol, 8)
    barrier = pltpu.get_barrier_semaphore()
    for s in range(1, 16):
        pl.semaphore_signal(barrier, inc=1, device_id=(prow, lax.rem(pcol + s, 16)), device_id_type=MESH)
    for s in range(1, 8):
        pl.semaphore_signal(barrier, inc=1, device_id=(lax.rem(prow + s, 8), pcol), device_id_type=MESH)

    @pl.when(jnp.logical_not(at_home))
    def _():
        pl.semaphore_signal(barrier, inc=1, device_id=twin, device_id_type=MESH)

    device = prow * 16 + pcol
    line = jnp.broadcast_to(placed_ref[pl.ds(device // 4, 1), :], (8, 128))
    mine = pltpu.roll(line, lax.rem(4 - lax.rem(device, 4), 4) * 32, 1)[0:1, :32]
    group = (mine >> 6) & 7
    row = lax.broadcasted_iota(jnp.int32, (64, 32), 0)
    match = group == (row >> 3)
    ahead = (lax.broadcasted_iota(jnp.int32, (32, 32), 0) < lax.broadcasted_iota(jnp.int32, (32, 32), 1)).astype(BF16)
    rank = jnp.dot(match.astype(F32).astype(BF16), ahead, preferred_element_type=F32).astype(jnp.int32)
    chosen = match & (rank == (row & 7))
    sel = chosen.astype(F32).astype(BF16)
    for r in range(RANK):
        send_a[:, :, 512 * r:512 * r + 512] = jnp.dot(sel, factors_ref[r], preferred_element_type=F32).reshape(8, 8, 512).astype(BF16)

    def total(v):
        return jnp.sum(jnp.where(chosen, v.astype(F32), 0.0), axis=1, keepdims=True)
    lane = lax.broadcasted_iota(jnp.int32, (64, 128), 1)
    tags = jnp.where(lane == 0, total(mine >> 6), jnp.where(lane == 1, total(mine & 63), jnp.where(lane == 2, total(mine * 0 + 1), 0.0)))
    send_a[:, :, 2048:] = tags.reshape(8, 8, 128).astype(BF16)
    got_a[prow] = send_a[prow]

    kind = (placed_ref[...] >> 6) & 15
    spot = lax.broadcasted_iota(jnp.int32, kind.shape, 0) * 4 + (lax.broadcasted_iota(jnp.int32, kind.shape, 1) >> 5)
    prior = (spot & 15) < pcol
    base = [jnp.sum((prior & (kind == prow + 8 * h)).astype(F32), keepdims=True).astype(jnp.int32) for h in range(2)]

    pl.semaphore_wait(barrier, jnp.where(at_home, 22, 23))

    def copy(src, dst, n, to):
        return pltpu.make_async_remote_copy(src, dst, ss.at[n], rs.at[n], device_id=to, device_id_type=MESH)

    def along_prow(s):
        return (lax.rem(prow + s, 8), pcol)

    def along_pcol(s):
        return (prow, lax.rem(pcol + s, 16))

    def slab(ref, i, n):
        return ref.at[pl.ds(pl.multiple_of(i * n, n), n)]

    def a_copy(s):
        return copy(send_a.at[lax.rem(prow + s, 8)], got_a.at[prow], s - 1, along_prow(s))

    def b_copy(s):
        return copy(send_b.at[lax.rem(pcol + s, 16)], got_b.at[pcol], 7 + s - 1, along_pcol(s))

    def twin_copy():
        return copy(piece_ref, cols_ref.at[twin[0]], 22, twin)

    def rows_view(colour, x, y):
        return rows_ref.at[x, y, :, pl.ds(1152 * colour, 1152 if colour == 0 else 1024)]

    def cols_view(z, core):
        return cols_ref.at[z * 2 + core]

    for s in range(1, 8):
        a_copy(s).start()
    for s in range(1, 8):
        spot = got_a.at[lax.rem(prow + 8 - s, 8)]
        copy(spot, spot, s - 1, along_prow(1)).wait_recv()

    got = got_a[...].astype(F32).reshape(64, W).astype(BF16)
    tags = got[:, 2048:].astype(F32)
    valid = tags[:, 2:3] > 0.5
    half = (tags[:, 0:1].astype(jnp.int32) >> 3) & 1
    slot = jnp.zeros((64, 1), jnp.int32)
    for h in range(2):
        li = earlier(valid & (half == h))
        slot = jnp.where(half == h, (8 * h + ((base[h] + li) & 7)) * 8 + (li >> 3), slot)
    send_b[...] = lax.dot_general(pick(slot, valid, 128), got, TT, preferred_element_type=F32).reshape(16, 8, W).astype(BF16)
    got_b[pcol] = send_b[pcol]
    for s in range(1, 16):
        b_copy(s).start()
    for s in range(1, 16):
        spot = got_b.at[lax.rem(pcol + 16 - s, 16)]
        copy(spot, spot, 7 + s - 1, along_prow(1)).wait_recv()

    got = got_b[...].astype(F32).reshape(128, W).astype(BF16)
    valid = got[:, 2048:].astype(F32)[:, 2:3] > 0.5
    piece = lax.dot_general(pick(earlier(valid), valid, 32), got, TT, preferred_element_type=F32).astype(BF16)
    piece_ref[...] = piece
    rows_ref[pcol // 4, lax.rem(pcol, 4)] = piece

    @pl.when(at_home)
    def _():
        cols_ref[prow] = piece

    @pl.when(jnp.logical_not(at_home))
    def _():
        twin_copy().start()
    plane = Plane(rows_view, ps, pr, None)
    column = Column(cols_view, zs, zr)
    core = lax.rem(prow, 2)
    other = prow + 1 - 2 * core

    def across(n, z, whose):
        part = cols_view(z, whose)
        return pltpu.make_async_remote_copy(part, part, xs.at[n], xr.at[n], device_id=(other, pcol), device_id_type=MESH)
    todo = plane.stages()
    todo[0]()
    todo[1]()

    @pl.when(jnp.logical_not(at_home))
    def _():
        copy(cols_ref.at[prow], cols_ref.at[prow], 22, twin).wait_recv()
    column.message(0).start()
    column.message(1).start()
    across(0, prow // 2, core).start()
    todo[2]()
    todo[3]()
    at = [prow // 2, column.landed(0)]
    column.message(2).start()
    across(1, at[1], core).start()
    todo[4]()
    at.append(column.landed(1))
    across(2, at[2], core).start()
    todo[5]()
    at.append(column.landed(2))
    across(3, at[3], core).start()
    todo[6]()
    todo[7]()
    sign = 1 - 2 * core
    for n, shift in enumerate((0, sign, -sign, 2)):
        across(n, lax.rem(prow // 2 + shift + OFFS, 4), 1 - core).wait_recv()
        across(n, at[n], core).wait_send()
    plane.drain()
    column.drain()
    for s in range(1, 8):
        a_copy(s).wait_send()
    for s in range(1, 16):
        b_copy(s).wait_send()

    @pl.when(jnp.logical_not(at_home))
    def _():
        twin_copy().wait_send()


def route(factors, placed):
    return pl.pallas_call(
        route_kernel,
        out_shape=(jax.ShapeDtypeStruct((4, 4, 32, W), BF16), jax.ShapeDtypeStruct((8, 32, W), BF16)),
        in_specs=[pl.BlockSpec(memory_space=pltpu.VMEM)] * 2,
        out_specs=[pl.BlockSpec(memory_space=pltpu.VMEM)] * 2,
        scratch_shapes=[
            pltpu.VMEM((8, 8, W), BF16),
            pltpu.VMEM((8, 8, W), BF16),
            pltpu.VMEM((16, 8, W), BF16),
            pltpu.VMEM((16, 8, W), BF16),
            pltpu.VMEM((32, W), BF16),
            pltpu.SemaphoreType.DMA((23,)),
            pltpu.SemaphoreType.DMA((23,)),
            pltpu.SemaphoreType.DMA((30,)),
            pltpu.SemaphoreType.DMA((30,)),
            pltpu.SemaphoreType.DMA((3,)),
            pltpu.SemaphoreType.DMA((3,)),
            pltpu.SemaphoreType.DMA((4,)),
            pltpu.SemaphoreType.DMA((4,)),
        ],
        compiler_params=pltpu.CompilerParams(collective_id=1, has_side_effects=True, vmem_limit_bytes=24 << 20),
        name="route",
    )(factors, placed)


def pair_kernel(rows_ref, cols_ref, xf_ref, zf_ref, local_ref, front_ref, out_ref, x_ref, z_ref, send, recv, zsend, zrecv, psend, precv):
    prow, pcol = lax.axis_index("prow"), lax.axis_index("pcol")
    z, core = prow // 2, lax.rem(prow, 2)
    other = (prow + 1 - 2 * core, pcol)

    def tile_view(at, whose):
        return out_ref.at[pcol // 4, lax.rem(pcol, 4), at, whose]

    def block_view(colour, x, y):
        return out_ref.at[x, y, :, core, pl.ds(32 * colour, 32)]

    def across(colour, part, n):
        return pltpu.make_async_remote_copy(part, part, psend.at[colour * 16 + n], precv.at[colour * 16 + n],
                                            device_id=other, device_id_type=MESH)
    plane = Plane(block_view, send, recv, lambda colour, part, n: across(colour, part, n).start())
    column = Column(tile_view, zsend, zrecv)
    barrier = pltpu.get_barrier_semaphore()
    for step in (1, -1):
        pl.semaphore_signal(barrier, inc=1, device_id=plane.peer(0, 0, step), device_id_type=MESH)
        pl.semaphore_signal(barrier, inc=1, device_id=plane.peer(0, 1, step), device_id_type=MESH)
        pl.semaphore_signal(barrier, inc=1, device_id=(lax.rem(z + step + OFFS, 4) * 2 + core, pcol), device_id_type=MESH)
    pl.semaphore_signal(barrier, inc=1, device_id=other, device_id_type=MESH)
    depth = xf_ref.shape[0]

    def load(src, first, count, shift, at):
        tags = src[:, 2048:].astype(F32).astype(jnp.int32)
        spot = (tags[:, 0:1] >> shift) * NB + tags[:, 1:2] - first
        rows = lax.dot_general(pick(spot, None, count), src[:, :2048], TT, preferred_element_type=F32).astype(BF16)
        stack = jnp.concatenate([rows[:, r * depth:(r + 1) * depth] for r in range(RANK)], axis=0)
        for dst, mat in ((x_ref, xf_ref), (z_ref, zf_ref)):
            images = jnp.dot(stack, mat[...], preferred_element_type=F32).astype(BF16)
            for r in range(RANK):
                dst[r, at:at + count, :] = images[r * count:(r + 1) * count, :]

    def pair(base, m, other, n):
        acc = None
        for q in range(RANK):
            left_x = jnp.concatenate([x_ref[r, base:base + m, :] for r in range(RANK)], axis=0)
            left_z = jnp.concatenate([z_ref[r, base:base + m, :] for r in range(RANK)], axis=0)
            term = (lax.dot_general(left_x, x_ref[q, other:other + n, :], TN, preferred_element_type=F32)
                    * lax.dot_general(left_z, z_ref[q, other:other + n, :], TN, preferred_element_type=F32))
            term = (term[:m] + term[m:2 * m]) - (term[2 * m:3 * m] + term[3 * m:])
            if acc is None:
                acc = term
            elif SIGNS[q] > 0:
                acc = acc + term
            else:
                acc = acc - term
        return acc

    def chunk(base):
        block = pair(base, 64, 512, 256)
        local_ref[base:base + 64, :] = block

    def turn(base):
        front_ref[:, base:base + 128] = local_ref[base:base + 128, 0:128].T[:NB, :]

    load(cols_ref, 0, 64, 4, 512)
    load(rows_ref, 0, 128, 3, 0)
    out_ref[pcol // 4, lax.rem(pcol, 4), z, core] = pair(512, 64, 0, 128)
    pl.semaphore_wait(barrier, 7)
    column.message(0).start()
    column.message(1).start()
    load(cols_ref, 64, 192, 4, 576)
    column.landed(0)
    column.message(2).start()
    column.landed(1)
    load(rows_ref, 128, 128, 3, 128)
    column.landed(2)
    todo = plane.stages()
    todo[0]()
    for colour in range(2):
        across(colour, plane.view(colour, 0, 0), 0).start()
    load(rows_ref, 256, 256, 3, 256)
    todo[1]()
    for n in range(5):
        chunk(64 * n)
        todo[2 + n]()
    for n in range(5, 8):
        chunk(64 * n)
    for n in range(4):
        turn(128 * n)
    todo[7]()
    plane.drain()
    column.drain()
    mirror = Plane(lambda colour, x, y: out_ref.at[x, y, :, 1 - core, pl.ds(32 * colour, 32)], send, recv, None)
    for colour in range(2):
        for n in range(16):
            leg, o, kind = (0, 0, n - 1) if n < 4 else (1, (n - 4) // 3, (n - 4) % 3)
            come = (-plane.sign, plane.sign, 2)[kind]
            first, second = (0, 0) if n == 0 else ((come, 0) if leg == 0 else (plane.offs[o], come))
            across(colour, plane.view(colour, first, second), n).wait_send()
            come = (plane.sign, -plane.sign, 2)[kind]
            hop = (0, plane.sign, -plane.sign, 2)[o]
            first, second = (0, 0) if n == 0 else ((come, 0) if leg == 0 else (hop, come))
            across(colour, mirror.view(colour, first, second), n).wait_recv()


def pair_blocks(rows, cols, x_factor, z_factor):
    d = x_factor.shape[0]
    return pl.pallas_call(
        pair_kernel,
        out_shape=(
            jax.ShapeDtypeStruct((512, 256), F32),
            jax.ShapeDtypeStruct((NB, 512), F32),
            jax.ShapeDtypeStruct((4, 4, 4, 2, NB, 128), F32),
        ),
        in_specs=[pl.BlockSpec(memory_space=pltpu.VMEM)] * 4,
        out_specs=[pl.BlockSpec(memory_space=pltpu.VMEM)] * 3,
        scratch_shapes=[
            pltpu.VMEM((RANK, 768, d), BF16),
            pltpu.VMEM((RANK, 768, d), BF16),
            pltpu.SemaphoreType.DMA((30,)),
            pltpu.SemaphoreType.DMA((30,)),
            pltpu.SemaphoreType.DMA((3,)),
            pltpu.SemaphoreType.DMA((3,)),
            pltpu.SemaphoreType.DMA((32,)),
            pltpu.SemaphoreType.DMA((32,)),
        ],
        compiler_params=pltpu.CompilerParams(collective_id=2, has_side_effects=True, vmem_limit_bytes=40 << 20),
        name="pairs",
    )(rows, cols, x_factor, z_factor)


def factor_kernel(tiles_ref, front_ref, top_ref, rest_ref, inv_hi_ref, inv_lo_ref, low_hi_ref, low_lo_ref,
                  a_ref, diag_ref, inv_ref, tmp_ref, pcat_ref, qcat_ref, icat_ref, send, recv, ps, pr):
    prow, pcol = lax.axis_index("prow"), lax.axis_index("pcol")

    def front_view(colour, x, y):
        return rest_ref.at[pl.ds(pl.multiple_of((x * 4 + y) * NB, NB), NB), pl.ds(256 * colour, 256)]

    def top_place(p, h):
        return rest_ref.at[pl.ds(pl.multiple_of(h * 512 + p * NB, NB), NB), pl.ds(512, 256)]

    plane = Plane(front_view, ps, pr, None)
    todo = plane.stages()
    barrier = pltpu.get_barrier_semaphore()
    for leg in range(2):
        for step in (1, -1):
            pl.semaphore_signal(barrier, inc=1, device_id=plane.peer(0, leg, step), device_id_type=MESH)
    for s in range(1, 8):
        pl.semaphore_signal(barrier, inc=1, device_id=(lax.rem(prow + s, 8), pcol), device_id_type=MESH)
    rest_ref[pl.ds(pl.multiple_of(pcol * NB, NB), NB), 0:512] = front_ref[...]
    for h in range(2):
        rest_ref[pl.ds(pl.multiple_of(h * 512 + prow * NB, NB), NB), 512:768] = top_ref[h * NB:h * NB + NB]

    def top_copy(s, h):
        n = (s - 1) * 2 + h
        return pltpu.make_async_remote_copy(
            top_ref.at[pl.ds(h * NB, NB)], top_place(prow, h), send.at[n], recv.at[n],
            device_id=(lax.rem(prow + s, 8), pcol), device_id_type=MESH)

    left = lax.broadcasted_iota(jnp.int32, (NB, 128), 1) < NB

    def fill(i, carry):
        at = pl.ds(pl.multiple_of(i * NB, NB), NB)
        for k in range(4):
            even, odd = tiles_ref[i * 8 + 2 * k], tiles_ref[i * 8 + 2 * k + 1]
            a_ref[at, 128 * k:128 * k + 128] = jnp.where(left, even, pltpu.roll(odd, NB, 1))
            a_ref[at, 512 + 128 * k:640 + 128 * k] = jnp.where(left, pltpu.roll(even, NB, 1), odd)
        return carry
    lax.fori_loop(0, 16, fill, 0)
    pl.semaphore_wait(barrier, 11)
    for s in range(1, 8):
        for h in range(2):
            top_copy(s, h).start()

    def bulk(j, off):
        done = j * 128
        cat = icat_ref[...]
        for r in range(4):
            hi, lo = split(a_ref[256 * r:256 * r + 256, pl.ds(off, 128)])
            v = lax.dot_general(jnp.concatenate([hi, lo, hi], axis=1), cat, TN, preferred_element_type=F32)
            row = lax.broadcasted_iota(jnp.int32, (256, 128), 0) + 256 * r
            hi, lo = split(jnp.where(row >= done, v, 0.0))
            pcat_ref[256 * r:256 * r + 256, 0:128] = hi
            pcat_ref[256 * r:256 * r + 256, 128:256] = lo
            pcat_ref[256 * r:256 * r + 256, 256:384] = hi
            qcat_ref[256 * r:256 * r + 256, 0:128] = hi
            qcat_ref[256 * r:256 * r + 256, 128:256] = hi
            qcat_ref[256 * r:256 * r + 256, 256:384] = lo
            low_hi_ref[256 * r:256 * r + 256, pl.ds(off, 128)] = hi
            low_lo_ref[256 * r:256 * r + 256, pl.ds(off, 128)] = lo
        for r in range(4):
            for k in range(r + 1):
                a_ref[256 * r:256 * r + 256, 256 * k:256 * k + 256] -= lax.dot_general(
                    pcat_ref[256 * r:256 * r + 256, :], qcat_ref[256 * k:256 * k + 256, :], TN, preferred_element_type=F32)

    def keep(off):
        hi, lo = split(inv_ref[...])
        inv_hi_ref[pl.ds(off, 128), :] = hi
        inv_lo_ref[pl.ds(off, 128), :] = lo
        icat_ref[:, 0:128] = hi
        icat_ref[:, 128:256] = hi
        icat_ref[:, 256:384] = lo

    def ahead(off):
        nxt = pl.multiple_of(off + 128, 128)
        hi, lo = split(a_ref[pl.ds(nxt, 128), pl.ds(off, 128)])
        v = lax.dot_general(jnp.concatenate([hi, lo, hi], axis=1), icat_ref[...], TN, preferred_element_type=F32)
        hi, lo = split(v)
        diag_ref[...] = a_ref[pl.ds(nxt, 128), pl.ds(nxt, 128)] - lax.dot_general(
            jnp.concatenate([hi, lo, hi], axis=1), jnp.concatenate([hi, hi, lo], axis=1), TN, preferred_element_type=F32)

    todo[0]()
    diag_ref[...] = a_ref[0:128, 0:128]
    invert_block(diag_ref, inv_ref, tmp_ref)
    keep(0)
    ahead(0)

    def step(j, carry):
        off = pl.multiple_of(j * 128, 128)
        for n in range(1, 8):
            @pl.when(j == n)
            def _(n=n):
                todo[n]()
        invert_block(diag_ref, inv_ref, tmp_ref)
        bulk(j, pl.multiple_of(off - 128, 128))
        keep(off)

        @pl.when(j < 7)
        def _():
            ahead(off)
        return carry
    lax.fori_loop(1, 8, step, 0)
    plane.drain()
    for s in range(1, 8):
        for h in range(2):
            n = (s - 1) * 2 + h
            top_copy(s, h).wait_send()
            place = top_place(lax.rem(prow + 8 - s, 8), h)
            pltpu.make_async_remote_copy(place, place, send.at[n], recv.at[n],
                                         device_id=(prow, pcol), device_id_type=MESH).wait_recv()


def factor(tiles, front, top):
    return pl.pallas_call(
        factor_kernel,
        out_shape=(
            jax.ShapeDtypeStruct((KK, 768), F32),
            jax.ShapeDtypeStruct((KK, 128), BF16),
            jax.ShapeDtypeStruct((KK, 128), BF16),
            jax.ShapeDtypeStruct((KK, KK), BF16),
            jax.ShapeDtypeStruct((KK, KK), BF16),
        ),
        in_specs=[pl.BlockSpec(memory_space=pltpu.VMEM)] * 3,
        out_specs=[pl.BlockSpec(memory_space=pltpu.VMEM)] * 5,
        scratch_shapes=[
            pltpu.VMEM((KK, KK), F32),
            pltpu.VMEM((128, 128), F32),
            pltpu.VMEM((128, 128), F32),
            pltpu.VMEM((144, 128), F32),
            pltpu.VMEM((KK, 384), BF16),
            pltpu.VMEM((KK, 384), BF16),
            pltpu.VMEM((128, 384), BF16),
            pltpu.SemaphoreType.DMA((14,)),
            pltpu.SemaphoreType.DMA((14,)),
            pltpu.SemaphoreType.DMA((30,)),
            pltpu.SemaphoreType.DMA((30,)),
        ],
        compiler_params=pltpu.CompilerParams(collective_id=3, has_side_effects=True, vmem_limit_bytes=40 << 20),
        name="factor",
    )(tiles, front, top)


def solve_kernel(rest_ref, inv_hi_ref, inv_lo_ref, low_hi_ref, low_lo_ref, local_ref, trail_ref, panel_ref,
                 hi_ref, lo_ref, p_ref):
    for j in range(KK // 128):
        x = rest_ref[128 * j:128 * j + 128, :]
        if j:
            lh, ll = low_hi_ref[128 * j:128 * j + 128, :128 * j], low_lo_ref[128 * j:128 * j + 128, :128 * j]
            ph, pw = hi_ref[:128 * j, :], lo_ref[:128 * j, :]
            x = x - (lax.dot_general(lh, ph, NN, preferred_element_type=F32)
                     + lax.dot_general(lh, pw, NN, preferred_element_type=F32)
                     + lax.dot_general(ll, ph, NN, preferred_element_type=F32))
        xh, xl = split(x)
        ih, il = inv_hi_ref[128 * j:128 * j + 128, :], inv_lo_ref[128 * j:128 * j + 128, :]
        v = (lax.dot_general(ih, xh, NN, preferred_element_type=F32)
             + lax.dot_general(ih, xl, NN, preferred_element_type=F32)
             + lax.dot_general(il, xh, NN, preferred_element_type=F32))
        p_ref[128 * j:128 * j + 128, :] = v[:, :512]
        vh, vl = split(v)
        hi_ref[128 * j:128 * j + 128, :] = vh
        lo_ref[128 * j:128 * j + 128, :] = vl
    rh, rl = hi_ref[:, :512], lo_ref[:, :512]
    ch, cl = hi_ref[:, 512:], lo_ref[:, 512:]
    trail_ref[...] = local_ref[...] - (lax.dot_general(rh, ch, TT, preferred_element_type=F32)
                                       + lax.dot_general(rh, cl, TT, preferred_element_type=F32)
                                       + lax.dot_general(rl, ch, TT, preferred_element_type=F32))
    pcol = lax.axis_index("pcol")
    panel_ref[...] = p_ref[pl.ds(pl.multiple_of(pcol * NB, NB), NB), :].T


def solve(rest, inv_hi, inv_lo, low_hi, low_lo, local):
    return pl.pallas_call(
        solve_kernel,
        out_shape=(jax.ShapeDtypeStruct((512, 256), F32), jax.ShapeDtypeStruct((512, NB), F32)),
        in_specs=[pl.BlockSpec(memory_space=pltpu.VMEM)] * 6,
        out_specs=[pl.BlockSpec(memory_space=pltpu.VMEM)] * 2,
        scratch_shapes=[pltpu.VMEM((KK, 768), BF16)] * 2 + [pltpu.VMEM((KK, 512), F32)],
        compiler_params=pltpu.CompilerParams(vmem_limit_bytes=40 << 20),
        name="solve",
    )(rest, inv_hi, inv_lo, low_hi, low_lo, local)


def per_device(factors, x_factor, zinv_factor, placement):
    rows, cols = route(factors, placement.reshape(32, 128))
    local, front, tiles = pair_blocks(rows.reshape(512, W), cols.reshape(256, W), x_factor, zinv_factor)
    rest, inv_hi, inv_lo, low_hi, low_lo = factor(tiles.reshape(128, NB, 128), front, local)
    return solve(rest, inv_hi, inv_lo, low_hi, low_lo, local)


def solution(mesh):
    in_specs = (P(None, ("prow", "pcol"), None), P(), P(), P())
    out_specs = (P("prow", "pcol"), P("prow", "pcol"))
    return jax.shard_map(per_device, mesh=mesh, in_specs=in_specs, out_specs=out_specs, check_vma=False)
```

```python
import functools
import jax
import jax.numpy as jnp
from jax import lax
from jax.experimental import pallas as pl
from jax.experimental.pallas import tpu as pltpu
from jax.sharding import PartitionSpec as P

RANK = 4
NB = 64
KK = 1024
F32, BF16 = jnp.float32, jnp.bfloat16
SIGNS = (1.0, 1.0, -1.0, -1.0)
MESH = pl.DeviceIdType.MESH
TN = (((1,), (1,)), ((), ()))
NN = (((1,), (0,)), ((), ()))
TT = (((0,), (0,)), ((), ()))


def split(v):
    hi = v.astype(BF16)
    return hi, (v - hi.astype(F32)).astype(BF16)


def spread(v):
    return jnp.broadcast_to(v, (8, 128))


def invert_block(block_ref, inv_ref, tmp_ref):
    lane = lax.broadcasted_iota(jnp.int32, (8, 128), 1)
    sub = lax.broadcasted_iota(jnp.int32, (8, 128), 0)
    rows = [block_ref[8 * i:8 * i + 8, :] for i in range(16)]
    for j in range(16):
        here = (lane >= 8 * j) & (lane < 8 * j + 8)
        mine = rows[j]
        spot = 72 * (j % 2)
        for q in range(8):
            tmp_ref[spot + 8 * q:spot + 8 * q + 8, :] = spread(mine[:, 8 * j + q:8 * j + q + 1])
        tmp_ref[spot + 64:spot + 72, :] = jnp.where(here, (lane == sub + 8 * j).astype(F32), mine)
        a = [[None] * 8 for _ in range(8)]
        for q in range(8):
            for s in range(q, 8):
                a[s][q] = tmp_ref[pl.ds(spot + 8 * q + s, 8, stride=0), :]
        r = [tmp_ref[pl.ds(spot + 64 + t, 8, stride=0), :] for t in range(8)]
        pivots, low = [], []
        for t in range(0, 8, 2):
            u = t + 1
            det = a[t][t] * a[u][u] - a[u][t] * a[u][t]
            inv_det = 1.0 / det
            p00, p01, p11 = a[u][u] * inv_det, -a[u][t] * inv_det, a[t][t] * inv_det
            pivots.append((p00, p01, p11, a[t][t], a[u][t], det))
            m = [[None] * 2 for _ in range(8)]
            for s in range(t + 2, 8):
                m[s][0] = a[s][t] * p00 + a[s][u] * p01
                m[s][1] = a[s][t] * p01 + a[s][u] * p11
            for s in range(t + 2, 8):
                for k in range(t + 2, s + 1):
                    a[s][k] = a[s][k] - (m[s][0] * a[k][t] + m[s][1] * a[k][u])
                r[s] = r[s] - (m[s][0] * r[t] + m[s][1] * r[u])
            low.append(m)
        packed, packed_d = r[0], pivots[0][3]
        for t in range(1, 8):
            p00, p01, p11, a00, a10, det = pivots[t // 2]
            row = a00 * r[t] - a10 * r[t - 1] if t % 2 else r[t]
            packed = jnp.where(sub == t, row, packed)
            packed_d = jnp.where(sub == t, a00 * det if t % 2 else a00, packed_d)
        inv_ref[8 * j:8 * j + 8, :] = jnp.where(lane < 8 * j + 8, packed * lax.rsqrt(packed_d), 0.0)
        if j == 15:
            break
        w = [None] * 8
        for t in (6, 4, 2, 0):
            p00, p01, p11 = pivots[t // 2][:3]
            w[t] = r[t] * p00 + r[t + 1] * p01
            w[t + 1] = r[t] * p01 + r[t + 1] * p11
            for s in range(t + 2, 8):
                w[t] = w[t] - low[t // 2][s][0] * w[s]
                w[t + 1] = w[t + 1] - low[t // 2][s][1] * w[s]
        for i in range(j + 1, 16):
            acc = jnp.where(here, 0.0, rows[i])
            for q in range(8):
                acc = acc - spread(rows[i][:, 8 * j + q:8 * j + q + 1]) * w[q]
            rows[i] = acc


OFFS = 4


class Plane:
    def __init__(self, view, send, recv, arrived):
        self.prow, self.pcol = lax.axis_index("prow"), lax.axis_index("pcol")
        self.me = (self.pcol // 4, lax.rem(self.pcol, 4))
        self.sign = 1 - 2 * lax.rem(self.prow, 2)
        self.offs = (0, -self.sign, self.sign, 2)
        self.raw, self.send, self.recv, self.arrived = view, send, recv, arrived

    def view(self, colour, first, second):
        steps = (first, second) if colour == 0 else (second, first)
        at = [lax.rem(v + s + OFFS, 4) for v, s in zip(self.me, steps)]
        return self.raw(colour, at[0], at[1])

    def peer(self, colour, leg, step):
        dim = leg if colour == 0 else 1 - leg
        at = [lax.rem(v + step + OFFS, 4) if d == dim else v for d, v in enumerate(self.me)]
        return (self.prow, at[0] * 4 + at[1])

    def message(self, colour, leg, o, kind):
        n = colour * 15 + (kind if leg == 0 else 3 + o * 3 + kind)
        carried = -self.sign if kind == 2 else 0
        part = self.view(colour, carried, 0) if leg == 0 else self.view(colour, self.offs[o], carried)
        to = self.peer(colour, leg, -self.sign if kind == 1 else self.sign)
        return pltpu.make_async_remote_copy(part, part, self.send.at[n], self.recv.at[n], device_id=to, device_id_type=MESH)

    def landed(self, colour, leg, o, kind):
        n = colour * 15 + (kind if leg == 0 else 3 + o * 3 + kind)
        come = (-self.sign, self.sign, 2)[kind]
        part = self.view(colour, come, 0) if leg == 0 else self.view(colour, self.offs[o], come)
        pltpu.make_async_remote_copy(part, part, self.send.at[n], self.recv.at[n],
                                     device_id=self.peer(colour, leg, 1), device_id_type=MESH).wait_recv()
        if self.arrived is not None:
            self.arrived(colour, part, 1 + (kind if leg == 0 else 3 + o * 3 + kind))

    def both(self, colour, leg, o):
        self.message(colour, leg, o, 0).start()
        self.message(colour, leg, o, 1).start()

    def stages(self):
        def relay(c, leg, o):
            self.landed(c, leg, o, 0)
            self.message(c, leg, o, 2).start()

        def s0():
            for c in range(2):
                self.both(c, 0, 0)
            for c in range(2):
                self.both(c, 1, 0)

        def s1():
            for c in range(2):
                relay(c, 0, 0)
                self.both(c, 1, 1)

        def s2():
            for c in range(2):
                self.landed(c, 0, 0, 1)
                self.both(c, 1, 2)

        def s3():
            for c in range(2):
                relay(c, 1, 0)

        def s4():
            for c in range(2):
                self.landed(c, 0, 0, 2)
                self.both(c, 1, 3)

        def s5():
            for o in (1, 2):
                for c in range(2):
                    relay(c, 1, o)

        def s6():
            for c in range(2):
                relay(c, 1, 3)

        def s7():
            for o in range(4):
                for c in range(2):
                    self.landed(c, 1, o, 1)
            for o in range(4):
                for c in range(2):
                    self.landed(c, 1, o, 2)
        return [s0, s1, s2, s3, s4, s5, s6, s7]

    def drain(self):
        for c in range(2):
            for kind in range(3):
                self.message(c, 0, 0, kind).wait_send()
                for o in range(4):
                    self.message(c, 1, o, kind).wait_send()


class Column:
    def __init__(self, view, send, recv):
        self.prow, self.pcol = lax.axis_index("prow"), lax.axis_index("pcol")
        self.z, self.core = self.prow // 2, lax.rem(self.prow, 2)
        self.sign = 1 - 2 * self.core
        self.raw, self.send, self.recv = view, send, recv

    def message(self, kind):
        part = self.raw(lax.rem(self.z + (-self.sign if kind == 2 else 0) + OFFS, 4), self.core)
        to = lax.rem(self.z + (-self.sign if kind == 1 else self.sign) + OFFS, 4)
        return pltpu.make_async_remote_copy(part, part, self.send.at[kind], self.recv.at[kind],
                                            device_id=(to * 2 + self.core, self.pcol), device_id_type=MESH)

    def landed(self, kind):
        at = lax.rem(self.z + (-self.sign, self.sign, 2)[kind] + OFFS, 4)
        part = self.raw(at, self.core)
        pltpu.make_async_remote_copy(part, part, self.send.at[kind], self.recv.at[kind],
                                     device_id=(self.prow, self.pcol), device_id_type=MESH).wait_recv()
        return at

    def drain(self):
        for kind in range(3):
            self.message(kind).wait_send()


W = 2176


def before(n):
    return (lax.broadcasted_iota(jnp.int32, (n, n), 0) > lax.broadcasted_iota(jnp.int32, (n, n), 1)).astype(BF16)


def earlier(mask):
    n = mask.shape[0]
    wide = jnp.broadcast_to(mask.astype(F32), (n, 128)).astype(BF16)
    return jnp.dot(before(n), wide, preferred_element_type=F32)[:, 0:1].astype(jnp.int32)


def pick(index, valid, n):
    lane = lax.broadcasted_iota(jnp.int32, (index.shape[0], n), 1)
    hit = lane == index
    if valid is not None:
        hit = hit & valid
    return hit.astype(F32).astype(BF16)


def route_kernel(factors_hbm, placed_hbm, rows_ref, cols_ref, factors_ref, placed_ref, ls,
                 send_a, got_a, send_b, got_b, piece_ref, ss, rs, ps, pr, zs, zr, xs, xr):
    prow, pcol = lax.axis_index("prow"), lax.axis_index("pcol")
    twin = (lax.rem(pcol, 8), prow + 8 * (pcol // 8))
    at_home = prow == lax.rem(pcol, 8)
    fetch = [pltpu.make_async_copy(placed_hbm, placed_ref, ls.at[0]), pltpu.make_async_copy(factors_hbm, factors_ref, ls.at[1])]
    for f in fetch:
        f.start()
    barrier = pltpu.get_barrier_semaphore()
    for s in range(1, 16):
        pl.semaphore_signal(barrier, inc=1, device_id=(prow, lax.rem(pcol + s, 16)), device_id_type=MESH)
    for s in range(1, 8):
        pl.semaphore_signal(barrier, inc=1, device_id=(lax.rem(prow + s, 8), pcol), device_id_type=MESH)

    @pl.when(jnp.logical_not(at_home))
    def _():
        pl.semaphore_signal(barrier, inc=1, device_id=twin, device_id_type=MESH)

    device = prow * 16 + pcol
    fetch[0].wait()
    line = jnp.broadcast_to(placed_ref[pl.ds(device // 4, 1), :], (8, 128))
    mine = pltpu.roll(line, lax.rem(4 - lax.rem(device, 4), 4) * 32, 1)[0:1, :32]
    group = (mine >> 6) & 7
    row = lax.broadcasted_iota(jnp.int32, (64, 32), 0)
    match = group == (row >> 3)
    ahead = (lax.broadcasted_iota(jnp.int32, (32, 32), 0) < lax.broadcasted_iota(jnp.int32, (32, 32), 1)).astype(BF16)
    rank = jnp.dot(match.astype(F32).astype(BF16), ahead, preferred_element_type=F32).astype(jnp.int32)
    chosen = match & (rank == (row & 7))
    sel = chosen.astype(F32).astype(BF16)
    fetch[1].wait()
    for r in range(RANK):
        send_a[:, :, 512 * r:512 * r + 512] = jnp.dot(sel, factors_ref[r], preferred_element_type=F32).reshape(8, 8, 512).astype(BF16)

    def total(v):
        return jnp.sum(jnp.where(chosen, v.astype(F32), 0.0), axis=1, keepdims=True)
    lane = lax.broadcasted_iota(jnp.int32, (64, 128), 1)
    tags = jnp.where(lane == 0, total(mine >> 6), jnp.where(lane == 1, total(mine & 63), jnp.where(lane == 2, total(mine * 0 + 1), 0.0)))
    send_a[:, :, 2048:] = tags.reshape(8, 8, 128).astype(BF16)
    got_a[prow] = send_a[prow]

    kind = (placed_ref[...] >> 6) & 15
    spot = lax.broadcasted_iota(jnp.int32, kind.shape, 0) * 4 + (lax.broadcasted_iota(jnp.int32, kind.shape, 1) >> 5)
    prior = (spot & 15) < pcol
    base = [jnp.sum((prior & (kind == prow + 8 * h)).astype(F32), keepdims=True).astype(jnp.int32) for h in range(2)]

    pl.semaphore_wait(barrier, jnp.where(at_home, 22, 23))

    def copy(src, dst, n, to):
        return pltpu.make_async_remote_copy(src, dst, ss.at[n], rs.at[n], device_id=to, device_id_type=MESH)

    def along_prow(s):
        return (lax.rem(prow + s, 8), pcol)

    def along_pcol(s):
        return (prow, lax.rem(pcol + s, 16))

    def slab(ref, i, n):
        return ref.at[pl.ds(pl.multiple_of(i * n, n), n)]

    def a_copy(s):
        return copy(send_a.at[lax.rem(prow + s, 8)], got_a.at[prow], s - 1, along_prow(s))

    def b_copy(s):
        return copy(send_b.at[lax.rem(pcol + s, 16)], got_b.at[pcol], 7 + s - 1, along_pcol(s))

    def twin_copy():
        return copy(piece_ref, cols_ref.at[twin[0]], 22, twin)

    def rows_view(colour, x, y):
        return rows_ref.at[x, y, :, pl.ds(1152 * colour, 1152 if colour == 0 else 1024)]

    def cols_view(z, core):
        return cols_ref.at[z * 2 + core]

    for s in range(1, 8):
        a_copy(s).start()
    for s in range(1, 8):
        spot = got_a.at[lax.rem(prow + 8 - s, 8)]
        copy(spot, spot, s - 1, along_prow(1)).wait_recv()

    got = got_a[...].astype(F32).reshape(64, W).astype(BF16)
    tags = got[:, 2048:].astype(F32)
    valid = tags[:, 2:3] > 0.5
    half = (tags[:, 0:1].astype(jnp.int32) >> 3) & 1
    slot = jnp.zeros((64, 1), jnp.int32)
    for h in range(2):
        li = earlier(valid & (half == h))
        slot = jnp.where(half == h, (8 * h + ((base[h] + li) & 7)) * 8 + (li >> 3), slot)
    send_b[...] = lax.dot_general(pick(slot, valid, 128), got, TT, preferred_element_type=F32).reshape(16, 8, W).astype(BF16)
    got_b[pcol] = send_b[pcol]
    for s in range(1, 16):
        b_copy(s).start()
    for s in range(1, 16):
        spot = got_b.at[lax.rem(pcol + 16 - s, 16)]
        copy(spot, spot, 7 + s - 1, along_prow(1)).wait_recv()

    got = got_b[...].astype(F32).reshape(128, W).astype(BF16)
    valid = got[:, 2048:].astype(F32)[:, 2:3] > 0.5
    piece = lax.dot_general(pick(earlier(valid), valid, 32), got, TT, preferred_element_type=F32).astype(BF16)
    piece_ref[...] = piece
    rows_ref[pcol // 4, lax.rem(pcol, 4)] = piece

    @pl.when(at_home)
    def _():
        cols_ref[prow] = piece

    @pl.when(jnp.logical_not(at_home))
    def _():
        twin_copy().start()
    plane = Plane(rows_view, ps, pr, None)
    column = Column(cols_view, zs, zr)
    core = lax.rem(prow, 2)
    other = prow + 1 - 2 * core

    def across(n, z, whose):
        part = cols_view(z, whose)
        return pltpu.make_async_remote_copy(part, part, xs.at[n], xr.at[n], device_id=(other, pcol), device_id_type=MESH)
    todo = plane.stages()
    todo[0]()
    todo[1]()

    @pl.when(jnp.logical_not(at_home))
    def _():
        copy(cols_ref.at[prow], cols_ref.at[prow], 22, twin).wait_recv()
    column.message(0).start()
    column.message(1).start()
    across(0, prow // 2, core).start()
    todo[2]()
    todo[3]()
    at = [prow // 2, column.landed(0)]
    column.message(2).start()
    across(1, at[1], core).start()
    todo[4]()
    at.append(column.landed(1))
    across(2, at[2], core).start()
    todo[5]()
    at.append(column.landed(2))
    across(3, at[3], core).start()
    todo[6]()
    todo[7]()
    sign = 1 - 2 * core
    for n, shift in enumerate((0, sign, -sign, 2)):
        across(n, lax.rem(prow // 2 + shift + OFFS, 4), 1 - core).wait_recv()
        across(n, at[n], core).wait_send()
    plane.drain()
    column.drain()
    for s in range(1, 8):
        a_copy(s).wait_send()
    for s in range(1, 16):
        b_copy(s).wait_send()

    @pl.when(jnp.logical_not(at_home))
    def _():
        twin_copy().wait_send()


def route(factors, placed):
    return pl.pallas_call(
        route_kernel,
        out_shape=(jax.ShapeDtypeStruct((4, 4, 32, W), BF16), jax.ShapeDtypeStruct((8, 32, W), BF16)),
        in_specs=[pl.BlockSpec(memory_space=pltpu.HBM)] * 2,
        out_specs=[pl.BlockSpec(memory_space=pltpu.VMEM)] * 2,
        scratch_shapes=[
            pltpu.VMEM(factors.shape, BF16),
            pltpu.VMEM((32, 128), jnp.int32),
            pltpu.SemaphoreType.DMA((2,)),
            pltpu.VMEM((8, 8, W), BF16),
            pltpu.VMEM((8, 8, W), BF16),
            pltpu.VMEM((16, 8, W), BF16),
            pltpu.VMEM((16, 8, W), BF16),
            pltpu.VMEM((32, W), BF16),
            pltpu.SemaphoreType.DMA((23,)),
            pltpu.SemaphoreType.DMA((23,)),
            pltpu.SemaphoreType.DMA((30,)),
            pltpu.SemaphoreType.DMA((30,)),
            pltpu.SemaphoreType.DMA((3,)),
            pltpu.SemaphoreType.DMA((3,)),
            pltpu.SemaphoreType.DMA((4,)),
            pltpu.SemaphoreType.DMA((4,)),
        ],
        compiler_params=pltpu.CompilerParams(collective_id=1, has_side_effects=True, vmem_limit_bytes=24 << 20),
        name="route",
    )(factors, placed)


def pair_kernel(rows_ref, cols_ref, xf_hbm, zf_hbm, local_ref, front_ref, out_ref, xf_ref, zf_ref, ls, x_ref, z_ref, send, recv, zsend, zrecv, psend, precv):
    prow, pcol = lax.axis_index("prow"), lax.axis_index("pcol")
    z, core = prow // 2, lax.rem(prow, 2)
    other = (prow + 1 - 2 * core, pcol)

    def tile_view(at, whose):
        return out_ref.at[pcol // 4, lax.rem(pcol, 4), at, whose]

    def block_view(colour, x, y):
        return out_ref.at[x, y, :, core, pl.ds(32 * colour, 32)]

    def across(colour, part, n):
        return pltpu.make_async_remote_copy(part, part, psend.at[colour * 16 + n], precv.at[colour * 16 + n],
                                            device_id=other, device_id_type=MESH)
    fetch = [pltpu.make_async_copy(xf_hbm, xf_ref, ls.at[0]), pltpu.make_async_copy(zf_hbm, zf_ref, ls.at[1])]
    for f in fetch:
        f.start()
    plane = Plane(block_view, send, recv, lambda colour, part, n: across(colour, part, n).start())
    column = Column(tile_view, zsend, zrecv)
    barrier = pltpu.get_barrier_semaphore()
    for step in (1, -1):
        pl.semaphore_signal(barrier, inc=1, device_id=plane.peer(0, 0, step), device_id_type=MESH)
        pl.semaphore_signal(barrier, inc=1, device_id=plane.peer(0, 1, step), device_id_type=MESH)
        pl.semaphore_signal(barrier, inc=1, device_id=(lax.rem(z + step + OFFS, 4) * 2 + core, pcol), device_id_type=MESH)
    pl.semaphore_signal(barrier, inc=1, device_id=other, device_id_type=MESH)
    depth = xf_ref.shape[0]

    def load(src, first, count, shift, at, wait=False):
        tags = src[:, 2048:].astype(F32).astype(jnp.int32)
        spot = (tags[:, 0:1] >> shift) * NB + tags[:, 1:2] - first
        rows = lax.dot_general(pick(spot, None, count), src[:, :2048], TT, preferred_element_type=F32).astype(BF16)
        stack = jnp.concatenate([rows[:, r * depth:(r + 1) * depth] for r in range(RANK)], axis=0)
        if wait:
            for f in fetch:
                f.wait()
        for dst, mat in ((x_ref, xf_ref), (z_ref, zf_ref)):
            images = jnp.dot(stack, mat[...], preferred_element_type=F32).astype(BF16)
            for r in range(RANK):
                dst[r, at:at + count, :] = images[r * count:(r + 1) * count, :]

    def pair(base, m, other, n):
        acc = None
        for q in range(RANK):
            left_x = jnp.concatenate([x_ref[r, base:base + m, :] for r in range(RANK)], axis=0)
            left_z = jnp.concatenate([z_ref[r, base:base + m, :] for r in range(RANK)], axis=0)
            term = (lax.dot_general(left_x, x_ref[q, other:other + n, :], TN, preferred_element_type=F32)
                    * lax.dot_general(left_z, z_ref[q, other:other + n, :], TN, preferred_element_type=F32))
            term = (term[:m] + term[m:2 * m]) - (term[2 * m:3 * m] + term[3 * m:])
            if acc is None:
                acc = term
            elif SIGNS[q] > 0:
                acc = acc + term
            else:
                acc = acc - term
        return acc

    def chunk(base):
        block = pair(base, 64, 512, 256)
        local_ref[base:base + 64, :] = block

    def turn(base):
        front_ref[:, base:base + 128] = local_ref[base:base + 128, 0:128].T[:NB, :]

    load(cols_ref, 0, 64, 4, 512, True)
    load(rows_ref, 0, 128, 3, 0)
    out_ref[pcol // 4, lax.rem(pcol, 4), z, core] = pair(512, 64, 0, 128)
    pl.semaphore_wait(barrier, 7)
    column.message(0).start()
    column.message(1).start()
    load(cols_ref, 64, 192, 4, 576)
    column.landed(0)
    column.message(2).start()
    column.landed(1)
    load(rows_ref, 128, 128, 3, 128)
    column.landed(2)
    todo = plane.stages()
    todo[0]()
    for colour in range(2):
        across(colour, plane.view(colour, 0, 0), 0).start()
    load(rows_ref, 256, 256, 3, 256)
    todo[1]()
    for n in range(5):
        chunk(64 * n)
        todo[2 + n]()
    for n in range(5, 8):
        chunk(64 * n)
    for n in range(4):
        turn(128 * n)
    todo[7]()
    plane.drain()
    column.drain()
    mirror = Plane(lambda colour, x, y: out_ref.at[x, y, :, 1 - core, pl.ds(32 * colour, 32)], send, recv, None)
    for colour in range(2):
        for n in range(16):
            leg, o, kind = (0, 0, n - 1) if n < 4 else (1, (n - 4) // 3, (n - 4) % 3)
            come = (-plane.sign, plane.sign, 2)[kind]
            first, second = (0, 0) if n == 0 else ((come, 0) if leg == 0 else (plane.offs[o], come))
            across(colour, plane.view(colour, first, second), n).wait_send()
            come = (plane.sign, -plane.sign, 2)[kind]
            hop = (0, plane.sign, -plane.sign, 2)[o]
            first, second = (0, 0) if n == 0 else ((come, 0) if leg == 0 else (hop, come))
            across(colour, mirror.view(colour, first, second), n).wait_recv()


def pair_blocks(rows, cols, x_factor, z_factor):
    d = x_factor.shape[0]
    return pl.pallas_call(
        pair_kernel,
        out_shape=(
            jax.ShapeDtypeStruct((512, 256), F32),
            jax.ShapeDtypeStruct((NB, 512), F32),
            jax.ShapeDtypeStruct((4, 4, 4, 2, NB, 128), F32),
        ),
        in_specs=[pl.BlockSpec(memory_space=pltpu.VMEM)] * 2 + [pl.BlockSpec(memory_space=pltpu.HBM)] * 2,
        out_specs=[pl.BlockSpec(memory_space=pltpu.VMEM)] * 3,
        scratch_shapes=[
            pltpu.VMEM(x_factor.shape, BF16),
            pltpu.VMEM(z_factor.shape, BF16),
            pltpu.SemaphoreType.DMA((2,)),
            pltpu.VMEM((RANK, 768, d), BF16),
            pltpu.VMEM((RANK, 768, d), BF16),
            pltpu.SemaphoreType.DMA((30,)),
            pltpu.SemaphoreType.DMA((30,)),
            pltpu.SemaphoreType.DMA((3,)),
            pltpu.SemaphoreType.DMA((3,)),
            pltpu.SemaphoreType.DMA((32,)),
            pltpu.SemaphoreType.DMA((32,)),
        ],
        compiler_params=pltpu.CompilerParams(collective_id=2, has_side_effects=True, vmem_limit_bytes=40 << 20),
        name="pairs",
    )(rows, cols, x_factor, z_factor)


def factor_kernel(tiles_ref, front_ref, top_ref, rest_ref, inv_hi_ref, inv_lo_ref, low_hi_ref, low_lo_ref,
                  a_ref, diag_ref, inv_ref, tmp_ref, pcat_ref, qcat_ref, icat_ref, send, recv, ps, pr):
    prow, pcol = lax.axis_index("prow"), lax.axis_index("pcol")

    def front_view(colour, x, y):
        return rest_ref.at[pl.ds(pl.multiple_of((x * 4 + y) * NB, NB), NB), pl.ds(256 * colour, 256)]

    def top_place(p, h):
        return rest_ref.at[pl.ds(pl.multiple_of(h * 512 + p * NB, NB), NB), pl.ds(512, 256)]

    plane = Plane(front_view, ps, pr, None)
    todo = plane.stages()
    barrier = pltpu.get_barrier_semaphore()
    for leg in range(2):
        for step in (1, -1):
            pl.semaphore_signal(barrier, inc=1, device_id=plane.peer(0, leg, step), device_id_type=MESH)
    for s in range(1, 8):
        pl.semaphore_signal(barrier, inc=1, device_id=(lax.rem(prow + s, 8), pcol), device_id_type=MESH)
    rest_ref[pl.ds(pl.multiple_of(pcol * NB, NB), NB), 0:512] = front_ref[...]
    for h in range(2):
        rest_ref[pl.ds(pl.multiple_of(h * 512 + prow * NB, NB), NB), 512:768] = top_ref[h * NB:h * NB + NB]

    def top_copy(s, h):
        n = (s - 1) * 2 + h
        return pltpu.make_async_remote_copy(
            top_ref.at[pl.ds(h * NB, NB)], top_place(prow, h), send.at[n], recv.at[n],
            device_id=(lax.rem(prow + s, 8), pcol), device_id_type=MESH)

    left = lax.broadcasted_iota(jnp.int32, (NB, 128), 1) < NB

    def fill(i, carry):
        at = pl.ds(pl.multiple_of(i * NB, NB), NB)
        for k in range(4):
            even, odd = tiles_ref[i * 8 + 2 * k], tiles_ref[i * 8 + 2 * k + 1]
            a_ref[at, 128 * k:128 * k + 128] = jnp.where(left, even, pltpu.roll(odd, NB, 1))
            a_ref[at, 512 + 128 * k:640 + 128 * k] = jnp.where(left, pltpu.roll(even, NB, 1), odd)
        return carry
    lax.fori_loop(0, 16, fill, 0)
    pl.semaphore_wait(barrier, 11)
    for s in range(1, 8):
        for h in range(2):
            top_copy(s, h).start()

    def bulk(j, off):
        done = j * 128
        cat = icat_ref[...]
        for r in range(4):
            hi, lo = split(a_ref[256 * r:256 * r + 256, pl.ds(off, 128)])
            v = lax.dot_general(jnp.concatenate([hi, lo, hi], axis=1), cat, TN, preferred_element_type=F32)
            row = lax.broadcasted_iota(jnp.int32, (256, 128), 0) + 256 * r
            hi, lo = split(jnp.where(row >= done, v, 0.0))
            pcat_ref[256 * r:256 * r + 256, 0:128] = hi
            pcat_ref[256 * r:256 * r + 256, 128:256] = lo
            pcat_ref[256 * r:256 * r + 256, 256:384] = hi
            qcat_ref[256 * r:256 * r + 256, 0:128] = hi
            qcat_ref[256 * r:256 * r + 256, 128:256] = hi
            qcat_ref[256 * r:256 * r + 256, 256:384] = lo
            low_hi_ref[256 * r:256 * r + 256, pl.ds(off, 128)] = hi
            low_lo_ref[256 * r:256 * r + 256, pl.ds(off, 128)] = lo
        for r in range(4):
            for k in range(r + 1):
                a_ref[256 * r:256 * r + 256, 256 * k:256 * k + 256] -= lax.dot_general(
                    pcat_ref[256 * r:256 * r + 256, :], qcat_ref[256 * k:256 * k + 256, :], TN, preferred_element_type=F32)

    def keep(off):
        hi, lo = split(inv_ref[...])
        inv_hi_ref[pl.ds(off, 128), :] = hi
        inv_lo_ref[pl.ds(off, 128), :] = lo
        icat_ref[:, 0:128] = hi
        icat_ref[:, 128:256] = hi
        icat_ref[:, 256:384] = lo

    def ahead(off):
        nxt = pl.multiple_of(off + 128, 128)
        hi, lo = split(a_ref[pl.ds(nxt, 128), pl.ds(off, 128)])
        v = lax.dot_general(jnp.concatenate([hi, lo, hi], axis=1), icat_ref[...], TN, preferred_element_type=F32)
        hi, lo = split(v)
        diag_ref[...] = a_ref[pl.ds(nxt, 128), pl.ds(nxt, 128)] - lax.dot_general(
            jnp.concatenate([hi, lo, hi], axis=1), jnp.concatenate([hi, hi, lo], axis=1), TN, preferred_element_type=F32)

    todo[0]()
    diag_ref[...] = a_ref[0:128, 0:128]
    invert_block(diag_ref, inv_ref, tmp_ref)
    keep(0)
    ahead(0)

    def step(j, carry):
        off = pl.multiple_of(j * 128, 128)
        for n in range(1, 8):
            @pl.when(j == n)
            def _(n=n):
                todo[n]()
        invert_block(diag_ref, inv_ref, tmp_ref)
        bulk(j, pl.multiple_of(off - 128, 128))
        keep(off)

        @pl.when(j < 7)
        def _():
            ahead(off)
        return carry
    lax.fori_loop(1, 8, step, 0)
    plane.drain()
    for s in range(1, 8):
        for h in range(2):
            n = (s - 1) * 2 + h
            top_copy(s, h).wait_send()
            place = top_place(lax.rem(prow + 8 - s, 8), h)
            pltpu.make_async_remote_copy(place, place, send.at[n], recv.at[n],
                                         device_id=(prow, pcol), device_id_type=MESH).wait_recv()


def factor(tiles, front, top):
    return pl.pallas_call(
        factor_kernel,
        out_shape=(
            jax.ShapeDtypeStruct((KK, 768), F32),
            jax.ShapeDtypeStruct((KK, 128), BF16),
            jax.ShapeDtypeStruct((KK, 128), BF16),
            jax.ShapeDtypeStruct((KK, KK), BF16),
            jax.ShapeDtypeStruct((KK, KK), BF16),
        ),
        in_specs=[pl.BlockSpec(memory_space=pltpu.VMEM)] * 3,
        out_specs=[pl.BlockSpec(memory_space=pltpu.VMEM)] * 5,
        scratch_shapes=[
            pltpu.VMEM((KK, KK), F32),
            pltpu.VMEM((128, 128), F32),
            pltpu.VMEM((128, 128), F32),
            pltpu.VMEM((144, 128), F32),
            pltpu.VMEM((KK, 384), BF16),
            pltpu.VMEM((KK, 384), BF16),
            pltpu.VMEM((128, 384), BF16),
            pltpu.SemaphoreType.DMA((14,)),
            pltpu.SemaphoreType.DMA((14,)),
            pltpu.SemaphoreType.DMA((30,)),
            pltpu.SemaphoreType.DMA((30,)),
        ],
        compiler_params=pltpu.CompilerParams(collective_id=3, has_side_effects=True, vmem_limit_bytes=40 << 20),
        name="factor",
    )(tiles, front, top)


def solve_kernel(rest_ref, inv_hi_ref, inv_lo_ref, low_hi_ref, low_lo_ref, local_ref, trail_ref, panel_ref,
                 hi_ref, lo_ref, p_ref):
    for j in range(KK // 128):
        x = rest_ref[128 * j:128 * j + 128, :]
        if j:
            lh, ll = low_hi_ref[128 * j:128 * j + 128, :128 * j], low_lo_ref[128 * j:128 * j + 128, :128 * j]
            ph, pw = hi_ref[:128 * j, :], lo_ref[:128 * j, :]
            x = x - (lax.dot_general(lh, ph, NN, preferred_element_type=F32)
                     + lax.dot_general(lh, pw, NN, preferred_element_type=F32)
                     + lax.dot_general(ll, ph, NN, preferred_element_type=F32))
        xh, xl = split(x)
        ih, il = inv_hi_ref[128 * j:128 * j + 128, :], inv_lo_ref[128 * j:128 * j + 128, :]
        v = (lax.dot_general(ih, xh, NN, preferred_element_type=F32)
             + lax.dot_general(ih, xl, NN, preferred_element_type=F32)
             + lax.dot_general(il, xh, NN, preferred_element_type=F32))
        p_ref[128 * j:128 * j + 128, :] = v[:, :512]
        vh, vl = split(v)
        hi_ref[128 * j:128 * j + 128, :] = vh
        lo_ref[128 * j:128 * j + 128, :] = vl
    rh, rl = hi_ref[:, :512], lo_ref[:, :512]
    ch, cl = hi_ref[:, 512:], lo_ref[:, 512:]
    trail_ref[...] = local_ref[...] - (lax.dot_general(rh, ch, TT, preferred_element_type=F32)
                                       + lax.dot_general(rh, cl, TT, preferred_element_type=F32)
                                       + lax.dot_general(rl, ch, TT, preferred_element_type=F32))
    pcol = lax.axis_index("pcol")
    panel_ref[...] = p_ref[pl.ds(pl.multiple_of(pcol * NB, NB), NB), :].T


def solve(rest, inv_hi, inv_lo, low_hi, low_lo, local):
    return pl.pallas_call(
        solve_kernel,
        out_shape=(jax.ShapeDtypeStruct((512, 256), F32), jax.ShapeDtypeStruct((512, NB), F32)),
        in_specs=[pl.BlockSpec(memory_space=pltpu.VMEM)] * 6,
        out_specs=[pl.BlockSpec(memory_space=pltpu.VMEM)] * 2,
        scratch_shapes=[pltpu.VMEM((KK, 768), BF16)] * 2 + [pltpu.VMEM((KK, 512), F32)],
        compiler_params=pltpu.CompilerParams(vmem_limit_bytes=40 << 20),
        name="solve",
    )(rest, inv_hi, inv_lo, low_hi, low_lo, local)


def per_device(factors, x_factor, zinv_factor, placement):
    rows, cols = route(factors, placement.reshape(32, 128))
    local, front, tiles = pair_blocks(rows.reshape(512, W), cols.reshape(256, W), x_factor, zinv_factor)
    rest, inv_hi, inv_lo, low_hi, low_lo = factor(tiles.reshape(128, NB, 128), front, local)
    return solve(rest, inv_hi, inv_lo, low_hi, low_lo, local)


def solution(mesh):
    in_specs = (P(None, ("prow", "pcol"), None), P(), P(), P())
    out_specs = (P("prow", "pcol"), P("prow", "pcol"))
    return jax.shard_map(per_device, mesh=mesh, in_specs=in_specs, out_specs=out_specs, check_vma=False)
```

```python
import functools
import jax
import jax.numpy as jnp
from jax import lax
from jax.experimental import pallas as pl
from jax.experimental.pallas import tpu as pltpu
from jax.sharding import PartitionSpec as P

RANK = 4
NB = 64
KK = 1024
F32, BF16 = jnp.float32, jnp.bfloat16
SIGNS = (1.0, 1.0, -1.0, -1.0)
MESH = pl.DeviceIdType.MESH
TN = (((1,), (1,)), ((), ()))
NN = (((1,), (0,)), ((), ()))
TT = (((0,), (0,)), ((), ()))


def split(v):
    hi = v.astype(BF16)
    return hi, (v - hi.astype(F32)).astype(BF16)


def spread(v):
    return jnp.broadcast_to(v, (8, 128))


def invert_block(block_ref, inv_ref, tmp_ref):
    lane = lax.broadcasted_iota(jnp.int32, (8, 128), 1)
    sub = lax.broadcasted_iota(jnp.int32, (8, 128), 0)
    rows = [block_ref[8 * i:8 * i + 8, :] for i in range(16)]
    for j in range(16):
        here = (lane >= 8 * j) & (lane < 8 * j + 8)
        mine = rows[j]
        spot = 72 * (j % 2)
        for q in range(8):
            tmp_ref[spot + 8 * q:spot + 8 * q + 8, :] = spread(mine[:, 8 * j + q:8 * j + q + 1])
        tmp_ref[spot + 64:spot + 72, :] = jnp.where(here, (lane == sub + 8 * j).astype(F32), mine)
        a = [[None] * 8 for _ in range(8)]
        for q in range(8):
            for s in range(q, 8):
                a[s][q] = tmp_ref[pl.ds(spot + 8 * q + s, 8, stride=0), :]
        r = [tmp_ref[pl.ds(spot + 64 + t, 8, stride=0), :] for t in range(8)]
        pivots, low = [], []
        for t in range(0, 8, 2):
            u = t + 1
            det = a[t][t] * a[u][u] - a[u][t] * a[u][t]
            inv_det = 1.0 / det
            p00, p01, p11 = a[u][u] * inv_det, -a[u][t] * inv_det, a[t][t] * inv_det
            pivots.append((p00, p01, p11, a[t][t], a[u][t], det))
            m = [[None] * 2 for _ in range(8)]
            for s in range(t + 2, 8):
                m[s][0] = a[s][t] * p00 + a[s][u] * p01
                m[s][1] = a[s][t] * p01 + a[s][u] * p11
            for s in range(t + 2, 8):
                for k in range(t + 2, s + 1):
                    a[s][k] = a[s][k] - (m[s][0] * a[k][t] + m[s][1] * a[k][u])
                r[s] = r[s] - (m[s][0] * r[t] + m[s][1] * r[u])
            low.append(m)
        packed, packed_d = r[0], pivots[0][3]
        for t in range(1, 8):
            p00, p01, p11, a00, a10, det = pivots[t // 2]
            row = a00 * r[t] - a10 * r[t - 1] if t % 2 else r[t]
            packed = jnp.where(sub == t, row, packed)
            packed_d = jnp.where(sub == t, a00 * det if t % 2 else a00, packed_d)
        inv_ref[8 * j:8 * j + 8, :] = jnp.where(lane < 8 * j + 8, packed * lax.rsqrt(packed_d), 0.0)
        if j == 15:
            break
        w = [None] * 8
        for t in (6, 4, 2, 0):
            p00, p01, p11 = pivots[t // 2][:3]
            w[t] = r[t] * p00 + r[t + 1] * p01
            w[t + 1] = r[t] * p01 + r[t + 1] * p11
            for s in range(t + 2, 8):
                w[t] = w[t] - low[t // 2][s][0] * w[s]
                w[t + 1] = w[t + 1] - low[t // 2][s][1] * w[s]
        for i in range(j + 1, 16):
            acc = jnp.where(here, 0.0, rows[i])
            for q in range(8):
                acc = acc - spread(rows[i][:, 8 * j + q:8 * j + q + 1]) * w[q]
            rows[i] = acc


OFFS = 4


class Plane:
    def __init__(self, view, send, recv, arrived):
        self.prow, self.pcol = lax.axis_index("prow"), lax.axis_index("pcol")
        self.me = (self.pcol // 4, lax.rem(self.pcol, 4))
        self.sign = 1 - 2 * lax.rem(self.prow, 2)
        self.offs = (0, -self.sign, self.sign, 2)
        self.raw, self.send, self.recv, self.arrived = view, send, recv, arrived

    def view(self, colour, first, second):
        steps = (first, second) if colour == 0 else (second, first)
        at = [lax.rem(v + s + OFFS, 4) for v, s in zip(self.me, steps)]
        return self.raw(colour, at[0], at[1])

    def peer(self, colour, leg, step):
        dim = leg if colour == 0 else 1 - leg
        at = [lax.rem(v + step + OFFS, 4) if d == dim else v for d, v in enumerate(self.me)]
        return (self.prow, at[0] * 4 + at[1])

    def message(self, colour, leg, o, kind):
        n = colour * 15 + (kind if leg == 0 else 3 + o * 3 + kind)
        carried = -self.sign if kind == 2 else 0
        part = self.view(colour, carried, 0) if leg == 0 else self.view(colour, self.offs[o], carried)
        to = self.peer(colour, leg, -self.sign if kind == 1 else self.sign)
        return pltpu.make_async_remote_copy(part, part, self.send.at[n], self.recv.at[n], device_id=to, device_id_type=MESH)

    def landed(self, colour, leg, o, kind):
        n = colour * 15 + (kind if leg == 0 else 3 + o * 3 + kind)
        come = (-self.sign, self.sign, 2)[kind]
        part = self.view(colour, come, 0) if leg == 0 else self.view(colour, self.offs[o], come)
        pltpu.make_async_remote_copy(part, part, self.send.at[n], self.recv.at[n],
                                     device_id=self.peer(colour, leg, 1), device_id_type=MESH).wait_recv()
        if self.arrived is not None:
            self.arrived(colour, part, 1 + (kind if leg == 0 else 3 + o * 3 + kind))

    def both(self, colour, leg, o):
        self.message(colour, leg, o, 0).start()
        self.message(colour, leg, o, 1).start()

    def stages(self):
        def relay(c, leg, o):
            self.landed(c, leg, o, 0)
            self.message(c, leg, o, 2).start()

        def s0():
            for c in range(2):
                self.both(c, 0, 0)
            for c in range(2):
                self.both(c, 1, 0)

        def s1():
            for c in range(2):
                relay(c, 0, 0)
                self.both(c, 1, 1)

        def s2():
            for c in range(2):
                self.landed(c, 0, 0, 1)
                self.both(c, 1, 2)

        def s3():
            for c in range(2):
                relay(c, 1, 0)

        def s4():
            for c in range(2):
                self.landed(c, 0, 0, 2)
                self.both(c, 1, 3)

        def s5():
            for o in (1, 2):
                for c in range(2):
                    relay(c, 1, o)

        def s6():
            for c in range(2):
                relay(c, 1, 3)

        def s7():
            for o in range(4):
                for c in range(2):
                    self.landed(c, 1, o, 1)
            for o in range(4):
                for c in range(2):
                    self.landed(c, 1, o, 2)
        return [s0, s1, s2, s3, s4, s5, s6, s7]

    def drain(self):
        for c in range(2):
            for kind in range(3):
                self.message(c, 0, 0, kind).wait_send()
                for o in range(4):
                    self.message(c, 1, o, kind).wait_send()


class Column:
    def __init__(self, view, send, recv):
        self.prow, self.pcol = lax.axis_index("prow"), lax.axis_index("pcol")
        self.z, self.core = self.prow // 2, lax.rem(self.prow, 2)
        self.sign = 1 - 2 * self.core
        self.raw, self.send, self.recv = view, send, recv

    def message(self, kind):
        part = self.raw(lax.rem(self.z + (-self.sign if kind == 2 else 0) + OFFS, 4), self.core)
        to = lax.rem(self.z + (-self.sign if kind == 1 else self.sign) + OFFS, 4)
        return pltpu.make_async_remote_copy(part, part, self.send.at[kind], self.recv.at[kind],
                                            device_id=(to * 2 + self.core, self.pcol), device_id_type=MESH)

    def landed(self, kind):
        at = lax.rem(self.z + (-self.sign, self.sign, 2)[kind] + OFFS, 4)
        part = self.raw(at, self.core)
        pltpu.make_async_remote_copy(part, part, self.send.at[kind], self.recv.at[kind],
                                     device_id=(self.prow, self.pcol), device_id_type=MESH).wait_recv()
        return at

    def drain(self):
        for kind in range(3):
            self.message(kind).wait_send()


W = 2176


def before(n):
    return (lax.broadcasted_iota(jnp.int32, (n, n), 0) > lax.broadcasted_iota(jnp.int32, (n, n), 1)).astype(BF16)


def earlier(mask):
    n = mask.shape[0]
    wide = jnp.broadcast_to(mask.astype(F32), (n, 128)).astype(BF16)
    return jnp.dot(before(n), wide, preferred_element_type=F32)[:, 0:1].astype(jnp.int32)


def pick(index, valid, n):
    lane = lax.broadcasted_iota(jnp.int32, (index.shape[0], n), 1)
    hit = lane == index
    if valid is not None:
        hit = hit & valid
    return hit.astype(F32).astype(BF16)


def route_kernel(factors_ref, placed_ref, rows_ref, cols_ref,
                 send_a, got_a, send_b, got_b, piece_ref, ss, rs, ps, pr, zs, zr, xs, xr):
    prow, pcol = lax.axis_index("prow"), lax.axis_index("pcol")
    twin = (lax.rem(pcol, 8), prow + 8 * (pcol // 8))
    at_home = prow == lax.rem(pcol, 8)
    barrier = pltpu.get_barrier_semaphore()
    for s in range(1, 16):
        pl.semaphore_signal(barrier, inc=1, device_id=(prow, lax.rem(pcol + s, 16)), device_id_type=MESH)
    for s in range(1, 8):
        pl.semaphore_signal(barrier, inc=1, device_id=(lax.rem(prow + s, 8), pcol), device_id_type=MESH)

    @pl.when(jnp.logical_not(at_home))
    def _():
        pl.semaphore_signal(barrier, inc=1, device_id=twin, device_id_type=MESH)

    device = prow * 16 + pcol
    line = jnp.broadcast_to(placed_ref[pl.ds(device // 4, 1), :], (8, 128))
    mine = pltpu.roll(line, lax.rem(4 - lax.rem(device, 4), 4) * 32, 1)[0:1, :32]
    group = (mine >> 6) & 7
    row = lax.broadcasted_iota(jnp.int32, (64, 32), 0)
    match = group == (row >> 3)
    ahead = (lax.broadcasted_iota(jnp.int32, (32, 32), 0) < lax.broadcasted_iota(jnp.int32, (32, 32), 1)).astype(BF16)
    rank = jnp.dot(match.astype(F32).astype(BF16), ahead, preferred_element_type=F32).astype(jnp.int32)
    chosen = match & (rank == (row & 7))
    sel = chosen.astype(F32).astype(BF16)
    for r in range(RANK):
        send_a[:, :, 512 * r:512 * r + 512] = jnp.dot(sel, factors_ref[r], preferred_element_type=F32).reshape(8, 8, 512).astype(BF16)

    def total(v):
        return jnp.sum(jnp.where(chosen, v.astype(F32), 0.0), axis=1, keepdims=True)
    lane = lax.broadcasted_iota(jnp.int32, (64, 128), 1)
    tags = jnp.where(lane == 0, total(mine >> 6), jnp.where(lane == 1, total(mine & 63), jnp.where(lane == 2, total(mine * 0 + 1), 0.0)))
    send_a[:, :, 2048:] = tags.reshape(8, 8, 128).astype(BF16)
    got_a[prow] = send_a[prow]

    kind = (placed_ref[...] >> 6) & 15
    spot = lax.broadcasted_iota(jnp.int32, kind.shape, 0) * 4 + (lax.broadcasted_iota(jnp.int32, kind.shape, 1) >> 5)
    prior = (spot & 15) < pcol
    base = [jnp.sum((prior & (kind == prow + 8 * h)).astype(F32), keepdims=True).astype(jnp.int32) for h in range(2)]

    pl.semaphore_wait(barrier, jnp.where(at_home, 22, 23))

    def copy(src, dst, n, to):
        return pltpu.make_async_remote_copy(src, dst, ss.at[n], rs.at[n], device_id=to, device_id_type=MESH)

    def along_prow(s):
        return (lax.rem(prow + s, 8), pcol)

    def along_pcol(s):
        return (prow, lax.rem(pcol + s, 16))

    def slab(ref, i, n):
        return ref.at[pl.ds(pl.multiple_of(i * n, n), n)]

    def a_copy(s):
        return copy(send_a.at[lax.rem(prow + s, 8)], got_a.at[prow], s - 1, along_prow(s))

    def b_copy(s):
        return copy(send_b.at[lax.rem(pcol + s, 16)], got_b.at[pcol], 7 + s - 1, along_pcol(s))

    def twin_copy():
        return copy(piece_ref, cols_ref.at[twin[0]], 22, twin)

    def rows_view(colour, x, y):
        return rows_ref.at[x, y, :, pl.ds(1152 * colour, 1152 if colour == 0 else 1024)]

    def cols_view(z, core):
        return cols_ref.at[z * 2 + core]

    for s in range(1, 8):
        a_copy(s).start()
    for s in range(1, 8):
        spot = got_a.at[lax.rem(prow + 8 - s, 8)]
        copy(spot, spot, s - 1, along_prow(1)).wait_recv()

    got = got_a[...].astype(F32).reshape(64, W).astype(BF16)
    tags = got[:, 2048:].astype(F32)
    valid = tags[:, 2:3] > 0.5
    half = (tags[:, 0:1].astype(jnp.int32) >> 3) & 1
    slot = jnp.zeros((64, 1), jnp.int32)
    for h in range(2):
        li = earlier(valid & (half == h))
        slot = jnp.where(half == h, (8 * h + ((base[h] + li) & 7)) * 8 + (li >> 3), slot)
    send_b[...] = lax.dot_general(pick(slot, valid, 128), got, TT, preferred_element_type=F32).reshape(16, 8, W).astype(BF16)
    got_b[pcol] = send_b[pcol]
    for s in range(1, 16):
        b_copy(s).start()
    for s in range(1, 16):
        spot = got_b.at[lax.rem(pcol + 16 - s, 16)]
        copy(spot, spot, 7 + s - 1, along_prow(1)).wait_recv()

    got = got_b[...].astype(F32).reshape(128, W).astype(BF16)
    valid = got[:, 2048:].astype(F32)[:, 2:3] > 0.5
    piece = lax.dot_general(pick(earlier(valid), valid, 32), got, TT, preferred_element_type=F32).astype(BF16)
    piece_ref[...] = piece
    rows_ref[pcol // 4, lax.rem(pcol, 4)] = piece

    @pl.when(at_home)
    def _():
        cols_ref[prow] = piece

    @pl.when(jnp.logical_not(at_home))
    def _():
        twin_copy().start()
    plane = Plane(rows_view, ps, pr, None)
    column = Column(cols_view, zs, zr)
    core = lax.rem(prow, 2)
    other = prow + 1 - 2 * core

    def across(n, z, whose):
        part = cols_view(z, whose)
        return pltpu.make_async_remote_copy(part, part, xs.at[n], xr.at[n], device_id=(other, pcol), device_id_type=MESH)
    todo = plane.stages()
    todo[0]()
    todo[1]()

    @pl.when(jnp.logical_not(at_home))
    def _():
        copy(cols_ref.at[prow], cols_ref.at[prow], 22, twin).wait_recv()
    column.message(0).start()
    column.message(1).start()
    across(0, prow // 2, core).start()
    todo[2]()
    todo[3]()
    at = [prow // 2, column.landed(0)]
    column.message(2).start()
    across(1, at[1], core).start()
    todo[4]()
    at.append(column.landed(1))
    across(2, at[2], core).start()
    todo[5]()
    at.append(column.landed(2))
    across(3, at[3], core).start()
    todo[6]()
    todo[7]()
    sign = 1 - 2 * core
    for n, shift in enumerate((0, sign, -sign, 2)):
        across(n, lax.rem(prow // 2 + shift + OFFS, 4), 1 - core).wait_recv()
        across(n, at[n], core).wait_send()
    plane.drain()
    column.drain()
    for s in range(1, 8):
        a_copy(s).wait_send()
    for s in range(1, 16):
        b_copy(s).wait_send()

    @pl.when(jnp.logical_not(at_home))
    def _():
        twin_copy().wait_send()


def route(factors, placed):
    return pl.pallas_call(
        route_kernel,
        out_shape=(jax.ShapeDtypeStruct((4, 4, 32, W), BF16), jax.ShapeDtypeStruct((8, 32, W), BF16)),
        in_specs=[pl.BlockSpec(memory_space=pltpu.VMEM)] * 2,
        out_specs=[pl.BlockSpec(memory_space=pltpu.VMEM)] * 2,
        scratch_shapes=[
            pltpu.VMEM((8, 8, W), BF16),
            pltpu.VMEM((8, 8, W), BF16),
            pltpu.VMEM((16, 8, W), BF16),
            pltpu.VMEM((16, 8, W), BF16),
            pltpu.VMEM((32, W), BF16),
            pltpu.SemaphoreType.DMA((23,)),
            pltpu.SemaphoreType.DMA((23,)),
            pltpu.SemaphoreType.DMA((30,)),
            pltpu.SemaphoreType.DMA((30,)),
            pltpu.SemaphoreType.DMA((3,)),
            pltpu.SemaphoreType.DMA((3,)),
            pltpu.SemaphoreType.DMA((4,)),
            pltpu.SemaphoreType.DMA((4,)),
        ],
        compiler_params=pltpu.CompilerParams(collective_id=1, has_side_effects=True, vmem_limit_bytes=24 << 20),
        name="route",
    )(factors, placed)


def pair_kernel(rows_ref, cols_ref, xf_ref, zf_ref, local_ref, front_ref, out_ref, x_ref, z_ref, send, recv, zsend, zrecv, psend, precv):
    prow, pcol = lax.axis_index("prow"), lax.axis_index("pcol")
    z, core = prow // 2, lax.rem(prow, 2)
    other = (prow + 1 - 2 * core, pcol)

    def tile_view(at, whose):
        return out_ref.at[pcol // 4, lax.rem(pcol, 4), at, whose]

    def block_view(colour, x, y):
        return out_ref.at[x, y, :, core, pl.ds(32 * colour, 32)]

    def across(colour, part, n):
        return pltpu.make_async_remote_copy(part, part, psend.at[colour * 16 + n], precv.at[colour * 16 + n],
                                            device_id=other, device_id_type=MESH)
    plane = Plane(block_view, send, recv, lambda colour, part, n: across(colour, part, n).start())
    column = Column(tile_view, zsend, zrecv)
    barrier = pltpu.get_barrier_semaphore()
    for step in (1, -1):
        pl.semaphore_signal(barrier, inc=1, device_id=plane.peer(0, 0, step), device_id_type=MESH)
        pl.semaphore_signal(barrier, inc=1, device_id=plane.peer(0, 1, step), device_id_type=MESH)
        pl.semaphore_signal(barrier, inc=1, device_id=(lax.rem(z + step + OFFS, 4) * 2 + core, pcol), device_id_type=MESH)
    pl.semaphore_signal(barrier, inc=1, device_id=other, device_id_type=MESH)
    depth = xf_ref.shape[0]

    def load(src, first, count, shift, at):
        tags = src[:, 2048:].astype(F32).astype(jnp.int32)
        spot = (tags[:, 0:1] >> shift) * NB + tags[:, 1:2] - first
        rows = lax.dot_general(pick(spot, None, count), src[:, :2048], TT, preferred_element_type=F32).astype(BF16)
        stack = jnp.concatenate([rows[:, r * depth:(r + 1) * depth] for r in range(RANK)], axis=0)
        for dst, mat in ((x_ref, xf_ref), (z_ref, zf_ref)):
            images = jnp.dot(stack, mat[...], preferred_element_type=F32).astype(BF16)
            for r in range(RANK):
                dst[r, at:at + count, :] = images[r * count:(r + 1) * count, :]

    def pair(base, m, other, n):
        acc = None
        for q in range(RANK):
            left_x = jnp.concatenate([x_ref[r, base:base + m, :] for r in range(RANK)], axis=0)
            left_z = jnp.concatenate([z_ref[r, base:base + m, :] for r in range(RANK)], axis=0)
            term = (lax.dot_general(left_x, x_ref[q, other:other + n, :], TN, preferred_element_type=F32)
                    * lax.dot_general(left_z, z_ref[q, other:other + n, :], TN, preferred_element_type=F32))
            term = (term[:m] + term[m:2 * m]) - (term[2 * m:3 * m] + term[3 * m:])
            if acc is None:
                acc = term
            elif SIGNS[q] > 0:
                acc = acc + term
            else:
                acc = acc - term
        return acc

    def chunk(base):
        block = pair(base, 64, 512, 256)
        local_ref[base:base + 64, :] = block

    def turn(base):
        front_ref[:, base:base + 128] = local_ref[base:base + 128, 0:128].T[:NB, :]

    load(cols_ref, 0, 64, 4, 512)
    load(rows_ref, 0, 128, 3, 0)
    out_ref[pcol // 4, lax.rem(pcol, 4), z, core] = pair(512, 64, 0, 128)
    pl.semaphore_wait(barrier, 7)
    column.message(0).start()
    column.message(1).start()
    load(cols_ref, 64, 192, 4, 576)
    column.landed(0)
    column.message(2).start()
    column.landed(1)
    load(rows_ref, 128, 128, 3, 128)
    column.landed(2)
    todo = plane.stages()
    todo[0]()
    for colour in range(2):
        across(colour, plane.view(colour, 0, 0), 0).start()
    load(rows_ref, 256, 256, 3, 256)
    todo[1]()
    for n in range(5):
        chunk(64 * n)
        todo[2 + n]()
    for n in range(5, 8):
        chunk(64 * n)
    for n in range(4):
        turn(128 * n)
    todo[7]()
    plane.drain()
    column.drain()
    mirror = Plane(lambda colour, x, y: out_ref.at[x, y, :, 1 - core, pl.ds(32 * colour, 32)], send, recv, None)
    for colour in range(2):
        for n in range(16):
            leg, o, kind = (0, 0, n - 1) if n < 4 else (1, (n - 4) // 3, (n - 4) % 3)
            come = (-plane.sign, plane.sign, 2)[kind]
            first, second = (0, 0) if n == 0 else ((come, 0) if leg == 0 else (plane.offs[o], come))
            across(colour, plane.view(colour, first, second), n).wait_send()
            come = (plane.sign, -plane.sign, 2)[kind]
            hop = (0, plane.sign, -plane.sign, 2)[o]
            first, second = (0, 0) if n == 0 else ((come, 0) if leg == 0 else (hop, come))
            across(colour, mirror.view(colour, first, second), n).wait_recv()


def pair_blocks(rows, cols, x_factor, z_factor):
    d = x_factor.shape[0]
    return pl.pallas_call(
        pair_kernel,
        out_shape=(
            jax.ShapeDtypeStruct((512, 256), F32),
            jax.ShapeDtypeStruct((NB, 512), F32),
            jax.ShapeDtypeStruct((4, 4, 4, 2, NB, 128), F32),
        ),
        in_specs=[pl.BlockSpec(memory_space=pltpu.VMEM)] * 4,
        out_specs=[pl.BlockSpec(memory_space=pltpu.VMEM)] * 3,
        scratch_shapes=[
            pltpu.VMEM((RANK, 768, d), BF16),
            pltpu.VMEM((RANK, 768, d), BF16),
            pltpu.SemaphoreType.DMA((30,)),
            pltpu.SemaphoreType.DMA((30,)),
            pltpu.SemaphoreType.DMA((3,)),
            pltpu.SemaphoreType.DMA((3,)),
            pltpu.SemaphoreType.DMA((32,)),
            pltpu.SemaphoreType.DMA((32,)),
        ],
        compiler_params=pltpu.CompilerParams(collective_id=2, has_side_effects=True, vmem_limit_bytes=40 << 20),
        name="pairs",
    )(rows, cols, x_factor, z_factor)


def factor_kernel(tiles_ref, front_ref, top_ref, rest_ref, inv_hi_ref, inv_lo_ref, low_hi_ref, low_lo_ref, sol_hi_ref, sol_lo_ref,
                  a_ref, diag_ref, inv_ref, tmp_ref, pcat_ref, qcat_ref, icat_ref, send, recv, ps, pr):
    prow, pcol = lax.axis_index("prow"), lax.axis_index("pcol")

    def front_view(colour, x, y):
        return rest_ref.at[pl.ds(pl.multiple_of((x * 4 + y) * NB, NB), NB), pl.ds(256 * colour, 256)]

    def top_place(p, h):
        return rest_ref.at[pl.ds(pl.multiple_of(h * 512 + p * NB, NB), NB), pl.ds(512, 256)]

    plane = Plane(front_view, ps, pr, None)
    todo = plane.stages()
    barrier = pltpu.get_barrier_semaphore()
    for leg in range(2):
        for step in (1, -1):
            pl.semaphore_signal(barrier, inc=1, device_id=plane.peer(0, leg, step), device_id_type=MESH)
    for s in range(1, 8):
        pl.semaphore_signal(barrier, inc=1, device_id=(lax.rem(prow + s, 8), pcol), device_id_type=MESH)
    rest_ref[pl.ds(pl.multiple_of(pcol * NB, NB), NB), 0:512] = front_ref[...]
    for h in range(2):
        rest_ref[pl.ds(pl.multiple_of(h * 512 + prow * NB, NB), NB), 512:768] = top_ref[h * NB:h * NB + NB]

    def top_copy(s, h):
        n = (s - 1) * 2 + h
        return pltpu.make_async_remote_copy(
            top_ref.at[pl.ds(h * NB, NB)], top_place(prow, h), send.at[n], recv.at[n],
            device_id=(lax.rem(prow + s, 8), pcol), device_id_type=MESH)

    left = lax.broadcasted_iota(jnp.int32, (NB, 128), 1) < NB

    def fill(i, carry):
        at = pl.ds(pl.multiple_of(i * NB, NB), NB)
        for k in range(4):
            even, odd = tiles_ref[i * 8 + 2 * k], tiles_ref[i * 8 + 2 * k + 1]
            a_ref[at, 128 * k:128 * k + 128] = jnp.where(left, even, pltpu.roll(odd, NB, 1))
            a_ref[at, 512 + 128 * k:640 + 128 * k] = jnp.where(left, pltpu.roll(even, NB, 1), odd)
        return carry
    lax.fori_loop(0, 16, fill, 0)
    pl.semaphore_wait(barrier, 11)
    for s in range(1, 8):
        for h in range(2):
            top_copy(s, h).start()

    def bulk(j, off):
        done = j * 128
        cat = icat_ref[...]
        for r in range(4):
            hi, lo = split(a_ref[256 * r:256 * r + 256, pl.ds(off, 128)])
            v = lax.dot_general(jnp.concatenate([hi, lo, hi], axis=1), cat, TN, preferred_element_type=F32)
            row = lax.broadcasted_iota(jnp.int32, (256, 128), 0) + 256 * r
            hi, lo = split(jnp.where(row >= done, v, 0.0))
            pcat_ref[256 * r:256 * r + 256, 0:128] = hi
            pcat_ref[256 * r:256 * r + 256, 128:256] = lo
            pcat_ref[256 * r:256 * r + 256, 256:384] = hi
            qcat_ref[256 * r:256 * r + 256, 0:128] = hi
            qcat_ref[256 * r:256 * r + 256, 128:256] = hi
            qcat_ref[256 * r:256 * r + 256, 256:384] = lo
            low_hi_ref[256 * r:256 * r + 256, pl.ds(off, 128)] = hi
            low_lo_ref[256 * r:256 * r + 256, pl.ds(off, 128)] = lo
        for r in range(4):
            for k in range(r + 1):
                a_ref[256 * r:256 * r + 256, 256 * k:256 * k + 256] -= lax.dot_general(
                    pcat_ref[256 * r:256 * r + 256, :], qcat_ref[256 * k:256 * k + 256, :], TN, preferred_element_type=F32)

    def keep(off):
        hi, lo = split(inv_ref[...])
        inv_hi_ref[pl.ds(off, 128), :] = hi
        inv_lo_ref[pl.ds(off, 128), :] = lo
        icat_ref[:, 0:128] = hi
        icat_ref[:, 128:256] = hi
        icat_ref[:, 256:384] = lo

    def ahead(off):
        nxt = pl.multiple_of(off + 128, 128)
        hi, lo = split(a_ref[pl.ds(nxt, 128), pl.ds(off, 128)])
        v = lax.dot_general(jnp.concatenate([hi, lo, hi], axis=1), icat_ref[...], TN, preferred_element_type=F32)
        hi, lo = split(v)
        diag_ref[...] = a_ref[pl.ds(nxt, 128), pl.ds(nxt, 128)] - lax.dot_general(
            jnp.concatenate([hi, lo, hi], axis=1), jnp.concatenate([hi, hi, lo], axis=1), TN, preferred_element_type=F32)

    todo[0]()
    diag_ref[...] = a_ref[0:128, 0:128]
    invert_block(diag_ref, inv_ref, tmp_ref)
    keep(0)
    ahead(0)

    def thin(hi, lo, vh, vl):
        return (lax.dot_general(hi, vh, NN, preferred_element_type=F32) + lax.dot_general(hi, vl, NN, preferred_element_type=F32)
                + lax.dot_general(lo, vh, NN, preferred_element_type=F32))

    def panel_rows(e):
        top_at = pl.multiple_of(e * 256, 256)
        low_at = pl.multiple_of(e * 256 + 128, 128)
        top, low = pl.ds(top_at, 128), pl.ds(low_at, 128)
        xh, xl = split(rest_ref[top, :])
        th, tl = split(thin(inv_hi_ref[top, :], inv_lo_ref[top, :], xh, xl))
        x = rest_ref[low, :] - thin(low_hi_ref[low, pl.ds(top_at, 128)], low_lo_ref[low, pl.ds(top_at, 128)], th, tl)
        xh, xl = split(x)
        bh, bl = split(thin(inv_hi_ref[low, :], inv_lo_ref[low, :], xh, xl))
        sol_hi_ref[top, :] = th
        sol_lo_ref[top, :] = tl
        sol_hi_ref[low, :] = bh
        sol_lo_ref[low, :] = bl
        vh = jnp.concatenate([th, bh], axis=0)
        vl = jnp.concatenate([tl, bl], axis=0)
        for t in range(1, 4):
            lh = low_hi_ref[256 * t:256 * t + 256, pl.ds(top_at, 256)]
            ll = low_lo_ref[256 * t:256 * t + 256, pl.ds(top_at, 256)]
            v = thin(lh, ll, vh, vl)
            rest_ref[256 * t:256 * t + 256, :] -= jnp.where(e < t, v, 0.0)

    def step(j, carry):
        off = pl.multiple_of(j * 128, 128)
        for n in range(1, 5):
            @pl.when(j == n)
            def _(n=n):
                todo[2 * n - 1]()
                if n < 4:
                    todo[2 * n]()
        invert_block(diag_ref, inv_ref, tmp_ref)
        bulk(j, pl.multiple_of(off - 128, 128))
        keep(off)
        ahead(off)
        return carry
    lax.fori_loop(1, 5, step, 0)
    for s in range(1, 8):
        for h in range(2):
            n = (s - 1) * 2 + h
            place = top_place(lax.rem(prow + 8 - s, 8), h)
            pltpu.make_async_remote_copy(place, place, send.at[n], recv.at[n],
                                         device_id=(prow, pcol), device_id_type=MESH).wait_recv()
            top_copy(s, h).wait_send()
    plane.drain()

    def last(j, carry):
        off = pl.multiple_of(j * 128, 128)
        invert_block(diag_ref, inv_ref, tmp_ref)
        panel_rows(j - 5)
        bulk(j, pl.multiple_of(off - 128, 128))
        keep(off)

        @pl.when(j < 7)
        def _():
            ahead(off)
        return carry
    lax.fori_loop(5, 8, last, 0)


def factor(tiles, front, top):
    return pl.pallas_call(
        factor_kernel,
        out_shape=(
            jax.ShapeDtypeStruct((KK, 768), F32),
            jax.ShapeDtypeStruct((KK, 128), BF16),
            jax.ShapeDtypeStruct((KK, 128), BF16),
            jax.ShapeDtypeStruct((KK, KK), BF16),
            jax.ShapeDtypeStruct((KK, KK), BF16),
            jax.ShapeDtypeStruct((768, 768), BF16),
            jax.ShapeDtypeStruct((768, 768), BF16),
        ),
        in_specs=[pl.BlockSpec(memory_space=pltpu.VMEM)] * 3,
        out_specs=[pl.BlockSpec(memory_space=pltpu.VMEM)] * 7,
        scratch_shapes=[
            pltpu.VMEM((KK, KK), F32),
            pltpu.VMEM((128, 128), F32),
            pltpu.VMEM((128, 128), F32),
            pltpu.VMEM((144, 128), F32),
            pltpu.VMEM((KK, 384), BF16),
            pltpu.VMEM((KK, 384), BF16),
            pltpu.VMEM((128, 384), BF16),
            pltpu.SemaphoreType.DMA((14,)),
            pltpu.SemaphoreType.DMA((14,)),
            pltpu.SemaphoreType.DMA((30,)),
            pltpu.SemaphoreType.DMA((30,)),
        ],
        compiler_params=pltpu.CompilerParams(collective_id=3, has_side_effects=True, vmem_limit_bytes=18 << 20),
        name="factor",
    )(tiles, front, top)


def solve_kernel(rest_ref, inv_hi_ref, inv_lo_ref, low_hi_ref, low_lo_ref, sol_hi_ref, sol_lo_ref, local_ref, trail_ref, panel_ref,
                 hi_ref, lo_ref):
    def thin(hi, lo, vh, vl):
        return (lax.dot_general(hi, vh, NN, preferred_element_type=F32) + lax.dot_general(hi, vl, NN, preferred_element_type=F32)
                + lax.dot_general(lo, vh, NN, preferred_element_type=F32))
    hi_ref[:768, :] = sol_hi_ref[...]
    lo_ref[:768, :] = sol_lo_ref[...]
    for j in (6, 7):
        at = slice(128 * j, 128 * j + 128)
        x = rest_ref[at, :]
        if j == 7:
            x = x - thin(low_hi_ref[896:, 768:896], low_lo_ref[896:, 768:896], hi_ref[768:896, :], lo_ref[768:896, :])
        xh, xl = split(x)
        vh, vl = split(thin(inv_hi_ref[at, :], inv_lo_ref[at, :], xh, xl))
        hi_ref[at, :] = vh
        lo_ref[at, :] = vl
    rh, rl = hi_ref[:, :512], lo_ref[:, :512]
    ch, cl = hi_ref[:, 512:], lo_ref[:, 512:]
    trail_ref[...] = local_ref[...] - (lax.dot_general(rh, ch, TT, preferred_element_type=F32)
                                       + lax.dot_general(rh, cl, TT, preferred_element_type=F32)
                                       + lax.dot_general(rl, ch, TT, preferred_element_type=F32))
    pcol = lax.axis_index("pcol")
    at = pl.ds(pl.multiple_of(pcol * NB, NB), NB)
    panel_ref[...] = hi_ref[at, :512].astype(F32) + lo_ref[at, :512].astype(F32)


def solve(rest, inv_hi, inv_lo, low_hi, low_lo, ahead_hi, ahead_lo, local):
    return pl.pallas_call(
        solve_kernel,
        out_shape=(jax.ShapeDtypeStruct((512, 256), F32), jax.ShapeDtypeStruct((NB, 512), F32)),
        in_specs=[pl.BlockSpec(memory_space=pltpu.VMEM)] * 8,
        out_specs=[pl.BlockSpec(memory_space=pltpu.VMEM)] * 2,
        scratch_shapes=[pltpu.VMEM((KK, 768), BF16)] * 2,
        compiler_params=pltpu.CompilerParams(vmem_limit_bytes=18 << 20),
        name="solve",
    )(rest, inv_hi, inv_lo, low_hi, low_lo, ahead_hi, ahead_lo, local)


def per_device(factors, x_factor, zinv_factor, placement):
    rows, cols = route(factors, placement.reshape(32, 128))
    local, front, tiles = pair_blocks(rows.reshape(512, W), cols.reshape(256, W), x_factor, zinv_factor)
    rest, inv_hi, inv_lo, low_hi, low_lo, ahead_hi, ahead_lo = factor(tiles.reshape(128, NB, 128), front, local)
    trailing, panel = solve(rest, inv_hi, inv_lo, low_hi, low_lo, ahead_hi, ahead_lo, local)
    return (trailing, panel.T)


def solution(mesh):
    in_specs = (P(None, ("prow", "pcol"), None), P(), P(), P())
    out_specs = (P("prow", "pcol"), P("prow", "pcol"))
    return jax.shard_map(per_device, mesh=mesh, in_specs=in_specs, out_specs=out_specs, check_vma=False)
```

```python
import functools
import jax
import jax.numpy as jnp
from jax import lax
from jax.experimental import pallas as pl
from jax.experimental.pallas import tpu as pltpu
from jax.sharding import PartitionSpec as P

RANK = 4
NB = 64
KK = 1024
F32, BF16 = jnp.float32, jnp.bfloat16
SIGNS = (1.0, 1.0, -1.0, -1.0)
MESH = pl.DeviceIdType.MESH
TN = (((1,), (1,)), ((), ()))
NN = (((1,), (0,)), ((), ()))
TT = (((0,), (0,)), ((), ()))


def split(v):
    hi = v.astype(BF16)
    return hi, (v - hi.astype(F32)).astype(BF16)


def spread(v):
    return jnp.broadcast_to(v, (8, 128))


def invert_block(block_ref, inv_ref, tmp_ref):
    lane = lax.broadcasted_iota(jnp.int32, (8, 128), 1)
    sub = lax.broadcasted_iota(jnp.int32, (8, 128), 0)
    rows = [block_ref[8 * i:8 * i + 8, :] for i in range(16)]
    for j in range(16):
        here = (lane >= 8 * j) & (lane < 8 * j + 8)
        mine = rows[j]
        spot = 72 * (j % 2)
        for q in range(8):
            tmp_ref[spot + 8 * q:spot + 8 * q + 8, :] = spread(mine[:, 8 * j + q:8 * j + q + 1])
        tmp_ref[spot + 64:spot + 72, :] = jnp.where(here, (lane == sub + 8 * j).astype(F32), mine)
        a = [[None] * 8 for _ in range(8)]
        for q in range(8):
            for s in range(q, 8):
                a[s][q] = tmp_ref[pl.ds(spot + 8 * q + s, 8, stride=0), :]
        r = [tmp_ref[pl.ds(spot + 64 + t, 8, stride=0), :] for t in range(8)]
        pivots, low = [], []
        for t in range(0, 8, 2):
            u = t + 1
            det = a[t][t] * a[u][u] - a[u][t] * a[u][t]
            inv_det = 1.0 / det
            p00, p01, p11 = a[u][u] * inv_det, -a[u][t] * inv_det, a[t][t] * inv_det
            pivots.append((p00, p01, p11, a[t][t], a[u][t], det))
            m = [[None] * 2 for _ in range(8)]
            for s in range(t + 2, 8):
                m[s][0] = a[s][t] * p00 + a[s][u] * p01
                m[s][1] = a[s][t] * p01 + a[s][u] * p11
            for s in range(t + 2, 8):
                for k in range(t + 2, s + 1):
                    a[s][k] = a[s][k] - (m[s][0] * a[k][t] + m[s][1] * a[k][u])
                r[s] = r[s] - (m[s][0] * r[t] + m[s][1] * r[u])
            low.append(m)
        packed, packed_d = r[0], pivots[0][3]
        for t in range(1, 8):
            p00, p01, p11, a00, a10, det = pivots[t // 2]
            row = a00 * r[t] - a10 * r[t - 1] if t % 2 else r[t]
            packed = jnp.where(sub == t, row, packed)
            packed_d = jnp.where(sub == t, a00 * det if t % 2 else a00, packed_d)
        inv_ref[8 * j:8 * j + 8, :] = jnp.where(lane < 8 * j + 8, packed * lax.rsqrt(packed_d), 0.0)
        if j == 15:
            break
        w = [None] * 8
        for t in (6, 4, 2, 0):
            p00, p01, p11 = pivots[t // 2][:3]
            w[t] = r[t] * p00 + r[t + 1] * p01
            w[t + 1] = r[t] * p01 + r[t + 1] * p11
            for s in range(t + 2, 8):
                w[t] = w[t] - low[t // 2][s][0] * w[s]
                w[t + 1] = w[t + 1] - low[t // 2][s][1] * w[s]
        for i in range(j + 1, 16):
            acc = jnp.where(here, 0.0, rows[i])
            for q in range(8):
                acc = acc - spread(rows[i][:, 8 * j + q:8 * j + q + 1]) * w[q]
            rows[i] = acc


OFFS = 4


class Plane:
    def __init__(self, view, send, recv, arrived):
        self.prow, self.pcol = lax.axis_index("prow"), lax.axis_index("pcol")
        self.me = (self.pcol // 4, lax.rem(self.pcol, 4))
        self.sign = 1 - 2 * lax.rem(self.prow, 2)
        self.offs = (0, -self.sign, self.sign, 2)
        self.raw, self.send, self.recv, self.arrived = view, send, recv, arrived

    def view(self, colour, first, second):
        steps = (first, second) if colour == 0 else (second, first)
        at = [lax.rem(v + s + OFFS, 4) for v, s in zip(self.me, steps)]
        return self.raw(colour, at[0], at[1])

    def peer(self, colour, leg, step):
        dim = leg if colour == 0 else 1 - leg
        at = [lax.rem(v + step + OFFS, 4) if d == dim else v for d, v in enumerate(self.me)]
        return (self.prow, at[0] * 4 + at[1])

    def message(self, colour, leg, o, kind):
        n = colour * 15 + (kind if leg == 0 else 3 + o * 3 + kind)
        carried = -self.sign if kind == 2 else 0
        part = self.view(colour, carried, 0) if leg == 0 else self.view(colour, self.offs[o], carried)
        to = self.peer(colour, leg, -self.sign if kind == 1 else self.sign)
        return pltpu.make_async_remote_copy(part, part, self.send.at[n], self.recv.at[n], device_id=to, device_id_type=MESH)

    def landed(self, colour, leg, o, kind):
        n = colour * 15 + (kind if leg == 0 else 3 + o * 3 + kind)
        come = (-self.sign, self.sign, 2)[kind]
        part = self.view(colour, come, 0) if leg == 0 else self.view(colour, self.offs[o], come)
        pltpu.make_async_remote_copy(part, part, self.send.at[n], self.recv.at[n],
                                     device_id=self.peer(colour, leg, 1), device_id_type=MESH).wait_recv()
        if self.arrived is not None:
            self.arrived(colour, part, 1 + (kind if leg == 0 else 3 + o * 3 + kind))

    def both(self, colour, leg, o):
        self.message(colour, leg, o, 0).start()
        self.message(colour, leg, o, 1).start()

    def stages(self):
        def relay(c, leg, o):
            self.landed(c, leg, o, 0)
            self.message(c, leg, o, 2).start()

        def s0():
            for c in range(2):
                self.both(c, 0, 0)
            for c in range(2):
                self.both(c, 1, 0)

        def s1():
            for c in range(2):
                relay(c, 0, 0)
                self.both(c, 1, 1)

        def s2():
            for c in range(2):
                self.landed(c, 0, 0, 1)
                self.both(c, 1, 2)

        def s3():
            for c in range(2):
                relay(c, 1, 0)

        def s4():
            for c in range(2):
                self.landed(c, 0, 0, 2)
                self.both(c, 1, 3)

        def s5():
            for o in (1, 2):
                for c in range(2):
                    relay(c, 1, o)

        def s6():
            for c in range(2):
                relay(c, 1, 3)

        def s7():
            for o in range(4):
                for c in range(2):
                    self.landed(c, 1, o, 1)
            for o in range(4):
                for c in range(2):
                    self.landed(c, 1, o, 2)
        return [s0, s1, s2, s3, s4, s5, s6, s7]

    def drain(self):
        for c in range(2):
            for kind in range(3):
                self.message(c, 0, 0, kind).wait_send()
                for o in range(4):
                    self.message(c, 1, o, kind).wait_send()


class Column:
    def __init__(self, view, send, recv):
        self.prow, self.pcol = lax.axis_index("prow"), lax.axis_index("pcol")
        self.z, self.core = self.prow // 2, lax.rem(self.prow, 2)
        self.sign = 1 - 2 * self.core
        self.raw, self.send, self.recv = view, send, recv

    def message(self, kind):
        part = self.raw(lax.rem(self.z + (-self.sign if kind == 2 else 0) + OFFS, 4), self.core)
        to = lax.rem(self.z + (-self.sign if kind == 1 else self.sign) + OFFS, 4)
        return pltpu.make_async_remote_copy(part, part, self.send.at[kind], self.recv.at[kind],
                                            device_id=(to * 2 + self.core, self.pcol), device_id_type=MESH)

    def landed(self, kind):
        at = lax.rem(self.z + (-self.sign, self.sign, 2)[kind] + OFFS, 4)
        part = self.raw(at, self.core)
        pltpu.make_async_remote_copy(part, part, self.send.at[kind], self.recv.at[kind],
                                     device_id=(self.prow, self.pcol), device_id_type=MESH).wait_recv()
        return at

    def drain(self):
        for kind in range(3):
            self.message(kind).wait_send()


W = 2176


def before(n):
    return (lax.broadcasted_iota(jnp.int32, (n, n), 0) > lax.broadcasted_iota(jnp.int32, (n, n), 1)).astype(BF16)


def earlier(mask):
    n = mask.shape[0]
    wide = jnp.broadcast_to(mask.astype(F32), (n, 128)).astype(BF16)
    return jnp.dot(before(n), wide, preferred_element_type=F32)[:, 0:1].astype(jnp.int32)


def pick(index, valid, n):
    lane = lax.broadcasted_iota(jnp.int32, (index.shape[0], n), 1)
    hit = lane == index
    if valid is not None:
        hit = hit & valid
    return hit.astype(F32).astype(BF16)


def route_kernel(factors_ref, placed_ref, rows_ref, cols_ref,
                 send_a, got_a, send_b, got_b, piece_ref, ss, rs, ps, pr, zs, zr, xs, xr):
    prow, pcol = lax.axis_index("prow"), lax.axis_index("pcol")
    twin = (lax.rem(pcol, 8), prow + 8 * (pcol // 8))
    at_home = prow == lax.rem(pcol, 8)
    barrier = pltpu.get_barrier_semaphore()
    for s in range(1, 16):
        pl.semaphore_signal(barrier, inc=1, device_id=(prow, lax.rem(pcol + s, 16)), device_id_type=MESH)
    for s in range(1, 8):
        pl.semaphore_signal(barrier, inc=1, device_id=(lax.rem(prow + s, 8), pcol), device_id_type=MESH)

    @pl.when(jnp.logical_not(at_home))
    def _():
        pl.semaphore_signal(barrier, inc=1, device_id=twin, device_id_type=MESH)

    device = prow * 16 + pcol
    line = jnp.broadcast_to(placed_ref[pl.ds(device // 4, 1), :], (8, 128))
    mine = pltpu.roll(line, lax.rem(4 - lax.rem(device, 4), 4) * 32, 1)[0:1, :32]
    group = (mine >> 6) & 7
    row = lax.broadcasted_iota(jnp.int32, (64, 32), 0)
    match = group == (row >> 3)
    ahead = (lax.broadcasted_iota(jnp.int32, (32, 32), 0) < lax.broadcasted_iota(jnp.int32, (32, 32), 1)).astype(BF16)
    rank = jnp.dot(match.astype(F32).astype(BF16), ahead, preferred_element_type=F32).astype(jnp.int32)
    chosen = match & (rank == (row & 7))
    sel = chosen.astype(F32).astype(BF16)
    for r in range(RANK):
        send_a[:, :, 512 * r:512 * r + 512] = jnp.dot(sel, factors_ref[r], preferred_element_type=F32).reshape(8, 8, 512).astype(BF16)

    def total(v):
        return jnp.sum(jnp.where(chosen, v.astype(F32), 0.0), axis=1, keepdims=True)
    lane = lax.broadcasted_iota(jnp.int32, (64, 128), 1)
    tags = jnp.where(lane == 0, total(mine >> 6), jnp.where(lane == 1, total(mine & 63), jnp.where(lane == 2, total(mine * 0 + 1), 0.0)))
    send_a[:, :, 2048:] = tags.reshape(8, 8, 128).astype(BF16)
    got_a[prow] = send_a[prow]

    kind = (placed_ref[...] >> 6) & 15
    spot = lax.broadcasted_iota(jnp.int32, kind.shape, 0) * 4 + (lax.broadcasted_iota(jnp.int32, kind.shape, 1) >> 5)
    prior = (spot & 15) < pcol
    base = [jnp.sum((prior & (kind == prow + 8 * h)).astype(F32), keepdims=True).astype(jnp.int32) for h in range(2)]

    pl.semaphore_wait(barrier, jnp.where(at_home, 22, 23))

    def copy(src, dst, n, to):
        return pltpu.make_async_remote_copy(src, dst, ss.at[n], rs.at[n], device_id=to, device_id_type=MESH)

    def along_prow(s):
        return (lax.rem(prow + s, 8), pcol)

    def along_pcol(s):
        return (prow, lax.rem(pcol + s, 16))

    def slab(ref, i, n):
        return ref.at[pl.ds(pl.multiple_of(i * n, n), n)]

    def a_copy(s):
        return copy(send_a.at[lax.rem(prow + s, 8)], got_a.at[prow], s - 1, along_prow(s))

    def b_copy(s):
        return copy(send_b.at[lax.rem(pcol + s, 16)], got_b.at[pcol], 7 + s - 1, along_pcol(s))

    def twin_copy():
        return copy(piece_ref, cols_ref.at[twin[0]], 22, twin)

    def rows_view(colour, x, y):
        return rows_ref.at[x, y, :, pl.ds(1152 * colour, 1152 if colour == 0 else 1024)]

    def cols_view(z, core):
        return cols_ref.at[z * 2 + core]

    for s in range(1, 8):
        a_copy(s).start()
    for s in range(1, 8):
        spot = got_a.at[lax.rem(prow + 8 - s, 8)]
        copy(spot, spot, s - 1, along_prow(1)).wait_recv()

    got = got_a[...].astype(F32).reshape(64, W).astype(BF16)
    tags = got[:, 2048:].astype(F32)
    valid = tags[:, 2:3] > 0.5
    half = (tags[:, 0:1].astype(jnp.int32) >> 3) & 1
    slot = jnp.zeros((64, 1), jnp.int32)
    for h in range(2):
        li = earlier(valid & (half == h))
        slot = jnp.where(half == h, (8 * h + ((base[h] + li) & 7)) * 8 + (li >> 3), slot)
    send_b[...] = lax.dot_general(pick(slot, valid, 128), got, TT, preferred_element_type=F32).reshape(16, 8, W).astype(BF16)
    got_b[pcol] = send_b[pcol]
    for s in range(1, 16):
        b_copy(s).start()
    for s in range(1, 16):
        spot = got_b.at[lax.rem(pcol + 16 - s, 16)]
        copy(spot, spot, 7 + s - 1, along_prow(1)).wait_recv()

    got = got_b[...].astype(F32).reshape(128, W).astype(BF16)
    valid = got[:, 2048:].astype(F32)[:, 2:3] > 0.5
    piece = lax.dot_general(pick(earlier(valid), valid, 32), got, TT, preferred_element_type=F32).astype(BF16)
    piece_ref[...] = piece
    rows_ref[pcol // 4, lax.rem(pcol, 4)] = piece

    @pl.when(at_home)
    def _():
        cols_ref[prow] = piece

    @pl.when(jnp.logical_not(at_home))
    def _():
        twin_copy().start()
    plane = Plane(rows_view, ps, pr, None)
    column = Column(cols_view, zs, zr)
    core = lax.rem(prow, 2)
    other = prow + 1 - 2 * core

    def across(n, z, whose):
        part = cols_view(z, whose)
        return pltpu.make_async_remote_copy(part, part, xs.at[n], xr.at[n], device_id=(other, pcol), device_id_type=MESH)
    todo = plane.stages()
    todo[0]()
    todo[1]()

    @pl.when(jnp.logical_not(at_home))
    def _():
        copy(cols_ref.at[prow], cols_ref.at[prow], 22, twin).wait_recv()
    column.message(0).start()
    column.message(1).start()
    across(0, prow // 2, core).start()
    todo[2]()
    todo[3]()
    at = [prow // 2, column.landed(0)]
    column.message(2).start()
    across(1, at[1], core).start()
    todo[4]()
    at.append(column.landed(1))
    across(2, at[2], core).start()
    todo[5]()
    at.append(column.landed(2))
    across(3, at[3], core).start()
    todo[6]()
    todo[7]()
    sign = 1 - 2 * core
    for n, shift in enumerate((0, sign, -sign, 2)):
        across(n, lax.rem(prow // 2 + shift + OFFS, 4), 1 - core).wait_recv()
        across(n, at[n], core).wait_send()
    plane.drain()
    column.drain()
    for s in range(1, 8):
        a_copy(s).wait_send()
    for s in range(1, 16):
        b_copy(s).wait_send()

    @pl.when(jnp.logical_not(at_home))
    def _():
        twin_copy().wait_send()


def route(factors, placed):
    return pl.pallas_call(
        route_kernel,
        out_shape=(jax.ShapeDtypeStruct((4, 4, 32, W), BF16), jax.ShapeDtypeStruct((8, 32, W), BF16)),
        in_specs=[pl.BlockSpec(memory_space=pltpu.VMEM)] * 2,
        out_specs=[pl.BlockSpec(memory_space=pltpu.VMEM)] * 2,
        scratch_shapes=[
            pltpu.VMEM((8, 8, W), BF16),
            pltpu.VMEM((8, 8, W), BF16),
            pltpu.VMEM((16, 8, W), BF16),
            pltpu.VMEM((16, 8, W), BF16),
            pltpu.VMEM((32, W), BF16),
            pltpu.SemaphoreType.DMA((23,)),
            pltpu.SemaphoreType.DMA((23,)),
            pltpu.SemaphoreType.DMA((30,)),
            pltpu.SemaphoreType.DMA((30,)),
            pltpu.SemaphoreType.DMA((3,)),
            pltpu.SemaphoreType.DMA((3,)),
            pltpu.SemaphoreType.DMA((4,)),
            pltpu.SemaphoreType.DMA((4,)),
        ],
        compiler_params=pltpu.CompilerParams(collective_id=1, has_side_effects=True, vmem_limit_bytes=24 << 20),
        name="route",
    )(factors, placed)


def pair_kernel(rows_ref, cols_ref, xf_ref, zf_ref, local_ref, front_ref, out_ref, x_ref, z_ref, send, recv, zsend, zrecv, psend, precv):
    prow, pcol = lax.axis_index("prow"), lax.axis_index("pcol")
    z, core = prow // 2, lax.rem(prow, 2)
    other = (prow + 1 - 2 * core, pcol)

    def tile_view(at, whose):
        return out_ref.at[pcol // 4, lax.rem(pcol, 4), at, whose]

    def block_view(colour, x, y):
        return out_ref.at[x, y, :, core, pl.ds(32 * colour, 32)]

    def across(colour, part, n):
        return pltpu.make_async_remote_copy(part, part, psend.at[colour * 16 + n], precv.at[colour * 16 + n],
                                            device_id=other, device_id_type=MESH)
    plane = Plane(block_view, send, recv, lambda colour, part, n: across(colour, part, n).start())
    column = Column(tile_view, zsend, zrecv)
    barrier = pltpu.get_barrier_semaphore()
    for step in (1, -1):
        pl.semaphore_signal(barrier, inc=1, device_id=plane.peer(0, 0, step), device_id_type=MESH)
        pl.semaphore_signal(barrier, inc=1, device_id=plane.peer(0, 1, step), device_id_type=MESH)
        pl.semaphore_signal(barrier, inc=1, device_id=(lax.rem(z + step + OFFS, 4) * 2 + core, pcol), device_id_type=MESH)
    pl.semaphore_signal(barrier, inc=1, device_id=other, device_id_type=MESH)
    depth = xf_ref.shape[0]

    def load(src, first, count, shift, at):
        tags = src[:, 2048:].astype(F32).astype(jnp.int32)
        spot = (tags[:, 0:1] >> shift) * NB + tags[:, 1:2] - first
        rows = lax.dot_general(pick(spot, None, count), src[:, :2048], TT, preferred_element_type=F32).astype(BF16)
        stack = jnp.concatenate([rows[:, r * depth:(r + 1) * depth] for r in range(RANK)], axis=0)
        for dst, mat in ((x_ref, xf_ref), (z_ref, zf_ref)):
            images = jnp.dot(stack, mat[...], preferred_element_type=F32).astype(BF16)
            for r in range(RANK):
                dst[r, at:at + count, :] = images[r * count:(r + 1) * count, :]

    def pair(base, m, other, n):
        acc = None
        for q in range(RANK):
            left_x = jnp.concatenate([x_ref[r, base:base + m, :] for r in range(RANK)], axis=0)
            left_z = jnp.concatenate([z_ref[r, base:base + m, :] for r in range(RANK)], axis=0)
            term = (lax.dot_general(left_x, x_ref[q, other:other + n, :], TN, preferred_element_type=F32)
                    * lax.dot_general(left_z, z_ref[q, other:other + n, :], TN, preferred_element_type=F32))
            term = (term[:m] + term[m:2 * m]) - (term[2 * m:3 * m] + term[3 * m:])
            if acc is None:
                acc = term
            elif SIGNS[q] > 0:
                acc = acc + term
            else:
                acc = acc - term
        return acc

    def chunk(base):
        block = pair(base, 64, 512, 256)
        local_ref[base:base + 64, :] = block

    def turn(base):
        front_ref[:, base:base + 128] = local_ref[base:base + 128, 0:128].T[:NB, :]

    load(cols_ref, 0, 64, 4, 512)
    load(rows_ref, 0, 128, 3, 0)
    out_ref[pcol // 4, lax.rem(pcol, 4), z, core] = pair(512, 64, 0, 128)
    pl.semaphore_wait(barrier, 7)
    column.message(0).start()
    column.message(1).start()
    load(cols_ref, 64, 192, 4, 576)
    column.landed(0)
    column.message(2).start()
    column.landed(1)
    chunk(0)
    column.landed(2)
    todo = plane.stages()
    todo[0]()
    for colour in range(2):
        across(colour, plane.view(colour, 0, 0), 0).start()
    load(rows_ref, 128, 384, 3, 128)
    todo[1]()
    for n in range(1, 6):
        chunk(64 * n)
        todo[1 + n]()
    for n in range(6, 8):
        chunk(64 * n)
    for n in range(4):
        turn(128 * n)
    todo[7]()
    plane.drain()
    column.drain()
    mirror = Plane(lambda colour, x, y: out_ref.at[x, y, :, 1 - core, pl.ds(32 * colour, 32)], send, recv, None)
    for colour in range(2):
        for n in range(16):
            leg, o, kind = (0, 0, n - 1) if n < 4 else (1, (n - 4) // 3, (n - 4) % 3)
            come = (-plane.sign, plane.sign, 2)[kind]
            first, second = (0, 0) if n == 0 else ((come, 0) if leg == 0 else (plane.offs[o], come))
            across(colour, plane.view(colour, first, second), n).wait_send()
            come = (plane.sign, -plane.sign, 2)[kind]
            hop = (0, plane.sign, -plane.sign, 2)[o]
            first, second = (0, 0) if n == 0 else ((come, 0) if leg == 0 else (hop, come))
            across(colour, mirror.view(colour, first, second), n).wait_recv()


def pair_blocks(rows, cols, x_factor, z_factor):
    d = x_factor.shape[0]
    return pl.pallas_call(
        pair_kernel,
        out_shape=(
            jax.ShapeDtypeStruct((512, 256), F32),
            jax.ShapeDtypeStruct((NB, 512), F32),
            jax.ShapeDtypeStruct((4, 4, 4, 2, NB, 128), F32),
        ),
        in_specs=[pl.BlockSpec(memory_space=pltpu.VMEM)] * 4,
        out_specs=[pl.BlockSpec(memory_space=pltpu.VMEM)] * 3,
        scratch_shapes=[
            pltpu.VMEM((RANK, 768, d), BF16),
            pltpu.VMEM((RANK, 768, d), BF16),
            pltpu.SemaphoreType.DMA((30,)),
            pltpu.SemaphoreType.DMA((30,)),
            pltpu.SemaphoreType.DMA((3,)),
            pltpu.SemaphoreType.DMA((3,)),
            pltpu.SemaphoreType.DMA((32,)),
            pltpu.SemaphoreType.DMA((32,)),
        ],
        compiler_params=pltpu.CompilerParams(collective_id=2, has_side_effects=True, vmem_limit_bytes=40 << 20),
        name="pairs",
    )(rows, cols, x_factor, z_factor)


def factor_kernel(tiles_ref, front_ref, top_ref, rest_ref, inv_hi_ref, inv_lo_ref, low_hi_ref, low_lo_ref, sol_hi_ref, sol_lo_ref,
                  a_ref, diag_ref, inv_ref, tmp_ref, pcat_ref, qcat_ref, icat_ref, send, recv, ps, pr):
    prow, pcol = lax.axis_index("prow"), lax.axis_index("pcol")

    def front_view(colour, x, y):
        return rest_ref.at[pl.ds(pl.multiple_of((x * 4 + y) * NB, NB), NB), pl.ds(256 * colour, 256)]

    def top_place(p, h):
        return rest_ref.at[pl.ds(pl.multiple_of(h * 512 + p * NB, NB), NB), pl.ds(512, 256)]

    plane = Plane(front_view, ps, pr, None)
    todo = plane.stages()
    barrier = pltpu.get_barrier_semaphore()
    for leg in range(2):
        for step in (1, -1):
            pl.semaphore_signal(barrier, inc=1, device_id=plane.peer(0, leg, step), device_id_type=MESH)
    for s in range(1, 8):
        pl.semaphore_signal(barrier, inc=1, device_id=(lax.rem(prow + s, 8), pcol), device_id_type=MESH)
    rest_ref[pl.ds(pl.multiple_of(pcol * NB, NB), NB), 0:512] = front_ref[...]
    for h in range(2):
        rest_ref[pl.ds(pl.multiple_of(h * 512 + prow * NB, NB), NB), 512:768] = top_ref[h * NB:h * NB + NB]

    def top_copy(s, h):
        n = (s - 1) * 2 + h
        return pltpu.make_async_remote_copy(
            top_ref.at[pl.ds(h * NB, NB)], top_place(prow, h), send.at[n], recv.at[n],
            device_id=(lax.rem(prow + s, 8), pcol), device_id_type=MESH)

    left = lax.broadcasted_iota(jnp.int32, (NB, 128), 1) < NB

    def fill(i, carry):
        at = pl.ds(pl.multiple_of(i * NB, NB), NB)
        for k in range(4):
            even, odd = tiles_ref[i * 8 + 2 * k], tiles_ref[i * 8 + 2 * k + 1]
            a_ref[at, 128 * k:128 * k + 128] = jnp.where(left, even, pltpu.roll(odd, NB, 1))
            a_ref[at, 512 + 128 * k:640 + 128 * k] = jnp.where(left, pltpu.roll(even, NB, 1), odd)
        return carry
    lax.fori_loop(0, 16, fill, 0)
    pl.semaphore_wait(barrier, 11)
    for s in range(1, 8):
        for h in range(2):
            top_copy(s, h).start()

    def bulk(j, off):
        done = j * 128
        cat = icat_ref[...]
        for r in range(4):
            hi, lo = split(a_ref[256 * r:256 * r + 256, pl.ds(off, 128)])
            v = lax.dot_general(jnp.concatenate([hi, lo, hi], axis=1), cat, TN, preferred_element_type=F32)
            row = lax.broadcasted_iota(jnp.int32, (256, 128), 0) + 256 * r
            hi, lo = split(jnp.where(row >= done, v, 0.0))
            pcat_ref[256 * r:256 * r + 256, 0:128] = hi
            pcat_ref[256 * r:256 * r + 256, 128:256] = lo
            pcat_ref[256 * r:256 * r + 256, 256:384] = hi
            qcat_ref[256 * r:256 * r + 256, 0:128] = hi
            qcat_ref[256 * r:256 * r + 256, 128:256] = hi
            qcat_ref[256 * r:256 * r + 256, 256:384] = lo
            low_hi_ref[256 * r:256 * r + 256, pl.ds(off, 128)] = hi
            low_lo_ref[256 * r:256 * r + 256, pl.ds(off, 128)] = lo
        for r in range(4):
            for k in range(r + 1):
                a_ref[256 * r:256 * r + 256, 256 * k:256 * k + 256] -= lax.dot_general(
                    pcat_ref[256 * r:256 * r + 256, :], qcat_ref[256 * k:256 * k + 256, :], TN, preferred_element_type=F32)

    def keep(off):
        hi, lo = split(inv_ref[...])
        inv_hi_ref[pl.ds(off, 128), :] = hi
        inv_lo_ref[pl.ds(off, 128), :] = lo
        icat_ref[:, 0:128] = hi
        icat_ref[:, 128:256] = hi
        icat_ref[:, 256:384] = lo

    def ahead(off):
        nxt = pl.multiple_of(off + 128, 128)
        hi, lo = split(a_ref[pl.ds(nxt, 128), pl.ds(off, 128)])
        v = lax.dot_general(jnp.concatenate([hi, lo, hi], axis=1), icat_ref[...], TN, preferred_element_type=F32)
        hi, lo = split(v)
        diag_ref[...] = a_ref[pl.ds(nxt, 128), pl.ds(nxt, 128)] - lax.dot_general(
            jnp.concatenate([hi, lo, hi], axis=1), jnp.concatenate([hi, hi, lo], axis=1), TN, preferred_element_type=F32)

    todo[0]()
    diag_ref[...] = a_ref[0:128, 0:128]
    invert_block(diag_ref, inv_ref, tmp_ref)
    keep(0)
    ahead(0)

    def thin(hi, lo, vh, vl):
        return (lax.dot_general(hi, vh, NN, preferred_element_type=F32) + lax.dot_general(hi, vl, NN, preferred_element_type=F32)
                + lax.dot_general(lo, vh, NN, preferred_element_type=F32))

    def panel_rows(e):
        top_at = pl.multiple_of(e * 256, 256)
        low_at = pl.multiple_of(e * 256 + 128, 128)
        top, low = pl.ds(top_at, 128), pl.ds(low_at, 128)
        xh, xl = split(rest_ref[top, :])
        th, tl = split(thin(inv_hi_ref[top, :], inv_lo_ref[top, :], xh, xl))
        x = rest_ref[low, :] - thin(low_hi_ref[low, pl.ds(top_at, 128)], low_lo_ref[low, pl.ds(top_at, 128)], th, tl)
        xh, xl = split(x)
        bh, bl = split(thin(inv_hi_ref[low, :], inv_lo_ref[low, :], xh, xl))
        sol_hi_ref[top, :] = th
        sol_lo_ref[top, :] = tl
        sol_hi_ref[low, :] = bh
        sol_lo_ref[low, :] = bl
        vh = jnp.concatenate([th, bh], axis=0)
        vl = jnp.concatenate([tl, bl], axis=0)
        for t in range(1, 4):
            lh = low_hi_ref[256 * t:256 * t + 256, pl.ds(top_at, 256)]
            ll = low_lo_ref[256 * t:256 * t + 256, pl.ds(top_at, 256)]
            v = thin(lh, ll, vh, vl)
            rest_ref[256 * t:256 * t + 256, :] -= jnp.where(e < t, v, 0.0)

    def step(j, carry):
        off = pl.multiple_of(j * 128, 128)
        for n in range(1, 5):
            @pl.when(j == n)
            def _(n=n):
                todo[2 * n - 1]()
                if n < 4:
                    todo[2 * n]()
        invert_block(diag_ref, inv_ref, tmp_ref)
        bulk(j, pl.multiple_of(off - 128, 128))
        keep(off)
        ahead(off)
        return carry
    lax.fori_loop(1, 5, step, 0)
    for s in range(1, 8):
        for h in range(2):
            n = (s - 1) * 2 + h
            place = top_place(lax.rem(prow + 8 - s, 8), h)
            pltpu.make_async_remote_copy(place, place, send.at[n], recv.at[n],
                                         device_id=(prow, pcol), device_id_type=MESH).wait_recv()
            top_copy(s, h).wait_send()
    plane.drain()

    def last(j, carry):
        off = pl.multiple_of(j * 128, 128)
        invert_block(diag_ref, inv_ref, tmp_ref)
        panel_rows(j - 5)
        bulk(j, pl.multiple_of(off - 128, 128))
        keep(off)

        @pl.when(j < 7)
        def _():
            ahead(off)
        return carry
    lax.fori_loop(5, 8, last, 0)


def factor(tiles, front, top):
    return pl.pallas_call(
        factor_kernel,
        out_shape=(
            jax.ShapeDtypeStruct((KK, 768), F32),
            jax.ShapeDtypeStruct((KK, 128), BF16),
            jax.ShapeDtypeStruct((KK, 128), BF16),
            jax.ShapeDtypeStruct((KK, KK), BF16),
            jax.ShapeDtypeStruct((KK, KK), BF16),
            jax.ShapeDtypeStruct((768, 768), BF16),
            jax.ShapeDtypeStruct((768, 768), BF16),
        ),
        in_specs=[pl.BlockSpec(memory_space=pltpu.VMEM)] * 3,
        out_specs=[pl.BlockSpec(memory_space=pltpu.VMEM)] * 7,
        scratch_shapes=[
            pltpu.VMEM((KK, KK), F32),
            pltpu.VMEM((128, 128), F32),
            pltpu.VMEM((128, 128), F32),
            pltpu.VMEM((144, 128), F32),
            pltpu.VMEM((KK, 384), BF16),
            pltpu.VMEM((KK, 384), BF16),
            pltpu.VMEM((128, 384), BF16),
            pltpu.SemaphoreType.DMA((14,)),
            pltpu.SemaphoreType.DMA((14,)),
            pltpu.SemaphoreType.DMA((30,)),
            pltpu.SemaphoreType.DMA((30,)),
        ],
        compiler_params=pltpu.CompilerParams(collective_id=3, has_side_effects=True, vmem_limit_bytes=18 << 20),
        name="factor",
    )(tiles, front, top)


def solve_kernel(rest_ref, inv_hi_ref, inv_lo_ref, low_hi_ref, low_lo_ref, sol_hi_ref, sol_lo_ref, local_ref, trail_ref, panel_ref,
                 hi_ref, lo_ref):
    def thin(hi, lo, vh, vl):
        return (lax.dot_general(hi, vh, NN, preferred_element_type=F32) + lax.dot_general(hi, vl, NN, preferred_element_type=F32)
                + lax.dot_general(lo, vh, NN, preferred_element_type=F32))
    hi_ref[:768, :] = sol_hi_ref[...]
    lo_ref[:768, :] = sol_lo_ref[...]
    for j in (6, 7):
        at = slice(128 * j, 128 * j + 128)
        x = rest_ref[at, :]
        if j == 7:
            x = x - thin(low_hi_ref[896:, 768:896], low_lo_ref[896:, 768:896], hi_ref[768:896, :], lo_ref[768:896, :])
        xh, xl = split(x)
        vh, vl = split(thin(inv_hi_ref[at, :], inv_lo_ref[at, :], xh, xl))
        hi_ref[at, :] = vh
        lo_ref[at, :] = vl
    rh, rl = hi_ref[:, :512], lo_ref[:, :512]
    ch, cl = hi_ref[:, 512:], lo_ref[:, 512:]
    trail_ref[...] = local_ref[...] - (lax.dot_general(rh, ch, TT, preferred_element_type=F32)
                                       + lax.dot_general(rh, cl, TT, preferred_element_type=F32)
                                       + lax.dot_general(rl, ch, TT, preferred_element_type=F32))
    pcol = lax.axis_index("pcol")
    at = pl.ds(pl.multiple_of(pcol * NB, NB), NB)
    panel_ref[...] = hi_ref[at, :512].astype(F32) + lo_ref[at, :512].astype(F32)


def solve(rest, inv_hi, inv_lo, low_hi, low_lo, ahead_hi, ahead_lo, local):
    return pl.pallas_call(
        solve_kernel,
        out_shape=(jax.ShapeDtypeStruct((512, 256), F32), jax.ShapeDtypeStruct((NB, 512), F32)),
        in_specs=[pl.BlockSpec(memory_space=pltpu.VMEM)] * 8,
        out_specs=[pl.BlockSpec(memory_space=pltpu.VMEM)] * 2,
        scratch_shapes=[pltpu.VMEM((KK, 768), BF16)] * 2,
        compiler_params=pltpu.CompilerParams(vmem_limit_bytes=18 << 20),
        name="solve",
    )(rest, inv_hi, inv_lo, low_hi, low_lo, ahead_hi, ahead_lo, local)


def per_device(factors, x_factor, zinv_factor, placement):
    rows, cols = route(factors, placement.reshape(32, 128))
    local, front, tiles = pair_blocks(rows.reshape(512, W), cols.reshape(256, W), x_factor, zinv_factor)
    rest, inv_hi, inv_lo, low_hi, low_lo, ahead_hi, ahead_lo = factor(tiles.reshape(128, NB, 128), front, local)
    trailing, panel = solve(rest, inv_hi, inv_lo, low_hi, low_lo, ahead_hi, ahead_lo, local)
    return (trailing, panel.T)


def solution(mesh):
    in_specs = (P(None, ("prow", "pcol"), None), P(), P(), P())
    out_specs = (P("prow", "pcol"), P("prow", "pcol"))
    return jax.shard_map(per_device, mesh=mesh, in_specs=in_specs, out_specs=out_specs, check_vma=False)
```

```python
import functools
import jax
import jax.numpy as jnp
from jax import lax
from jax.experimental import pallas as pl
from jax.experimental.pallas import tpu as pltpu
from jax.sharding import PartitionSpec as P

RANK = 4
NB = 64
KK = 1024
F32, BF16 = jnp.float32, jnp.bfloat16
SIGNS = (1.0, 1.0, -1.0, -1.0)
MESH = pl.DeviceIdType.MESH
TN = (((1,), (1,)), ((), ()))
NN = (((1,), (0,)), ((), ()))
TT = (((0,), (0,)), ((), ()))


def split(v):
    hi = v.astype(BF16)
    return hi, (v - hi.astype(F32)).astype(BF16)


def spread(v):
    return jnp.broadcast_to(v, (8, 128))


def invert_block(block_ref, inv_ref, tmp_ref):
    lane = lax.broadcasted_iota(jnp.int32, (8, 128), 1)
    sub = lax.broadcasted_iota(jnp.int32, (8, 128), 0)
    rows = [block_ref[8 * i:8 * i + 8, :] for i in range(16)]
    for j in range(16):
        here = (lane >= 8 * j) & (lane < 8 * j + 8)
        mine = rows[j]
        spot = 72 * (j % 2)
        for q in range(8):
            tmp_ref[spot + 8 * q:spot + 8 * q + 8, :] = spread(mine[:, 8 * j + q:8 * j + q + 1])
        tmp_ref[spot + 64:spot + 72, :] = jnp.where(here, (lane == sub + 8 * j).astype(F32), mine)
        a = [[None] * 8 for _ in range(8)]
        for q in range(8):
            for s in range(q, 8):
                a[s][q] = tmp_ref[pl.ds(spot + 8 * q + s, 8, stride=0), :]
        r = [tmp_ref[pl.ds(spot + 64 + t, 8, stride=0), :] for t in range(8)]
        pivots, low = [], []
        for t in range(0, 8, 2):
            u = t + 1
            det = a[t][t] * a[u][u] - a[u][t] * a[u][t]
            inv_det = 1.0 / det
            p00, p01, p11 = a[u][u] * inv_det, -a[u][t] * inv_det, a[t][t] * inv_det
            pivots.append((p00, p01, p11, a[t][t], a[u][t], det))
            m = [[None] * 2 for _ in range(8)]
            for s in range(t + 2, 8):
                m[s][0] = a[s][t] * p00 + a[s][u] * p01
                m[s][1] = a[s][t] * p01 + a[s][u] * p11
            for s in range(t + 2, 8):
                for k in range(t + 2, s + 1):
                    a[s][k] = a[s][k] - (m[s][0] * a[k][t] + m[s][1] * a[k][u])
                r[s] = r[s] - (m[s][0] * r[t] + m[s][1] * r[u])
            low.append(m)
        packed, packed_d = r[0], pivots[0][3]
        for t in range(1, 8):
            p00, p01, p11, a00, a10, det = pivots[t // 2]
            row = a00 * r[t] - a10 * r[t - 1] if t % 2 else r[t]
            packed = jnp.where(sub == t, row, packed)
            packed_d = jnp.where(sub == t, a00 * det if t % 2 else a00, packed_d)
        inv_ref[8 * j:8 * j + 8, :] = jnp.where(lane < 8 * j + 8, packed * lax.rsqrt(packed_d), 0.0)
        if j == 15:
            break
        w = [None] * 8
        for t in (6, 4, 2, 0):
            p00, p01, p11 = pivots[t // 2][:3]
            w[t] = r[t] * p00 + r[t + 1] * p01
            w[t + 1] = r[t] * p01 + r[t + 1] * p11
            for s in range(t + 2, 8):
                w[t] = w[t] - low[t // 2][s][0] * w[s]
                w[t + 1] = w[t + 1] - low[t // 2][s][1] * w[s]
        for i in range(j + 1, 16):
            acc = jnp.where(here, 0.0, rows[i])
            for q in range(8):
                acc = acc - spread(rows[i][:, 8 * j + q:8 * j + q + 1]) * w[q]
            rows[i] = acc


OFFS = 4


class Plane:
    def __init__(self, view, send, recv, arrived):
        self.prow, self.pcol = lax.axis_index("prow"), lax.axis_index("pcol")
        self.me = (self.pcol // 4, lax.rem(self.pcol, 4))
        self.sign = 1 - 2 * lax.rem(self.prow, 2)
        self.offs = (0, -self.sign, self.sign, 2)
        self.raw, self.send, self.recv, self.arrived = view, send, recv, arrived

    def view(self, colour, first, second):
        steps = (first, second) if colour == 0 else (second, first)
        at = [lax.rem(v + s + OFFS, 4) for v, s in zip(self.me, steps)]
        return self.raw(colour, at[0], at[1])

    def peer(self, colour, leg, step):
        dim = leg if colour == 0 else 1 - leg
        at = [lax.rem(v + step + OFFS, 4) if d == dim else v for d, v in enumerate(self.me)]
        return (self.prow, at[0] * 4 + at[1])

    def message(self, colour, leg, o, kind):
        n = colour * 15 + (kind if leg == 0 else 3 + o * 3 + kind)
        carried = -self.sign if kind == 2 else 0
        part = self.view(colour, carried, 0) if leg == 0 else self.view(colour, self.offs[o], carried)
        to = self.peer(colour, leg, -self.sign if kind == 1 else self.sign)
        return pltpu.make_async_remote_copy(part, part, self.send.at[n], self.recv.at[n], device_id=to, device_id_type=MESH)

    def landed(self, colour, leg, o, kind):
        n = colour * 15 + (kind if leg == 0 else 3 + o * 3 + kind)
        come = (-self.sign, self.sign, 2)[kind]
        part = self.view(colour, come, 0) if leg == 0 else self.view(colour, self.offs[o], come)
        pltpu.make_async_remote_copy(part, part, self.send.at[n], self.recv.at[n],
                                     device_id=self.peer(colour, leg, 1), device_id_type=MESH).wait_recv()
        if self.arrived is not None:
            self.arrived(colour, part, 1 + (kind if leg == 0 else 3 + o * 3 + kind))

    def both(self, colour, leg, o):
        self.message(colour, leg, o, 0).start()
        self.message(colour, leg, o, 1).start()

    def stages(self):
        def relay(c, leg, o):
            self.landed(c, leg, o, 0)
            self.message(c, leg, o, 2).start()

        def s0():
            for c in range(2):
                self.both(c, 0, 0)
            for c in range(2):
                self.both(c, 1, 0)

        def s1():
            for c in range(2):
                relay(c, 0, 0)
                self.both(c, 1, 1)

        def s2():
            for c in range(2):
                self.landed(c, 0, 0, 1)
                self.both(c, 1, 2)

        def s3():
            for c in range(2):
                relay(c, 1, 0)

        def s4():
            for c in range(2):
                self.landed(c, 0, 0, 2)
                self.both(c, 1, 3)

        def s5():
            for o in (1, 2):
                for c in range(2):
                    relay(c, 1, o)

        def s6():
            for c in range(2):
                relay(c, 1, 3)

        def s7():
            for o in range(4):
                for c in range(2):
                    self.landed(c, 1, o, 1)
            for o in range(4):
                for c in range(2):
                    self.landed(c, 1, o, 2)
        return [s0, s1, s2, s3, s4, s5, s6, s7]

    def drain(self):
        for c in range(2):
            for kind in range(3):
                self.message(c, 0, 0, kind).wait_send()
                for o in range(4):
                    self.message(c, 1, o, kind).wait_send()


class Column:
    def __init__(self, view, send, recv):
        self.prow, self.pcol = lax.axis_index("prow"), lax.axis_index("pcol")
        self.z, self.core = self.prow // 2, lax.rem(self.prow, 2)
        self.sign = 1 - 2 * self.core
        self.raw, self.send, self.recv = view, send, recv

    def message(self, kind):
        part = self.raw(lax.rem(self.z + (-self.sign if kind == 2 else 0) + OFFS, 4), self.core)
        to = lax.rem(self.z + (-self.sign if kind == 1 else self.sign) + OFFS, 4)
        return pltpu.make_async_remote_copy(part, part, self.send.at[kind], self.recv.at[kind],
                                            device_id=(to * 2 + self.core, self.pcol), device_id_type=MESH)

    def landed(self, kind):
        at = lax.rem(self.z + (-self.sign, self.sign, 2)[kind] + OFFS, 4)
        part = self.raw(at, self.core)
        pltpu.make_async_remote_copy(part, part, self.send.at[kind], self.recv.at[kind],
                                     device_id=(self.prow, self.pcol), device_id_type=MESH).wait_recv()
        return at

    def drain(self):
        for kind in range(3):
            self.message(kind).wait_send()


W = 2176


def before(n):
    return (lax.broadcasted_iota(jnp.int32, (n, n), 0) > lax.broadcasted_iota(jnp.int32, (n, n), 1)).astype(BF16)


def earlier(mask):
    n = mask.shape[0]
    wide = jnp.broadcast_to(mask.astype(F32), (n, 128)).astype(BF16)
    return jnp.dot(before(n), wide, preferred_element_type=F32)[:, 0:1].astype(jnp.int32)


def pick(index, valid, n):
    lane = lax.broadcasted_iota(jnp.int32, (index.shape[0], n), 1)
    hit = lane == index
    if valid is not None:
        hit = hit & valid
    return hit.astype(F32).astype(BF16)


def route_kernel(factors_ref, placed_ref, rows_ref, cols_ref,
                 send_a, got_a, send_b, got_b, piece_ref, ss, rs, ps, pr, zs, zr, xs, xr):
    prow, pcol = lax.axis_index("prow"), lax.axis_index("pcol")
    twin = (lax.rem(pcol, 8), prow + 8 * (pcol // 8))
    at_home = prow == lax.rem(pcol, 8)
    barrier = pltpu.get_barrier_semaphore()
    for s in range(1, 16):
        pl.semaphore_signal(barrier, inc=1, device_id=(prow, lax.rem(pcol + s, 16)), device_id_type=MESH)
    for s in range(1, 8):
        pl.semaphore_signal(barrier, inc=1, device_id=(lax.rem(prow + s, 8), pcol), device_id_type=MESH)

    @pl.when(jnp.logical_not(at_home))
    def _():
        pl.semaphore_signal(barrier, inc=1, device_id=twin, device_id_type=MESH)

    device = prow * 16 + pcol
    line = jnp.broadcast_to(placed_ref[pl.ds(device // 4, 1), :], (8, 128))
    mine = pltpu.roll(line, lax.rem(4 - lax.rem(device, 4), 4) * 32, 1)[0:1, :32]
    group = (mine >> 6) & 7
    row = lax.broadcasted_iota(jnp.int32, (64, 32), 0)
    match = group == (row >> 3)
    ahead = (lax.broadcasted_iota(jnp.int32, (32, 32), 0) < lax.broadcasted_iota(jnp.int32, (32, 32), 1)).astype(BF16)
    rank = jnp.dot(match.astype(F32).astype(BF16), ahead, preferred_element_type=F32).astype(jnp.int32)
    chosen = match & (rank == (row & 7))
    sel = chosen.astype(F32).astype(BF16)
    for r in range(RANK):
        send_a[:, :, 512 * r:512 * r + 512] = jnp.dot(sel, factors_ref[r], preferred_element_type=F32).reshape(8, 8, 512).astype(BF16)

    def total(v):
        return jnp.sum(jnp.where(chosen, v.astype(F32), 0.0), axis=1, keepdims=True)
    lane = lax.broadcasted_iota(jnp.int32, (64, 128), 1)
    tags = jnp.where(lane == 0, total(mine >> 6), jnp.where(lane == 1, total(mine & 63), jnp.where(lane == 2, total(mine * 0 + 1), 0.0)))
    send_a[:, :, 2048:] = tags.reshape(8, 8, 128).astype(BF16)
    got_a[prow] = send_a[prow]

    kind = (placed_ref[...] >> 6) & 15
    spot = lax.broadcasted_iota(jnp.int32, kind.shape, 0) * 4 + (lax.broadcasted_iota(jnp.int32, kind.shape, 1) >> 5)
    prior = (spot & 15) < pcol
    base = [jnp.sum((prior & (kind == prow + 8 * h)).astype(F32), keepdims=True).astype(jnp.int32) for h in range(2)]

    pl.semaphore_wait(barrier, jnp.where(at_home, 22, 23))

    def copy(src, dst, n, to):
        return pltpu.make_async_remote_copy(src, dst, ss.at[n], rs.at[n], device_id=to, device_id_type=MESH)

    def along_prow(s):
        return (lax.rem(prow + s, 8), pcol)

    def along_pcol(s):
        return (prow, lax.rem(pcol + s, 16))

    def slab(ref, i, n):
        return ref.at[pl.ds(pl.multiple_of(i * n, n), n)]

    def a_copy(s):
        return copy(send_a.at[lax.rem(prow + s, 8)], got_a.at[prow], s - 1, along_prow(s))

    def b_copy(s):
        return copy(send_b.at[lax.rem(pcol + s, 16)], got_b.at[pcol], 7 + s - 1, along_pcol(s))

    def twin_copy():
        return copy(piece_ref, cols_ref.at[twin[0]], 22, twin)

    def rows_view(colour, x, y):
        return rows_ref.at[x, y, :, pl.ds(1152 * colour, 1152 if colour == 0 else 1024)]

    def cols_view(z, core):
        return cols_ref.at[z * 2 + core]

    for s in (4, 3, 5, 2, 6, 7, 1):
        a_copy(s).start()
    for s in range(1, 8):
        spot = got_a.at[lax.rem(prow + 8 - s, 8)]
        copy(spot, spot, s - 1, along_prow(1)).wait_recv()

    got = got_a[...].astype(F32).reshape(64, W).astype(BF16)
    tags = got[:, 2048:].astype(F32)
    valid = tags[:, 2:3] > 0.5
    half = (tags[:, 0:1].astype(jnp.int32) >> 3) & 1
    slot = jnp.zeros((64, 1), jnp.int32)
    for h in range(2):
        li = earlier(valid & (half == h))
        slot = jnp.where(half == h, (8 * h + ((base[h] + li) & 7)) * 8 + (li >> 3), slot)
    send_b[...] = lax.dot_general(pick(slot, valid, 128), got, TT, preferred_element_type=F32).reshape(16, 8, W).astype(BF16)
    got_b[pcol] = send_b[pcol]
    for s in (10, 9, 11, 6, 14, 8, 2, 7, 13, 5, 15, 12, 4, 3, 1):
        b_copy(s).start()
    for s in range(1, 16):
        spot = got_b.at[lax.rem(pcol + 16 - s, 16)]
        copy(spot, spot, 7 + s - 1, along_prow(1)).wait_recv()

    got = got_b[...].astype(F32).reshape(128, W).astype(BF16)
    valid = got[:, 2048:].astype(F32)[:, 2:3] > 0.5
    piece = lax.dot_general(pick(earlier(valid), valid, 32), got, TT, preferred_element_type=F32).astype(BF16)
    piece_ref[...] = piece
    rows_ref[pcol // 4, lax.rem(pcol, 4)] = piece

    @pl.when(at_home)
    def _():
        cols_ref[prow] = piece

    @pl.when(jnp.logical_not(at_home))
    def _():
        twin_copy().start()
    plane = Plane(rows_view, ps, pr, None)
    column = Column(cols_view, zs, zr)
    core = lax.rem(prow, 2)
    other = prow + 1 - 2 * core

    def across(n, z, whose):
        part = cols_view(z, whose)
        return pltpu.make_async_remote_copy(part, part, xs.at[n], xr.at[n], device_id=(other, pcol), device_id_type=MESH)
    todo = plane.stages()
    todo[0]()
    todo[1]()

    @pl.when(jnp.logical_not(at_home))
    def _():
        copy(cols_ref.at[prow], cols_ref.at[prow], 22, twin).wait_recv()
    column.message(0).start()
    column.message(1).start()
    across(0, prow // 2, core).start()
    todo[2]()
    todo[3]()
    at = [prow // 2, column.landed(0)]
    column.message(2).start()
    across(1, at[1], core).start()
    todo[4]()
    at.append(column.landed(1))
    across(2, at[2], core).start()
    todo[5]()
    at.append(column.landed(2))
    across(3, at[3], core).start()
    todo[6]()
    todo[7]()
    sign = 1 - 2 * core
    for n, shift in enumerate((0, sign, -sign, 2)):
        across(n, lax.rem(prow // 2 + shift + OFFS, 4), 1 - core).wait_recv()
        across(n, at[n], core).wait_send()
    plane.drain()
    column.drain()
    for s in range(1, 8):
        a_copy(s).wait_send()
    for s in range(1, 16):
        b_copy(s).wait_send()

    @pl.when(jnp.logical_not(at_home))
    def _():
        twin_copy().wait_send()


def route(factors, placed):
    return pl.pallas_call(
        route_kernel,
        out_shape=(jax.ShapeDtypeStruct((4, 4, 32, W), BF16), jax.ShapeDtypeStruct((8, 32, W), BF16)),
        in_specs=[pl.BlockSpec(memory_space=pltpu.VMEM)] * 2,
        out_specs=[pl.BlockSpec(memory_space=pltpu.VMEM)] * 2,
        scratch_shapes=[
            pltpu.VMEM((8, 8, W), BF16),
            pltpu.VMEM((8, 8, W), BF16),
            pltpu.VMEM((16, 8, W), BF16),
            pltpu.VMEM((16, 8, W), BF16),
            pltpu.VMEM((32, W), BF16),
            pltpu.SemaphoreType.DMA((23,)),
            pltpu.SemaphoreType.DMA((23,)),
            pltpu.SemaphoreType.DMA((30,)),
            pltpu.SemaphoreType.DMA((30,)),
            pltpu.SemaphoreType.DMA((3,)),
            pltpu.SemaphoreType.DMA((3,)),
            pltpu.SemaphoreType.DMA((4,)),
            pltpu.SemaphoreType.DMA((4,)),
        ],
        compiler_params=pltpu.CompilerParams(collective_id=1, has_side_effects=True, vmem_limit_bytes=24 << 20),
        name="route",
    )(factors, placed)


def pair_kernel(rows_ref, cols_ref, xf_ref, zf_ref, local_ref, front_ref, out_ref, x_ref, z_ref, send, recv, zsend, zrecv, psend, precv):
    prow, pcol = lax.axis_index("prow"), lax.axis_index("pcol")
    z, core = prow // 2, lax.rem(prow, 2)
    other = (prow + 1 - 2 * core, pcol)

    def tile_view(at, whose):
        return out_ref.at[pcol // 4, lax.rem(pcol, 4), at, whose]

    def block_view(colour, x, y):
        return out_ref.at[x, y, :, core, pl.ds(32 * colour, 32)]

    def across(colour, part, n):
        return pltpu.make_async_remote_copy(part, part, psend.at[colour * 16 + n], precv.at[colour * 16 + n],
                                            device_id=other, device_id_type=MESH)
    plane = Plane(block_view, send, recv, lambda colour, part, n: across(colour, part, n).start())
    column = Column(tile_view, zsend, zrecv)
    barrier = pltpu.get_barrier_semaphore()
    for step in (1, -1):
        pl.semaphore_signal(barrier, inc=1, device_id=plane.peer(0, 0, step), device_id_type=MESH)
        pl.semaphore_signal(barrier, inc=1, device_id=plane.peer(0, 1, step), device_id_type=MESH)
        pl.semaphore_signal(barrier, inc=1, device_id=(lax.rem(z + step + OFFS, 4) * 2 + core, pcol), device_id_type=MESH)
    pl.semaphore_signal(barrier, inc=1, device_id=other, device_id_type=MESH)
    depth = xf_ref.shape[0]

    def load(src, first, count, shift, at):
        tags = src[:, 2048:].astype(F32).astype(jnp.int32)
        spot = (tags[:, 0:1] >> shift) * NB + tags[:, 1:2] - first
        rows = lax.dot_general(pick(spot, None, count), src[:, :2048], TT, preferred_element_type=F32).astype(BF16)
        stack = jnp.concatenate([rows[:, r * depth:(r + 1) * depth] for r in range(RANK)], axis=0)
        for dst, mat in ((x_ref, xf_ref), (z_ref, zf_ref)):
            images = jnp.dot(stack, mat[...], preferred_element_type=F32).astype(BF16)
            for r in range(RANK):
                dst[r, at:at + count, :] = images[r * count:(r + 1) * count, :]

    def pair(base, m, other, n):
        acc = None
        for q in range(RANK):
            left_x = jnp.concatenate([x_ref[r, base:base + m, :] for r in range(RANK)], axis=0)
            left_z = jnp.concatenate([z_ref[r, base:base + m, :] for r in range(RANK)], axis=0)
            term = (lax.dot_general(left_x, x_ref[q, other:other + n, :], TN, preferred_element_type=F32)
                    * lax.dot_general(left_z, z_ref[q, other:other + n, :], TN, preferred_element_type=F32))
            term = (term[:m] + term[m:2 * m]) - (term[2 * m:3 * m] + term[3 * m:])
            if acc is None:
                acc = term
            elif SIGNS[q] > 0:
                acc = acc + term
            else:
                acc = acc - term
        return acc

    def chunk(base):
        block = pair(base, 64, 512, 256)
        local_ref[base:base + 64, :] = block

    def turn(base):
        front_ref[:, base:base + 128] = local_ref[base:base + 128, 0:128].T[:NB, :]

    load(cols_ref, 0, 64, 4, 512)
    load(rows_ref, 0, 128, 3, 0)
    out_ref[pcol // 4, lax.rem(pcol, 4), z, core] = pair(512, 64, 0, 128)
    pl.semaphore_wait(barrier, 7)
    column.message(0).start()
    column.message(1).start()
    load(cols_ref, 64, 192, 4, 576)
    column.landed(0)
    column.message(2).start()
    column.landed(1)
    load(rows_ref, 128, 128, 3, 128)
    column.landed(2)
    todo = plane.stages()
    todo[0]()
    for colour in range(2):
        across(colour, plane.view(colour, 0, 0), 0).start()
    load(rows_ref, 256, 256, 3, 256)
    todo[1]()
    for n in range(5):
        chunk(64 * n)
        todo[2 + n]()
    for n in range(5, 8):
        chunk(64 * n)
    for n in range(4):
        turn(128 * n)
    todo[7]()
    plane.drain()
    column.drain()
    mirror = Plane(lambda colour, x, y: out_ref.at[x, y, :, 1 - core, pl.ds(32 * colour, 32)], send, recv, None)
    for colour in range(2):
        for n in range(16):
            leg, o, kind = (0, 0, n - 1) if n < 4 else (1, (n - 4) // 3, (n - 4) % 3)
            come = (-plane.sign, plane.sign, 2)[kind]
            first, second = (0, 0) if n == 0 else ((come, 0) if leg == 0 else (plane.offs[o], come))
            across(colour, plane.view(colour, first, second), n).wait_send()
            come = (plane.sign, -plane.sign, 2)[kind]
            hop = (0, plane.sign, -plane.sign, 2)[o]
            first, second = (0, 0) if n == 0 else ((come, 0) if leg == 0 else (hop, come))
            across(colour, mirror.view(colour, first, second), n).wait_recv()


def pair_blocks(rows, cols, x_factor, z_factor):
    d = x_factor.shape[0]
    return pl.pallas_call(
        pair_kernel,
        out_shape=(
            jax.ShapeDtypeStruct((512, 256), F32),
            jax.ShapeDtypeStruct((NB, 512), F32),
            jax.ShapeDtypeStruct((4, 4, 4, 2, NB, 128), F32),
        ),
        in_specs=[pl.BlockSpec(memory_space=pltpu.VMEM)] * 4,
        out_specs=[pl.BlockSpec(memory_space=pltpu.VMEM)] * 3,
        scratch_shapes=[
            pltpu.VMEM((RANK, 768, d), BF16),
            pltpu.VMEM((RANK, 768, d), BF16),
            pltpu.SemaphoreType.DMA((30,)),
            pltpu.SemaphoreType.DMA((30,)),
            pltpu.SemaphoreType.DMA((3,)),
            pltpu.SemaphoreType.DMA((3,)),
            pltpu.SemaphoreType.DMA((32,)),
            pltpu.SemaphoreType.DMA((32,)),
        ],
        compiler_params=pltpu.CompilerParams(collective_id=2, has_side_effects=True, vmem_limit_bytes=40 << 20),
        name="pairs",
    )(rows, cols, x_factor, z_factor)


def factor_kernel(tiles_ref, front_ref, top_ref, rest_ref, inv_hi_ref, inv_lo_ref, low_hi_ref, low_lo_ref, sol_hi_ref, sol_lo_ref,
                  a_ref, diag_ref, inv_ref, tmp_ref, pcat_ref, qcat_ref, icat_ref, send, recv, ps, pr):
    prow, pcol = lax.axis_index("prow"), lax.axis_index("pcol")

    def front_view(colour, x, y):
        return rest_ref.at[pl.ds(pl.multiple_of((x * 4 + y) * NB, NB), NB), pl.ds(256 * colour, 256)]

    def top_place(p, h):
        return rest_ref.at[pl.ds(pl.multiple_of(h * 512 + p * NB, NB), NB), pl.ds(512, 256)]

    plane = Plane(front_view, ps, pr, None)
    todo = plane.stages()
    barrier = pltpu.get_barrier_semaphore()
    for leg in range(2):
        for step in (1, -1):
            pl.semaphore_signal(barrier, inc=1, device_id=plane.peer(0, leg, step), device_id_type=MESH)
    for s in range(1, 8):
        pl.semaphore_signal(barrier, inc=1, device_id=(lax.rem(prow + s, 8), pcol), device_id_type=MESH)
    rest_ref[pl.ds(pl.multiple_of(pcol * NB, NB), NB), 0:512] = front_ref[...]
    for h in range(2):
        rest_ref[pl.ds(pl.multiple_of(h * 512 + prow * NB, NB), NB), 512:768] = top_ref[h * NB:h * NB + NB]

    def top_copy(s, h):
        n = (s - 1) * 2 + h
        return pltpu.make_async_remote_copy(
            top_ref.at[pl.ds(h * NB, NB)], top_place(prow, h), send.at[n], recv.at[n],
            device_id=(lax.rem(prow + s, 8), pcol), device_id_type=MESH)

    left = lax.broadcasted_iota(jnp.int32, (NB, 128), 1) < NB

    def fill(i, carry):
        at = pl.ds(pl.multiple_of(i * NB, NB), NB)
        for k in range(4):
            even, odd = tiles_ref[i * 8 + 2 * k], tiles_ref[i * 8 + 2 * k + 1]
            a_ref[at, 128 * k:128 * k + 128] = jnp.where(left, even, pltpu.roll(odd, NB, 1))
            a_ref[at, 512 + 128 * k:640 + 128 * k] = jnp.where(left, pltpu.roll(even, NB, 1), odd)
        return carry
    lax.fori_loop(0, 16, fill, 0)
    pl.semaphore_wait(barrier, 11)
    for s in range(1, 8):
        for h in range(2):
            top_copy(s, h).start()

    def bulk(j, off):
        done = j * 128
        cat = icat_ref[...]
        for r in range(4):
            hi, lo = split(a_ref[256 * r:256 * r + 256, pl.ds(off, 128)])
            v = lax.dot_general(jnp.concatenate([hi, lo, hi], axis=1), cat, TN, preferred_element_type=F32)
            row = lax.broadcasted_iota(jnp.int32, (256, 128), 0) + 256 * r
            hi, lo = split(jnp.where(row >= done, v, 0.0))
            pcat_ref[256 * r:256 * r + 256, 0:128] = hi
            pcat_ref[256 * r:256 * r + 256, 128:256] = lo
            pcat_ref[256 * r:256 * r + 256, 256:384] = hi
            qcat_ref[256 * r:256 * r + 256, 0:128] = hi
            qcat_ref[256 * r:256 * r + 256, 128:256] = hi
            qcat_ref[256 * r:256 * r + 256, 256:384] = lo
            low_hi_ref[256 * r:256 * r + 256, pl.ds(off, 128)] = hi
            low_lo_ref[256 * r:256 * r + 256, pl.ds(off, 128)] = lo
        for r in range(4):
            for k in range(r + 1):
                a_ref[256 * r:256 * r + 256, 256 * k:256 * k + 256] -= lax.dot_general(
                    pcat_ref[256 * r:256 * r + 256, :], qcat_ref[256 * k:256 * k + 256, :], TN, preferred_element_type=F32)

    def keep(off):
        hi, lo = split(inv_ref[...])
        inv_hi_ref[pl.ds(off, 128), :] = hi
        inv_lo_ref[pl.ds(off, 128), :] = lo
        icat_ref[:, 0:128] = hi
        icat_ref[:, 128:256] = hi
        icat_ref[:, 256:384] = lo

    def ahead(off):
        nxt = pl.multiple_of(off + 128, 128)
        hi, lo = split(a_ref[pl.ds(nxt, 128), pl.ds(off, 128)])
        v = lax.dot_general(jnp.concatenate([hi, lo, hi], axis=1), icat_ref[...], TN, preferred_element_type=F32)
        hi, lo = split(v)
        diag_ref[...] = a_ref[pl.ds(nxt, 128), pl.ds(nxt, 128)] - lax.dot_general(
            jnp.concatenate([hi, lo, hi], axis=1), jnp.concatenate([hi, hi, lo], axis=1), TN, preferred_element_type=F32)

    todo[0]()
    diag_ref[...] = a_ref[0:128, 0:128]
    invert_block(diag_ref, inv_ref, tmp_ref)
    keep(0)
    ahead(0)

    def thin(hi, lo, vh, vl):
        return (lax.dot_general(hi, vh, NN, preferred_element_type=F32) + lax.dot_general(hi, vl, NN, preferred_element_type=F32)
                + lax.dot_general(lo, vh, NN, preferred_element_type=F32))

    def panel_rows(e):
        top_at = pl.multiple_of(e * 256, 256)
        low_at = pl.multiple_of(e * 256 + 128, 128)
        top, low = pl.ds(top_at, 128), pl.ds(low_at, 128)
        xh, xl = split(rest_ref[top, :])
        th, tl = split(thin(inv_hi_ref[top, :], inv_lo_ref[top, :], xh, xl))
        x = rest_ref[low, :] - thin(low_hi_ref[low, pl.ds(top_at, 128)], low_lo_ref[low, pl.ds(top_at, 128)], th, tl)
        xh, xl = split(x)
        bh, bl = split(thin(inv_hi_ref[low, :], inv_lo_ref[low, :], xh, xl))
        sol_hi_ref[top, :] = th
        sol_lo_ref[top, :] = tl
        sol_hi_ref[low, :] = bh
        sol_lo_ref[low, :] = bl
        vh = jnp.concatenate([th, bh], axis=0)
        vl = jnp.concatenate([tl, bl], axis=0)
        for t in range(1, 4):
            lh = low_hi_ref[256 * t:256 * t + 256, pl.ds(top_at, 256)]
            ll = low_lo_ref[256 * t:256 * t + 256, pl.ds(top_at, 256)]
            v = thin(lh, ll, vh, vl)
            rest_ref[256 * t:256 * t + 256, :] -= jnp.where(e < t, v, 0.0)

    def step(j, carry):
        off = pl.multiple_of(j * 128, 128)
        for n in range(1, 5):
            @pl.when(j == n)
            def _(n=n):
                todo[2 * n - 1]()
                if n < 4:
                    todo[2 * n]()
        invert_block(diag_ref, inv_ref, tmp_ref)
        bulk(j, pl.multiple_of(off - 128, 128))
        keep(off)
        ahead(off)
        return carry
    lax.fori_loop(1, 5, step, 0)
    for s in range(1, 8):
        for h in range(2):
            n = (s - 1) * 2 + h
            place = top_place(lax.rem(prow + 8 - s, 8), h)
            pltpu.make_async_remote_copy(place, place, send.at[n], recv.at[n],
                                         device_id=(prow, pcol), device_id_type=MESH).wait_recv()
            top_copy(s, h).wait_send()
    plane.drain()

    def last(j, carry):
        off = pl.multiple_of(j * 128, 128)
        invert_block(diag_ref, inv_ref, tmp_ref)
        panel_rows(j - 5)
        bulk(j, pl.multiple_of(off - 128, 128))
        keep(off)

        @pl.when(j < 7)
        def _():
            ahead(off)
        return carry
    lax.fori_loop(5, 8, last, 0)


def factor(tiles, front, top):
    return pl.pallas_call(
        factor_kernel,
        out_shape=(
            jax.ShapeDtypeStruct((KK, 768), F32),
            jax.ShapeDtypeStruct((KK, 128), BF16),
            jax.ShapeDtypeStruct((KK, 128), BF16),
            jax.ShapeDtypeStruct((KK, KK), BF16),
            jax.ShapeDtypeStruct((KK, KK), BF16),
            jax.ShapeDtypeStruct((768, 768), BF16),
            jax.ShapeDtypeStruct((768, 768), BF16),
        ),
        in_specs=[pl.BlockSpec(memory_space=pltpu.VMEM)] * 3,
        out_specs=[pl.BlockSpec(memory_space=pltpu.VMEM)] * 7,
        scratch_shapes=[
            pltpu.VMEM((KK, KK), F32),
            pltpu.VMEM((128, 128), F32),
            pltpu.VMEM((128, 128), F32),
            pltpu.VMEM((144, 128), F32),
            pltpu.VMEM((KK, 384), BF16),
            pltpu.VMEM((KK, 384), BF16),
            pltpu.VMEM((128, 384), BF16),
            pltpu.SemaphoreType.DMA((14,)),
            pltpu.SemaphoreType.DMA((14,)),
            pltpu.SemaphoreType.DMA((30,)),
            pltpu.SemaphoreType.DMA((30,)),
        ],
        compiler_params=pltpu.CompilerParams(collective_id=3, has_side_effects=True, vmem_limit_bytes=18 << 20),
        name="factor",
    )(tiles, front, top)


def solve_kernel(rest_ref, inv_hi_ref, inv_lo_ref, low_hi_ref, low_lo_ref, sol_hi_ref, sol_lo_ref, local_ref, trail_ref, panel_ref,
                 hi_ref, lo_ref):
    def thin(hi, lo, vh, vl):
        return (lax.dot_general(hi, vh, NN, preferred_element_type=F32) + lax.dot_general(hi, vl, NN, preferred_element_type=F32)
                + lax.dot_general(lo, vh, NN, preferred_element_type=F32))
    hi_ref[:768, :] = sol_hi_ref[...]
    lo_ref[:768, :] = sol_lo_ref[...]
    for j in (6, 7):
        at = slice(128 * j, 128 * j + 128)
        x = rest_ref[at, :]
        if j == 7:
            x = x - thin(low_hi_ref[896:, 768:896], low_lo_ref[896:, 768:896], hi_ref[768:896, :], lo_ref[768:896, :])
        xh, xl = split(x)
        vh, vl = split(thin(inv_hi_ref[at, :], inv_lo_ref[at, :], xh, xl))
        hi_ref[at, :] = vh
        lo_ref[at, :] = vl
    rh, rl = hi_ref[:, :512], lo_ref[:, :512]
    ch, cl = hi_ref[:, 512:], lo_ref[:, 512:]
    trail_ref[...] = local_ref[...] - (lax.dot_general(rh, ch, TT, preferred_element_type=F32)
                                       + lax.dot_general(rh, cl, TT, preferred_element_type=F32)
                                       + lax.dot_general(rl, ch, TT, preferred_element_type=F32))
    pcol = lax.axis_index("pcol")
    at = pl.ds(pl.multiple_of(pcol * NB, NB), NB)
    panel_ref[...] = hi_ref[at, :512].astype(F32) + lo_ref[at, :512].astype(F32)


def solve(rest, inv_hi, inv_lo, low_hi, low_lo, ahead_hi, ahead_lo, local):
    return pl.pallas_call(
        solve_kernel,
        out_shape=(jax.ShapeDtypeStruct((512, 256), F32), jax.ShapeDtypeStruct((NB, 512), F32)),
        in_specs=[pl.BlockSpec(memory_space=pltpu.VMEM)] * 8,
        out_specs=[pl.BlockSpec(memory_space=pltpu.VMEM)] * 2,
        scratch_shapes=[pltpu.VMEM((KK, 768), BF16)] * 2,
        compiler_params=pltpu.CompilerParams(vmem_limit_bytes=18 << 20),
        name="solve",
    )(rest, inv_hi, inv_lo, low_hi, low_lo, ahead_hi, ahead_lo, local)


def per_device(factors, x_factor, zinv_factor, placement):
    rows, cols = route(factors, placement.reshape(32, 128))
    local, front, tiles = pair_blocks(rows.reshape(512, W), cols.reshape(256, W), x_factor, zinv_factor)
    rest, inv_hi, inv_lo, low_hi, low_lo, ahead_hi, ahead_lo = factor(tiles.reshape(128, NB, 128), front, local)
    trailing, panel = solve(rest, inv_hi, inv_lo, low_hi, low_lo, ahead_hi, ahead_lo, local)
    return (trailing, panel.T)


def solution(mesh):
    in_specs = (P(None, ("prow", "pcol"), None), P(), P(), P())
    out_specs = (P("prow", "pcol"), P("prow", "pcol"))
    return jax.shard_map(per_device, mesh=mesh, in_specs=in_specs, out_specs=out_specs, check_vma=False)
```
